128 devices in a mesh: dp: 8 (over y, x_hi), expert: 16 (over z, x_lo, core).
Axes of the slice: x: 4 (x_hi: 2, x_lo: 2; x = x_hi * 2 + x_lo), y: 4, z: 4, core: 2. Of those that a mesh axis runs over, the one named last changes fastest.
Arguments:
- tokens: bfloat16 [401408, 768], P(('dp', 'expert')), may hold values from -120 to 120
- router: bfloat16 [768, 16], replicated, may hold values from -1 to 1
- w_in: bfloat16 [16, 768, 3072], P('expert'), may hold values from -0.21875 to 0.21875
- w_out: bfloat16 [16, 3072, 768], P('expert'), may hold values from -0.109375 to 0.109375
- g_outputs: bfloat16 [401408, 768], P(('dp', 'expert')), may hold values from -6 to 6
Outputs:
- g_tokens: bfloat16 [401408, 768], P(('dp', 'expert'))
- g_router: float32 [768, 16], replicated
- g_w_in: float32 [16, 768, 3072], P('expert', 'dp')
- g_w_out: float32 [16, 3072, 768], P('expert', 'dp')
The draws below stay inside these ranges and needn't reach their ends.
All inputs are finite; a program needn't handle non-finite values.
Results may differ from the reference program's by a relative error of at most 0.02.
Values may be sent and summed in bfloat16 or wider, within the bound.
No kernel may reach another device: no remote copies, remote signals or barrier semaphores. Data moves between devices by JAX's collectives and lax.ppermute only.
A program may use at most 192 MiB of HBM per device.

```python
import math
import jax
import jax.numpy as jnp
from jax import lax

D = 768
FF = 3072
PATCHES = 196
EXPERTS = 16
IMAGES = 2048
TOKENS = 401408


def router_draw(key):
    base = jax.random.normal(jax.random.fold_in(key, 11), (D, EXPERTS), jnp.float32)
    shaped = 3.0 * base * D ** (-0.5)
    return jnp.clip(shaped, -1.0, 1.0)


def draw_router(key, part):
    return router_draw(key).astype(jnp.bfloat16)


def draw_tokens(key, part):
    base = jnp.clip(jax.random.normal(jax.random.fold_in(key, 27), (IMAGES, PATCHES, D), jnp.float32), -6.0, 6.0)
    return base.reshape(TOKENS, D).astype(jnp.bfloat16)


def block_levels(own_key, shape, shards, low, high):
    loudness, own = 1.0, jax.random.fold_in(own_key, 6)
    for axis_at, parts in shards:
        draws = jnp.exp(jax.random.uniform(jax.random.fold_in(own, axis_at), (parts,), jnp.float32, low / len(shards), high / len(shards)))
        loudness = loudness * jnp.repeat(draws, shape[axis_at] // parts).reshape([-1 if axis == axis_at else 1 for axis in range(len(shape))])
    return loudness


def normal_values(key, shape, deviation, reach, shards=(), kind=jnp.bfloat16):
    loudness = block_levels(key, shape, shards, -0.22, 0.18) if shards else 1.0
    drawn = jax.random.normal(key, shape, jnp.float32) * deviation * loudness
    return jnp.minimum(jnp.maximum(drawn, -reach), reach).astype(kind)


def setup_inputs(seed: int = 0) -> dict:
    key_list = jax.random.split(jax.random.key(seed), 6)
    return {
        "tokens": draw_tokens(jax.random.fold_in(key_list[5], 71), 0),
        "router": draw_router(jax.random.fold_in(key_list[5], 71), 0),
        "w_in": normal_values(key_list[2], (EXPERTS, D, FF), D ** -0.5, 0.21875, ((0, 16),)),
        "w_out": normal_values(key_list[3], (EXPERTS, FF, D), FF ** -0.5, 0.109375, ((0, 16),)),
        "g_outputs": normal_values(key_list[4], (TOKENS, D), 1.0, 6.0, ((0, 128),)),
    }


def token_side(tok_block, router):
    img_block = tok_block.shape[0]
    logits = jnp.dot(tok_block.reshape(-1, tok_block.shape[2]), router, preferred_element_type=jnp.float32)
    logits = logits.reshape(img_block, PATCHES, router.shape[1])
    dispatch = jax.nn.softmax(logits, axis=1)
    combine = jax.nn.softmax(logits, axis=2)
    return (dispatch, combine)

def reference(tokens, router, w_in, w_out, g_outputs):
    feat_width = tokens.shape[1]
    experts = router.shape[1]
    images = tokens.shape[0] // PATCHES
    block_size = math.gcd(images, 32)
    blocks = images // block_size
    tok_blocks = tokens.reshape(blocks, block_size, PATCHES, feat_width)
    grad_blocks = g_outputs.reshape(blocks, block_size, PATCHES, feat_width)

    def slot_inputs(tok_block):
        dispatch, combine = token_side(tok_block, router)
        dispatch_low = dispatch.astype(jnp.bfloat16).astype(jnp.float32)
        return jnp.einsum('bpe,bpd->bed', dispatch_low, tok_block.astype(jnp.float32)).astype(jnp.bfloat16)
    slot_in = lax.map(slot_inputs, tok_blocks).reshape(images, experts, feat_width)
    by_expert = jnp.transpose(slot_in, (1, 0, 2))

    def expert_forward(items):
        rows_in, w_first, w_second = items
        pre_act = jnp.dot(rows_in, w_first, preferred_element_type=jnp.float32)
        activated = jax.nn.gelu(pre_act).astype(jnp.bfloat16)
        return jnp.dot(activated, w_second, preferred_element_type=jnp.float32).astype(jnp.bfloat16)
    slot_out = lax.map(expert_forward, (by_expert, w_in, w_out))
    out_blocks = jnp.transpose(slot_out, (1, 0, 2)).reshape(blocks, block_size, experts, feat_width)

    def slot_grads(items):
        tok_block, grad_block = items
        dispatch, combine = token_side(tok_block, router)
        combine_low = combine.astype(jnp.bfloat16).astype(jnp.float32)
        return jnp.einsum('bpe,bpd->bed', combine_low, grad_block.astype(jnp.float32)).astype(jnp.bfloat16)
    grad_slot_out = lax.map(slot_grads, (tok_blocks, grad_blocks)).reshape(images, experts, feat_width)
    grad_by_expert = jnp.transpose(grad_slot_out, (1, 0, 2))

    def expert_backward(items):
        rows_in, rows_grad, w_first, w_second = items
        pre_act = jnp.dot(rows_in, w_first, preferred_element_type=jnp.float32)
        activated = jax.nn.gelu(pre_act).astype(jnp.bfloat16)
        unused, gelu_back = jax.vjp(jax.nn.gelu, pre_act)
        grad_act = jnp.dot(rows_grad, w_second.T, preferred_element_type=jnp.float32)
        grad_pre = gelu_back(grad_act)[0].astype(jnp.bfloat16)
        grad_first = jnp.dot(rows_in.T, grad_pre, preferred_element_type=jnp.float32)
        grad_second = jnp.dot(activated.T, rows_grad, preferred_element_type=jnp.float32)
        grad_rows = jnp.dot(grad_pre, w_first.T, preferred_element_type=jnp.float32).astype(jnp.bfloat16)
        return (grad_first, grad_second, grad_rows)
    grad_w_in, grad_w_out, grad_slot_in = lax.map(expert_backward, (by_expert, grad_by_expert, w_in, w_out))
    in_blocks = jnp.transpose(grad_slot_in, (1, 0, 2)).reshape(blocks, block_size, experts, feat_width)

    def token_grads(carry, items):
        tok_block, grad_block, out_block, in_grad_block = items
        dispatch, combine = token_side(tok_block, router)
        grad_comb = jnp.einsum('bpd,bed->bpe', grad_block.astype(jnp.float32), out_block.astype(jnp.float32))
        comb_part = combine * (grad_comb - lax.optimization_barrier(jnp.sum(combine * grad_comb, axis=2, keepdims=True)))
        grad_disp = jnp.einsum('bpd,bed->bpe', tok_block.astype(jnp.float32), in_grad_block.astype(jnp.float32))
        disp_part = dispatch * (grad_disp - lax.optimization_barrier(jnp.sum(dispatch * grad_disp, axis=1, keepdims=True)))
        grad_logits = (comb_part + disp_part).astype(jnp.bfloat16)
        flat_logits = grad_logits.reshape(-1, experts)
        dispatch_low = dispatch.astype(jnp.bfloat16).astype(jnp.float32)
        grad_tok = jnp.einsum('bpe,bed->bpd', dispatch_low, in_grad_block.astype(jnp.float32))
        grad_tok = grad_tok + jnp.dot(flat_logits, router.T, preferred_element_type=jnp.float32).reshape(grad_tok.shape)
        carry = carry + jnp.dot(tok_block.reshape(-1, feat_width).T, flat_logits, preferred_element_type=jnp.float32)
        return (carry, grad_tok.astype(jnp.bfloat16))
    start_sum = jnp.zeros((feat_width, experts), jnp.float32)
    grad_router, grad_tokens = lax.scan(token_grads, start_sum, (tok_blocks, grad_blocks, out_blocks, in_blocks))
    return (grad_tokens.reshape(tokens.shape[0], feat_width), grad_router, grad_w_in, grad_w_out)
```

```python
import jax
import jax.numpy as jnp
from jax import lax
from jax.experimental import pallas as pl
from jax.experimental.pallas import tpu as pltpu
from jax.sharding import Mesh, PartitionSpec as P

PATCHES = 196
GROUP = 4
XH = 2
VMEM_BYTES = 56 * 1024 * 1024
GELU_C = 0.7978845608028654
GELU_A = 0.044715

f32 = jnp.float32
bf16 = jnp.bfloat16


def contract(left, right, left_dim, right_dim):
    return lax.dot_general(
        left, right, (((left_dim,), (right_dim,)), ((), ())), preferred_element_type=f32
    )


def params():
    return pltpu.CompilerParams(
        dimension_semantics=("arbitrary",), vmem_limit_bytes=VMEM_BYTES
    )


def lane_images(width):
    lane = lax.broadcasted_iota(jnp.int32, (1, width), 1)
    image = jnp.zeros_like(lane)
    for i in range(1, width // PATCHES):
        image = image + (lane >= i * PATCHES).astype(jnp.int32)
    return image


def per_image(values, image, count, reduce, start):
    out = jnp.zeros_like(values)
    for i in range(count):
        own = reduce(jnp.where(image == i, values, start), axis=1, keepdims=True)
        out = jnp.where(image == i, own, out)
    return out


def gelu_parts(x):
    x2 = x * x
    th = jnp.tanh(GELU_C * x * (1.0 + GELU_A * x2))
    cdf = 0.5 + 0.5 * th
    slope = cdf + (0.5 * GELU_C) * x * (1.0 - th * th) * (1.0 + (3.0 * GELU_A) * x2)
    return x * cdf, slope


def token_forward_body(router_ref, x_ref, g_ref, slots_ref, disp_ref, comb_ref, rt, acc_x, acc_g):
    step = pl.program_id(0)
    experts, images, _ = slots_ref.shape
    feat = x_ref.shape[1]
    width = x_ref.shape[0]

    @pl.when(step == 0)
    def _():
        rt[...] = router_ref[...].astype(f32).T.astype(bf16)
        acc_x[...] = jnp.zeros_like(acc_x)
        acc_g[...] = jnp.zeros_like(acc_g)

    x = x_ref[...]
    logits = contract(rt[...], x, 1, 1)
    image = lane_images(width)
    top = per_image(logits, image, GROUP, jnp.max, -jnp.inf)
    raised = jnp.exp(logits - top)
    dispatch = raised / per_image(raised, image, GROUP, jnp.sum, 0.0)
    raised_e = jnp.exp(logits - jnp.max(logits, axis=0, keepdims=True))
    combine = raised_e / jnp.sum(raised_e, axis=0, keepdims=True)
    disp_ref[0] = dispatch
    comb_ref[0] = combine
    row = lax.broadcasted_iota(jnp.int32, (1, images, 1), 1)
    own = row == (image + step * GROUP)[None]
    spread_d = jnp.where(own, dispatch[:, None, :], 0.0).astype(bf16)
    spread_c = jnp.where(own, combine[:, None, :], 0.0).astype(bf16)
    acc_x[...] += jnp.dot(
        spread_d.reshape(experts * images, width), x, preferred_element_type=f32
    )
    acc_g[...] += jnp.dot(
        spread_c.reshape(experts * images, width), g_ref[...], preferred_element_type=f32
    )

    @pl.when(step == pl.num_programs(0) - 1)
    def _():
        slots_ref[:, :, :feat] = acc_x[...].astype(bf16).reshape(experts, images, feat)
        slots_ref[:, :, feat:] = acc_g[...].astype(bf16).reshape(experts, images, feat)


def token_forward(tokens, router, g_outputs):
    rows, feat = tokens.shape
    experts = router.shape[1]
    images = rows // PATCHES
    width = GROUP * PATCHES
    steps = rows // width
    return pl.pallas_call(
        token_forward_body,
        grid=(steps,),
        in_specs=[
            pl.BlockSpec((feat, experts), lambda i: (0, 0)),
            pl.BlockSpec((width, feat), lambda i: (i, 0)),
            pl.BlockSpec((width, feat), lambda i: (i, 0)),
        ],
        out_specs=[
            pl.BlockSpec((experts, images, 2 * feat), lambda i: (0, 0, 0)),
            pl.BlockSpec((1, experts, width), lambda i: (i, 0, 0)),
            pl.BlockSpec((1, experts, width), lambda i: (i, 0, 0)),
        ],
        out_shape=[
            jax.ShapeDtypeStruct((experts, images, 2 * feat), bf16),
            jax.ShapeDtypeStruct((steps, experts, width), f32),
            jax.ShapeDtypeStruct((steps, experts, width), f32),
        ],
        scratch_shapes=[
            pltpu.VMEM((experts, feat), bf16),
            pltpu.VMEM((experts * images, feat), f32),
            pltpu.VMEM((experts * images, feat), f32),
        ],
        compiler_params=params(),
        name="token_forward",
    )(router, tokens, g_outputs)


def expert_body(rows_ref, w1_ref, w2_ref, out_ref, acc_o, acc_g):
    step = pl.program_id(0)
    feat = w1_ref.shape[0]

    @pl.when(step == 0)
    def _():
        acc_o[...] = jnp.zeros_like(acc_o)
        acc_g[...] = jnp.zeros_like(acc_g)

    rows = rows_ref[:, :feat]
    grads = rows_ref[:, feat:]
    w1 = w1_ref[...]
    w2 = w2_ref[...]
    pre = jnp.dot(rows, w1, preferred_element_type=f32)
    act, slope = gelu_parts(pre)
    acc_o[...] += jnp.dot(act.astype(bf16), w2, preferred_element_type=f32)
    grad_pre = (contract(grads, w2, 1, 1) * slope).astype(bf16)
    acc_g[...] += contract(grad_pre, w1, 1, 1)

    @pl.when(step == pl.num_programs(0) - 1)
    def _():
        out_ref[:, :feat] = acc_o[...].astype(bf16)
        out_ref[:, feat:] = acc_g[...].astype(bf16)


def expert_rows(rows, w_in, w_out):
    count, double = rows.shape
    feat = double // 2
    hidden = w_in.shape[2]
    tile = 512
    return pl.pallas_call(
        expert_body,
        grid=(hidden // tile,),
        in_specs=[
            pl.BlockSpec((count, double), lambda i: (0, 0)),
            pl.BlockSpec((None, feat, tile), lambda i: (0, 0, i)),
            pl.BlockSpec((None, tile, feat), lambda i: (0, i, 0)),
        ],
        out_specs=pl.BlockSpec((count, double), lambda i: (0, 0)),
        out_shape=jax.ShapeDtypeStruct((count, double), bf16),
        scratch_shapes=[pltpu.VMEM((count, feat), f32), pltpu.VMEM((count, feat), f32)],
        compiler_params=params(),
        name="expert_rows",
    )(rows, w_in, w_out)


def weight_grad_body(
    pos_ref, p0, p1, p2, p3, p4, w1_ref, w2_ref, keep_in, send_in, keep_out, send_out, acc
):
    feat = w1_ref.shape[0]
    xh = pos_ref[1]
    step = pl.program_id(0)
    w1 = w1_ref[...]
    w2 = w2_ref[...]
    total_in = None
    total_out = None
    for piece in (p0, p1, p2, p3, p4):
        rows = piece[:, :feat]
        grads = piece[:, feat:]
        act, slope = gelu_parts(jnp.dot(rows, w1, preferred_element_type=f32))
        grad_pre = (contract(grads, w2, 1, 1) * slope).astype(bf16)
        part_out = contract(act.astype(bf16), grads, 0, 0)
        part_in = contract(rows, grad_pre, 0, 0)
        total_out = part_out if total_out is None else total_out + part_out
        total_in = part_in if total_in is None else total_in + part_in
    acc[...] = total_in.reshape(acc.shape)
    keep_in[...] = acc[:, pl.ds(xh, 1)].reshape(keep_in.shape)
    send_in[...] = acc[:, pl.ds(1 - xh, 1)].reshape(send_in.shape).astype(bf16)

    @pl.when(step == 0)
    def _():
        send_out[...] = total_out.astype(bf16)

    @pl.when(step == 1)
    def _():
        keep_out[...] = total_out


def weight_grads(pos, pieces, w_in, w_out, parts):
    feat = w_in.shape[1]
    hidden = w_in.shape[2]
    tile = hidden // (parts * XH)
    own = feat // (parts * XH)

    def half(i, pos):
        return XH * pos[0] + jnp.where(i == 0, 1 - pos[1], pos[1])

    def tile_at(i, pos):
        return jnp.where(i == 0, 1 - pos[1], pos[1])

    return pl.pallas_call(
        weight_grad_body,
        grid_spec=pltpu.PrefetchScalarGridSpec(
            num_scalar_prefetch=1,
            grid=(XH,),
            in_specs=[pl.BlockSpec(p.shape, lambda i, pos: (0, 0)) for p in pieces]
            + [
                pl.BlockSpec((None, feat, tile), lambda i, pos: (0, 0, half(i, pos))),
                pl.BlockSpec((None, tile, feat), lambda i, pos: (0, half(i, pos), 0)),
            ],
            out_specs=[
                pl.BlockSpec((parts, own, tile), lambda i, pos: (0, 0, tile_at(i, pos))),
                pl.BlockSpec((parts, own, tile), lambda i, pos: (0, 0, tile_at(i, pos))),
                pl.BlockSpec((tile, feat), lambda i, pos: (0, 0)),
                pl.BlockSpec((tile, feat), lambda i, pos: (0, 0)),
            ],
            scratch_shapes=[pltpu.VMEM((parts, XH, own, tile), f32)],
        ),
        out_shape=[
            jax.ShapeDtypeStruct((parts, own, XH * tile), f32),
            jax.ShapeDtypeStruct((parts, own, XH * tile), bf16),
            jax.ShapeDtypeStruct((tile, feat), f32),
            jax.ShapeDtypeStruct((tile, feat), bf16),
        ],
        compiler_params=params(),
        name="weight_grads",
    )(pos, *pieces, w_in, w_out)


def token_logits_body(back_ref, x_ref, g_ref, disp_ref, comb_ref, gl_ref, slots_ref, router_ref, mix):
    step = pl.program_id(0)
    experts, images, double = back_ref.shape
    feat = double // 2
    width = x_ref.shape[0]
    total = experts * images

    @pl.when(step == 0)
    def _():
        out_row = lax.broadcasted_iota(jnp.int32, (total, total), 0)
        in_row = lax.broadcasted_iota(jnp.int32, (total, total), 1)
        wanted = (out_row % experts) * images + out_row // experts
        swap = (in_row == wanted).astype(f32).astype(bf16)
        mix[...] = jnp.dot(
            swap, back_ref[...].reshape(total, double), preferred_element_type=f32
        ).astype(bf16)
        router_ref[...] = jnp.zeros_like(router_ref)

    x = x_ref[...]
    block = mix[pl.ds(pl.multiple_of(step * (GROUP * experts), GROUP * experts), GROUP * experts), :]
    slots_ref[0] = block[:, feat:]
    image = lane_images(width)

    def picked(both):
        out = jnp.zeros((experts, width), f32)
        for i in range(GROUP):
            out = jnp.where(image == i, both[i * experts : (i + 1) * experts], out)
        return out

    grad_comb = picked(contract(block[:, :feat], g_ref[...], 1, 1))
    grad_disp = picked(contract(block[:, feat:], x, 1, 1))
    dispatch = disp_ref[0]
    combine = comb_ref[0]
    comb_part = combine * (grad_comb - jnp.sum(combine * grad_comb, axis=0, keepdims=True))
    disp_part = dispatch * (
        grad_disp - per_image(dispatch * grad_disp, image, GROUP, jnp.sum, 0.0)
    )
    grad_logits = (comb_part + disp_part).astype(bf16)
    gl_ref[0] = grad_logits
    router_ref[...] += jnp.dot(grad_logits, x, preferred_element_type=f32)


def token_logits(back, tokens, g_outputs, dispatch, combine):
    experts, images, double = back.shape
    rows, feat = tokens.shape
    steps, _, width = dispatch.shape
    return pl.pallas_call(
        token_logits_body,
        grid=(steps,),
        in_specs=[
            pl.BlockSpec((experts, images, double), lambda i: (0, 0, 0)),
            pl.BlockSpec((width, feat), lambda i: (i, 0)),
            pl.BlockSpec((width, feat), lambda i: (i, 0)),
            pl.BlockSpec((1, experts, width), lambda i: (i, 0, 0)),
            pl.BlockSpec((1, experts, width), lambda i: (i, 0, 0)),
        ],
        out_specs=[
            pl.BlockSpec((1, experts, width), lambda i: (i, 0, 0)),
            pl.BlockSpec((1, GROUP * experts, feat), lambda i: (i, 0, 0)),
            pl.BlockSpec((experts, feat), lambda i: (0, 0)),
        ],
        out_shape=[
            jax.ShapeDtypeStruct((steps, experts, width), bf16),
            jax.ShapeDtypeStruct((steps, GROUP * experts, feat), bf16),
            jax.ShapeDtypeStruct((experts, feat), f32),
        ],
        scratch_shapes=[pltpu.VMEM((experts * images, double), bf16)],
        compiler_params=params(),
        name="token_logits",
    )(back, tokens, g_outputs, dispatch, combine)


def token_grads_body(gl_ref, slots_ref, disp_ref, router_ref, out_ref, rt):
    experts = gl_ref.shape[1]
    width = gl_ref.shape[2]

    @pl.when(pl.program_id(0) == 0)
    def _():
        rt[...] = router_ref[...].astype(f32).T.astype(bf16)

    image = lane_images(width)
    dispatch = disp_ref[0]
    left = jnp.concatenate(
        [jnp.where(image == i, dispatch, 0.0) for i in range(GROUP)], axis=0
    ).astype(bf16)
    left = jnp.concatenate([left, gl_ref[0]], axis=0)
    right = jnp.concatenate([slots_ref[0], rt[...]], axis=0)
    out_ref[...] = contract(left, right, 0, 0).astype(bf16)


def token_grads(grad_logits, slots, dispatch, router):
    steps, experts, width = grad_logits.shape
    feat = slots.shape[2]
    return pl.pallas_call(
        token_grads_body,
        grid=(steps,),
        in_specs=[
            pl.BlockSpec((1, experts, width), lambda i: (i, 0, 0)),
            pl.BlockSpec((1, GROUP * experts, feat), lambda i: (i, 0, 0)),
            pl.BlockSpec((1, experts, width), lambda i: (i, 0, 0)),
            pl.BlockSpec((feat, experts), lambda i: (0, 0)),
        ],
        out_specs=pl.BlockSpec((width, feat), lambda i: (i, 0)),
        out_shape=jax.ShapeDtypeStruct((steps * width, feat), bf16),
        scratch_shapes=[pltpu.VMEM((experts, feat), bf16)],
        compiler_params=params(),
        name="token_grads",
    )(grad_logits, slots, dispatch, router)


def shift(value, axis, by, count):
    return lax.ppermute(value, axis, [(i, (i + by) % count) for i in range(count)])


def everywhere_sum(value, sizes):
    for axis, count in sizes:
        value = sum([shift(value, axis, by, count) for by in range(1, count)], value)
    return value


def solution(mesh):
    dp, experts = mesh.shape["dp"], mesh.shape["expert"]
    ny = dp // XH
    inner = (("core", 2), ("xl", 2), ("z", experts // 4))
    fine = Mesh(
        mesh.devices.reshape(ny, XH, experts // 4, 2, 2), ("y", "xh", "z", "xl", "core")
    )
    dp_axes = ("y", "xh")
    ex_axes = ("z", "xl", "core")
    sizes = inner + (("y", ny), ("xh", XH))

    def on_device(tokens, router, w_in, w_out, g_outputs):
        feat = tokens.shape[1]
        slots, dispatch, combine = token_forward(tokens, router, g_outputs)
        arrived = lax.all_to_all(slots, ex_axes, split_axis=0, concat_axis=0, tiled=True)
        rows = arrived.reshape(-1, 2 * feat)
        half = rows.shape[0] // 2
        right = shift(rows, "y", 1, ny)
        left = shift(rows, "y", ny - 1, ny)
        far_a = shift(right[:half], "y", 1, ny)
        far_b = shift(left[half:], "y", ny - 1, ny)
        results = expert_rows(rows, w_in, w_out)
        back = lax.all_to_all(
            results.reshape(slots.shape), ex_axes, split_axis=0, concat_axis=0, tiled=True
        )
        pos = jnp.stack([lax.axis_index("y"), lax.axis_index("xh")]).astype(jnp.int32)
        keep_in, send_in, keep_out, send_out = weight_grads(
            pos, (rows, right, left, far_a, far_b), w_in, w_out, ny
        )
        came_in = shift(send_in, "xh", 1, XH)
        came_out = shift(send_out, "xh", 1, XH)
        part_in = (keep_in + came_in.astype(f32)).astype(bf16)
        spread = lax.all_to_all(part_in, "y", split_axis=0, concat_axis=0, tiled=True)
        grad_first = jnp.transpose(spread, (1, 0, 2)).reshape(spread.shape[1], -1).astype(f32)
        grad_second = keep_out + came_out.astype(f32)
        grad_logits, slot_grads, router_term = token_logits(
            back, tokens, g_outputs, dispatch, combine
        )
        grad_router = everywhere_sum(router_term, sizes).T
        grad_tok = token_grads(grad_logits, slot_grads, dispatch, router)
        return grad_tok, grad_router, grad_first[None], grad_second[None]

    return jax.shard_map(
        on_device,
        mesh=fine,
        in_specs=(
            P(dp_axes + ex_axes, None),
            P(),
            P(ex_axes, None, None),
            P(ex_axes, None, None),
            P(dp_axes + ex_axes, None),
        ),
        out_specs=(
            P(dp_axes + ex_axes, None),
            P(),
            P(ex_axes, dp_axes, None),
            P(ex_axes, dp_axes, None),
        ),
        check_vma=False,
    )
```

```python
import functools

import jax
import jax.numpy as jnp
from jax import lax
from jax.experimental import pallas as pl
from jax.experimental.pallas import tpu as pltpu
from jax.sharding import Mesh, PartitionSpec as P

PATCHES = 196
GROUP = 4
XH = 2
MIB = 1024 * 1024
GELU_C = 0.7978845608028654
GELU_A = 0.044715

f32 = jnp.float32
bf16 = jnp.bfloat16


def contract(left, right, left_dim, right_dim):
    return lax.dot_general(
        left, right, (((left_dim,), (right_dim,)), ((), ())), preferred_element_type=f32
    )


def params(mib):
    return pltpu.CompilerParams(vmem_limit_bytes=mib * MIB)


def pinned(value):
    return pltpu.with_memory_space_constraint(value, pltpu.HBM)


IN_VMEM = pl.BlockSpec(memory_space=pltpu.VMEM)
IN_PLACE = pl.BlockSpec(memory_space=pltpu.HBM)


def gelu_parts(x):
    x2 = x * x
    th = jnp.tanh(GELU_C * x * (1.0 + GELU_A * x2))
    cdf = 0.5 + 0.5 * th
    slope = cdf + (0.5 * GELU_C) * x * (1.0 - th * th) * (1.0 + (3.0 * GELU_A) * x2)
    return x * cdf, slope


def lane_images(width):
    lane = lax.broadcasted_iota(jnp.int32, (1, width), 1)
    image = jnp.zeros_like(lane)
    for i in range(1, width // PATCHES):
        image = image + (lane >= i * PATCHES).astype(jnp.int32)
    return image


def per_image(values, image, reduce, start):
    width = values.shape[1]
    out = jnp.zeros_like(values)
    for i in range(GROUP):
        low = i * PATCHES // 128 * 128
        high = min(-(-(i + 1) * PATCHES // 128) * 128, width)
        part = jnp.where(image[:, low:high] == i, values[:, low:high], start)
        own = reduce(part, axis=1, keepdims=True)
        out = jnp.where(image == i, own, out)
    return out


def per_slot_rows(weights, image):
    return jnp.concatenate(
        [jnp.where(image == i, weights, 0.0) for i in range(GROUP)], axis=0
    ).astype(bf16)


def swap_matrix(total, inner):
    outer = total // inner
    out_row = lax.broadcasted_iota(jnp.int32, (total, total), 0)
    in_row = lax.broadcasted_iota(jnp.int32, (total, total), 1)
    wanted = (out_row % outer) * inner + out_row // outer
    return (in_row == wanted).astype(f32).astype(bf16)


def block_copies(src, dst, sem):
    width = GROUP * PATCHES
    return [
        pltpu.make_async_copy(
            src.at[pl.ds(b * width, width)], dst.at[pl.ds(b * width, width)], sem.at[b]
        )
        for b in range(src.shape[0] // width)
    ]


def token_forward_body(
    rt_ref, x_hbm, g_hbm, slots_ref, disp_ref, comb_ref, x_ref, g_ref, acc, x_sem, g_sem
):
    experts, images, double = slots_ref.shape
    feat = double // 2
    width = GROUP * PATCHES
    steps = images // GROUP
    rows = GROUP * experts
    total = experts * images

    x_copies = block_copies(x_hbm, x_ref, x_sem)
    g_copies = block_copies(g_hbm, g_ref, g_sem)
    for copy in x_copies + g_copies:
        copy.start()
    image = lane_images(width)
    rt = rt_ref[...]
    spread = []
    for b in range(steps):
        x_copies[b].wait()
        x = x_ref[b * width : (b + 1) * width, :]
        logits = contract(rt, x, 1, 1)
        top = per_image(logits, image, jnp.max, -jnp.inf)
        raised = jnp.exp(logits - top)
        dispatch = raised / per_image(raised, image, jnp.sum, 0.0)
        raised_e = jnp.exp(logits - jnp.max(logits, axis=0, keepdims=True))
        combine = raised_e / jnp.sum(raised_e, axis=0, keepdims=True)
        disp_ref[b] = dispatch
        comb_ref[b] = combine
        spread.append(per_slot_rows(combine, image))
        acc[b * rows : (b + 1) * rows, :feat] = jnp.dot(
            per_slot_rows(dispatch, image), x, preferred_element_type=f32
        ).astype(bf16)
    for b in range(steps):
        g_copies[b].wait()
        acc[b * rows : (b + 1) * rows, feat:] = jnp.dot(
            spread[b], g_ref[b * width : (b + 1) * width, :], preferred_element_type=f32
        ).astype(bf16)
    slots_ref[...] = (
        jnp.dot(swap_matrix(total, experts), acc[...], preferred_element_type=f32)
        .astype(bf16)
        .reshape(experts, images, double)
    )


def token_forward(tokens, rt, g_outputs):
    rows, feat = tokens.shape
    experts = rt.shape[0]
    images = rows // PATCHES
    width = GROUP * PATCHES
    steps = rows // width
    return pl.pallas_call(
        token_forward_body,
        in_specs=[IN_VMEM, IN_PLACE, IN_PLACE],
        out_specs=[IN_VMEM, IN_VMEM, IN_VMEM],
        out_shape=[
            jax.ShapeDtypeStruct((experts, images, 2 * feat), bf16),
            jax.ShapeDtypeStruct((steps, experts, width), f32),
            jax.ShapeDtypeStruct((steps, experts, width), f32),
        ],
        scratch_shapes=[
            pltpu.VMEM((rows, feat), bf16),
            pltpu.VMEM((rows, feat), bf16),
            pltpu.VMEM((experts * images, 2 * feat), bf16),
            pltpu.SemaphoreType.DMA((steps,)),
            pltpu.SemaphoreType.DMA((steps,)),
        ],
        compiler_params=params(20),
        name="token_forward",
    )(rt, pinned(tokens), pinned(g_outputs))


def expert_body(rows_ref, w1_ref, w2_ref, out_ref):
    feat = w1_ref.shape[1]
    hidden = w1_ref.shape[2]
    tile = 768
    rows = rows_ref[:, :feat]
    grads = rows_ref[:, feat:]
    made, back = None, None
    for low in range(0, hidden, tile):
        w1 = w1_ref[0, :, low : low + tile]
        w2 = w2_ref[0, low : low + tile, :]
        act, slope = gelu_parts(jnp.dot(rows, w1, preferred_element_type=f32))
        part = jnp.dot(act.astype(bf16), w2, preferred_element_type=f32)
        made = part if made is None else made + part
        grad_pre = (contract(grads, w2, 1, 1) * slope).astype(bf16)
        part = contract(grad_pre, w1, 1, 1)
        back = part if back is None else back + part
    out_ref[:, :feat] = made.astype(bf16)
    out_ref[:, feat:] = back.astype(bf16)


def expert_rows(rows, w_in, w_out):
    return pl.pallas_call(
        expert_body,
        in_specs=[IN_VMEM] * 3,
        out_specs=IN_VMEM,
        out_shape=jax.ShapeDtypeStruct(rows.shape, bf16),
        compiler_params=params(12),
        name="expert_rows",
    )(rows, w_in, w_out)


def slice_grads(piece_refs, w1_hbm, w2_hbm, low, tile, both, act_all, pre_all, w1, w2, sem):
    feat = w1.shape[0]
    low = pl.multiple_of(low, tile)
    first = pltpu.make_async_copy(w1_hbm.at[0, :, pl.ds(low, tile)], w1, sem.at[0])
    second = pltpu.make_async_copy(w2_hbm.at[0, pl.ds(low, tile), :], w2, sem.at[1])
    first.start()
    second.start()
    at = 0
    for piece in piece_refs:
        both[at : at + piece.shape[0], :] = piece[...]
        at += piece.shape[0]
    rows = both[:, :feat]
    grads = both[:, feat:]
    first.wait()
    act, slope = gelu_parts(jnp.dot(rows, w1[...], preferred_element_type=f32))
    act_all[...] = act.astype(bf16)
    second.wait()
    pre_all[...] = (contract(grads, w2[...], 1, 1) * slope).astype(bf16)
    return contract(rows, pre_all[...], 0, 0), contract(act_all[...], grads, 0, 0)


def grads_body(count, first, *refs):
    pieces, (w1_ref, w2_ref) = refs[:count], refs[count : count + 2]
    refs = refs[count + 2 :]
    sums, refs = (None, refs) if first else (refs[:2], refs[2:])
    out_in, out_out, *scratch = refs
    tile = out_in.shape[1]
    low = lax.axis_index("y") * tile
    part_in, part_out = slice_grads(pieces, w1_ref, w2_ref, low, tile, *scratch)
    out_in[...] = part_in if first else sums[0][...] + part_in
    out_out[...] = part_out if first else sums[1][...] + part_out


def last_grads_body(count, *refs):
    pieces, (w1_ref, w2_ref, sum_in, sum_out) = refs[:count], refs[count : count + 4]
    keep_in, send_in, keep_out, send_out, acc_in, acc_out, *scratch = refs[count + 4 :]
    tile = sum_in.shape[1]
    low = lax.axis_index("y") * tile
    xh = lax.axis_index("xh")
    part_in, part_out = slice_grads(pieces, w1_ref, w2_ref, low, tile, *scratch)
    acc_in[...] = (sum_in[...] + part_in).reshape(acc_in.shape)
    acc_out[...] = (sum_out[...] + part_out).reshape(acc_out.shape)
    keep_in[...] = acc_in[:, pl.ds(xh, 1)].reshape(keep_in.shape)
    send_in[...] = acc_in[:, pl.ds(1 - xh, 1)].reshape(send_in.shape).astype(bf16)
    keep_out[...] = acc_out[xh]
    send_out[...] = acc_out[1 - xh].astype(bf16)


def piece_scratch(pieces, tile):
    count = sum(p.shape[0] for p in pieces)
    feat = pieces[0].shape[1] // 2
    return [
        pltpu.VMEM((count, 2 * feat), bf16),
        pltpu.VMEM((count, tile), bf16),
        pltpu.VMEM((count, tile), bf16),
        pltpu.VMEM((feat, tile), bf16),
        pltpu.VMEM((tile, feat), bf16),
        pltpu.SemaphoreType.DMA((2,)),
    ]


def weight_grads(pieces, w_in, w_out, sums, parts, name):
    feat, hidden = w_in.shape[1:]
    tile = hidden // parts
    count = sum(p.shape[0] for p in pieces)
    return pl.pallas_call(
        functools.partial(grads_body, len(pieces), not sums),
        in_specs=[IN_VMEM] * len(pieces) + [IN_PLACE] * 2 + [IN_VMEM] * len(sums),
        out_specs=[IN_VMEM] * 2,
        out_shape=[
            jax.ShapeDtypeStruct((feat, tile), f32),
            jax.ShapeDtypeStruct((tile, feat), f32),
        ],
        scratch_shapes=piece_scratch(pieces, tile),
        compiler_params=params(16),
        name=name,
    )(*pieces, pinned(w_in), pinned(w_out), *sums)


def last_weight_grads(pieces, w_in, w_out, sums, parts):
    feat, hidden = w_in.shape[1:]
    tile = hidden // parts
    own = feat // (parts * XH)
    count = sum(p.shape[0] for p in pieces)
    return pl.pallas_call(
        functools.partial(last_grads_body, len(pieces)),
        in_specs=[IN_VMEM] * len(pieces) + [IN_PLACE] * 2 + [IN_VMEM] * 2,
        out_specs=[IN_VMEM] * 4,
        out_shape=[
            jax.ShapeDtypeStruct((parts, own, tile), f32),
            jax.ShapeDtypeStruct((parts, own, tile), bf16),
            jax.ShapeDtypeStruct((tile // XH, feat), f32),
            jax.ShapeDtypeStruct((tile // XH, feat), bf16),
        ],
        scratch_shapes=[
            pltpu.VMEM((parts, XH, own, tile), f32),
            pltpu.VMEM((XH, tile // XH, feat), f32),
        ]
        + piece_scratch(pieces, tile),
        compiler_params=params(20),
        name="far_grads",
    )(*pieces, pinned(w_in), pinned(w_out), *sums)


def widen_body(in_ref, out_ref):
    parts, _, tile = in_ref.shape
    for i in range(parts):
        out_ref[0, :, i * tile : (i + 1) * tile] = in_ref[i].astype(f32)


def widen(spread):
    parts, own, tile = spread.shape
    return pl.pallas_call(
        widen_body,
        in_specs=[IN_VMEM],
        out_specs=IN_VMEM,
        out_shape=jax.ShapeDtypeStruct((1, own, parts * tile), f32),
        compiler_params=params(4),
        name="widen",
    )(spread)


def token_logits_body(
    back_ref, x_hbm, g_hbm, disp_ref, comb_ref, gl_ref, slots_ref, router_ref,
    mix, x_ref, g_ref, x_sem, g_sem
):
    experts, images, double = back_ref.shape
    feat = double // 2
    width = GROUP * PATCHES
    rows = GROUP * experts
    total = experts * images
    x_copies = block_copies(x_hbm, x_ref, x_sem)
    g_copies = block_copies(g_hbm, g_ref, g_sem)
    for x_copy, g_copy in zip(x_copies, g_copies):
        g_copy.start()
        x_copy.start()
    mix[...] = jnp.dot(
        swap_matrix(total, images),
        back_ref[...].reshape(total, double),
        preferred_element_type=f32,
    ).astype(bf16)
    image = lane_images(width)

    def picked(both):
        out = jnp.zeros((experts, width), f32)
        for i in range(GROUP):
            out = jnp.where(image == i, both[i * experts : (i + 1) * experts], out)
        return out

    router_sum = None
    for b in range(images // GROUP):
        g_copies[b].wait()
        x_copies[b].wait()
        x = x_ref[b * width : (b + 1) * width, :]
        g = g_ref[b * width : (b + 1) * width, :]
        block = mix[b * rows : (b + 1) * rows, :]
        slots_ref[b] = block[:, feat:]
        grad_comb = picked(contract(block[:, :feat], g, 1, 1))
        grad_disp = picked(contract(block[:, feat:], x, 1, 1))
        dispatch = disp_ref[b]
        combine = comb_ref[b]
        comb_part = combine * (grad_comb - jnp.sum(combine * grad_comb, axis=0, keepdims=True))
        disp_part = dispatch * (
            grad_disp - per_image(dispatch * grad_disp, image, jnp.sum, 0.0)
        )
        grad_logits = (comb_part + disp_part).astype(bf16)
        gl_ref[b] = grad_logits
        part = jnp.dot(grad_logits, x, preferred_element_type=f32)
        router_sum = part if router_sum is None else router_sum + part
    router_ref[...] = router_sum


def token_logits(back, tokens, g_outputs, dispatch, combine):
    experts, images, double = back.shape
    rows, feat = tokens.shape
    steps, _, width = dispatch.shape
    return pl.pallas_call(
        token_logits_body,
        in_specs=[IN_VMEM, IN_PLACE, IN_PLACE, IN_VMEM, IN_VMEM],
        out_specs=[IN_VMEM] * 3,
        out_shape=[
            jax.ShapeDtypeStruct((steps, experts, width), bf16),
            jax.ShapeDtypeStruct((steps, GROUP * experts, feat), bf16),
            jax.ShapeDtypeStruct((experts, feat), f32),
        ],
        scratch_shapes=[
            pltpu.VMEM((experts * images, double), bf16),
            pltpu.VMEM((rows, feat), bf16),
            pltpu.VMEM((rows, feat), bf16),
            pltpu.SemaphoreType.DMA((steps,)),
            pltpu.SemaphoreType.DMA((steps,)),
        ],
        compiler_params=params(20),
        name="token_logits",
    )(back, pinned(tokens), pinned(g_outputs), dispatch, combine)


def token_grads_body(gl_ref, slots_ref, disp_ref, rt_ref, out_ref):
    image = lane_images(gl_ref.shape[2])
    left = jnp.concatenate([per_slot_rows(disp_ref[0], image), gl_ref[0]], axis=0)
    right = jnp.concatenate([slots_ref[0], rt_ref[...]], axis=0)
    out_ref[...] = contract(left, right, 0, 0).astype(bf16)


def token_grads(grad_logits, slots, dispatch, rt):
    steps, experts, width = grad_logits.shape
    feat = slots.shape[2]
    return pl.pallas_call(
        token_grads_body,
        grid=(steps,),
        in_specs=[
            pl.BlockSpec((1, experts, width), lambda i: (i, 0, 0)),
            pl.BlockSpec((1, GROUP * experts, feat), lambda i: (i, 0, 0)),
            pl.BlockSpec((1, experts, width), lambda i: (i, 0, 0)),
            pl.BlockSpec((experts, feat), lambda i: (0, 0)),
        ],
        out_specs=pl.BlockSpec((width, feat), lambda i: (i, 0)),
        out_shape=jax.ShapeDtypeStruct((steps * width, feat), bf16),
        compiler_params=params(12),
        name="token_grads",
    )(grad_logits, slots, dispatch, rt)


def shift(value, axis, by, count):
    return lax.ppermute(value, axis, [(i, (i + by) % count) for i in range(count)])


def everywhere_sum(value, sizes):
    for axis, count in sizes:
        value = sum([shift(value, axis, by, count) for by in range(1, count)], value)
    return value


def solution(mesh):
    dp, experts = mesh.shape["dp"], mesh.shape["expert"]
    ny = dp // XH
    inner = (("core", 2), ("xl", 2), ("z", experts // 4))
    fine = Mesh(
        mesh.devices.reshape(ny, XH, experts // 4, 2, 2), ("y", "xh", "z", "xl", "core")
    )
    dp_axes = ("y", "xh")
    ex_axes = ("z", "xl", "core")
    sizes = inner + (("y", ny), ("xh", XH))

    def over_experts(value):
        return lax.all_to_all(value, ex_axes, split_axis=0, concat_axis=0, tiled=True)

    def on_device(tokens, router, w_in, w_out, g_outputs):
        rt = router.T
        slots, dispatch, combine = token_forward(tokens, rt, g_outputs)
        rows = over_experts(slots).reshape(-1, slots.shape[2])
        mid = rows.shape[0] // 2
        right = shift(rows, "y", 1, ny)
        left = shift(rows, "y", ny - 1, ny)
        results = expert_rows(rows, w_in, w_out)
        back = over_experts(results.reshape(slots.shape))
        own_sums = weight_grads((rows,), w_in, w_out, (), ny, "own_grads")
        far_a = shift(right[:mid], "y", 1, ny)
        far_b = shift(left[mid:], "y", ny - 1, ny)
        near_sums = weight_grads((right, left), w_in, w_out, tuple(own_sums), ny, "near_grads")
        back, near_sums = lax.optimization_barrier((back, tuple(near_sums)))
        grad_logits, slot_grads, router_term = token_logits(
            back, tokens, g_outputs, dispatch, combine
        )
        keep_in, send_in, keep_out, send_out = last_weight_grads(
            (far_a, far_b), w_in, w_out, near_sums, ny
        )
        came_in = shift(send_in, "xh", 1, XH)
        came_out = shift(send_out, "xh", 1, XH)
        part_in = (keep_in + came_in.astype(f32)).astype(bf16)
        spread = lax.all_to_all(part_in, "y", split_axis=0, concat_axis=0, tiled=True)
        grad_first = widen(spread)
        grad_second = keep_out + came_out.astype(f32)
        grad_router = everywhere_sum(router_term, sizes).T
        grad_tok = token_grads(grad_logits, slot_grads, dispatch, rt)
        return grad_tok, grad_router, grad_first, grad_second[None]

    return jax.shard_map(
        on_device,
        mesh=fine,
        in_specs=(
            P(dp_axes + ex_axes, None),
            P(),
            P(ex_axes, None, None),
            P(ex_axes, None, None),
            P(dp_axes + ex_axes, None),
        ),
        out_specs=(
            P(dp_axes + ex_axes, None),
            P(),
            P(ex_axes, dp_axes, None),
            P(ex_axes, dp_axes, None),
        ),
        check_vma=False,
    )
```

```python
import functools

import jax
import jax.numpy as jnp
from jax import lax
from jax.experimental import pallas as pl
from jax.experimental.pallas import tpu as pltpu
from jax.sharding import Mesh, PartitionSpec as P

PATCHES = 196
GROUP = 4
XH = 2
MIB = 1024 * 1024
GELU_C = 0.7978845608028654
GELU_A = 0.044715

f32 = jnp.float32
bf16 = jnp.bfloat16


def contract(left, right, left_dim, right_dim):
    return lax.dot_general(
        left, right, (((left_dim,), (right_dim,)), ((), ())), preferred_element_type=f32
    )


def params(mib):
    return pltpu.CompilerParams(vmem_limit_bytes=mib * MIB)


def pinned(value):
    return pltpu.with_memory_space_constraint(value, pltpu.HBM)


IN_VMEM = pl.BlockSpec(memory_space=pltpu.VMEM)
IN_PLACE = pl.BlockSpec(memory_space=pltpu.HBM)


def gelu_parts(x):
    x2 = x * x
    th = jnp.tanh(GELU_C * x * (1.0 + GELU_A * x2))
    cdf = 0.5 + 0.5 * th
    slope = cdf + (0.5 * GELU_C) * x * (1.0 - th * th) * (1.0 + (3.0 * GELU_A) * x2)
    return x * cdf, slope


def lane_images(width):
    lane = lax.broadcasted_iota(jnp.int32, (1, width), 1)
    image = jnp.zeros_like(lane)
    for i in range(1, width // PATCHES):
        image = image + (lane >= i * PATCHES).astype(jnp.int32)
    return image


def per_image(values, image, reduce, start):
    width = values.shape[1]
    out = jnp.zeros_like(values)
    for i in range(GROUP):
        low = i * PATCHES // 128 * 128
        high = min(-(-(i + 1) * PATCHES // 128) * 128, width)
        part = jnp.where(image[:, low:high] == i, values[:, low:high], start)
        own = reduce(part, axis=1, keepdims=True)
        out = jnp.where(image == i, own, out)
    return out


def per_slot_rows(weights, image):
    return jnp.concatenate(
        [jnp.where(image == i, weights, 0.0) for i in range(GROUP)], axis=0
    ).astype(bf16)


def swap_matrix(total, inner):
    outer = total // inner
    out_row = lax.broadcasted_iota(jnp.int32, (total, total), 0)
    in_row = lax.broadcasted_iota(jnp.int32, (total, total), 1)
    wanted = (out_row % outer) * inner + out_row // outer
    return (in_row == wanted).astype(f32).astype(bf16)


def block_copies(src, dst, sem):
    width = GROUP * PATCHES
    return [
        pltpu.make_async_copy(
            src.at[pl.ds(b * width, width)], dst.at[pl.ds(b * width, width)], sem.at[b]
        )
        for b in range(src.shape[0] // width)
    ]


def token_forward_body(
    rt_hbm, x_hbm, g_hbm, slots_ref, disp_ref, comb_ref,
    rt_ref, x_ref, g_ref, acc, rt_sem, x_sem, g_sem
):
    experts, images, double = slots_ref.shape
    feat = double // 2
    width = GROUP * PATCHES
    steps = images // GROUP
    rows = GROUP * experts
    total = experts * images

    x_copies = block_copies(x_hbm, x_ref, x_sem)
    g_copies = block_copies(g_hbm, g_ref, g_sem)
    rt_copy = pltpu.make_async_copy(rt_hbm, rt_ref, rt_sem)
    for copy in [rt_copy] + x_copies + g_copies:
        copy.start()
    rt_copy.wait()
    image = lane_images(width)
    rt = rt_ref[...]
    spread = []
    for b in range(steps):
        x_copies[b].wait()
        x = x_ref[b * width : (b + 1) * width, :]
        logits = contract(rt, x, 1, 1)
        top = per_image(logits, image, jnp.max, -jnp.inf)
        raised = jnp.exp(logits - top)
        dispatch = raised / per_image(raised, image, jnp.sum, 0.0)
        raised_e = jnp.exp(logits - jnp.max(logits, axis=0, keepdims=True))
        combine = raised_e / jnp.sum(raised_e, axis=0, keepdims=True)
        disp_ref[b] = dispatch
        comb_ref[b] = combine
        spread.append(per_slot_rows(combine, image))
        acc[b * rows : (b + 1) * rows, :feat] = jnp.dot(
            per_slot_rows(dispatch, image), x, preferred_element_type=f32
        ).astype(bf16)
    for b in range(steps):
        g_copies[b].wait()
        acc[b * rows : (b + 1) * rows, feat:] = jnp.dot(
            spread[b], g_ref[b * width : (b + 1) * width, :], preferred_element_type=f32
        ).astype(bf16)
    slots_ref[...] = (
        jnp.dot(swap_matrix(total, experts), acc[...], preferred_element_type=f32)
        .astype(bf16)
        .reshape(experts, images, double)
    )


def token_forward(tokens, rt, g_outputs):
    rows, feat = tokens.shape
    experts = rt.shape[0]
    images = rows // PATCHES
    width = GROUP * PATCHES
    steps = rows // width
    return pl.pallas_call(
        token_forward_body,
        in_specs=[IN_PLACE] * 3,
        out_specs=[IN_VMEM, IN_VMEM, IN_VMEM],
        out_shape=[
            jax.ShapeDtypeStruct((experts, images, 2 * feat), bf16),
            jax.ShapeDtypeStruct((steps, experts, width), f32),
            jax.ShapeDtypeStruct((steps, experts, width), f32),
        ],
        scratch_shapes=[
            pltpu.VMEM((experts, feat), bf16),
            pltpu.VMEM((rows, feat), bf16),
            pltpu.VMEM((rows, feat), bf16),
            pltpu.VMEM((experts * images, 2 * feat), bf16),
            pltpu.SemaphoreType.DMA(()),
            pltpu.SemaphoreType.DMA((steps,)),
            pltpu.SemaphoreType.DMA((steps,)),
        ],
        compiler_params=params(20),
        name="token_forward",
    )(pinned(rt), pinned(tokens), pinned(g_outputs))


def expert_body(rows_ref, w1_ref, w2_ref, out_ref):
    feat = w1_ref.shape[1]
    hidden = w1_ref.shape[2]
    tile = 768
    rows = rows_ref[:, :feat]
    grads = rows_ref[:, feat:]
    made, back = None, None
    for low in range(0, hidden, tile):
        w1 = w1_ref[0, :, low : low + tile]
        w2 = w2_ref[0, low : low + tile, :]
        act, slope = gelu_parts(jnp.dot(rows, w1, preferred_element_type=f32))
        part = jnp.dot(act.astype(bf16), w2, preferred_element_type=f32)
        made = part if made is None else made + part
        grad_pre = (contract(grads, w2, 1, 1) * slope).astype(bf16)
        part = contract(grad_pre, w1, 1, 1)
        back = part if back is None else back + part
    out_ref[:, :feat] = made.astype(bf16)
    out_ref[:, feat:] = back.astype(bf16)


def expert_rows(rows, w_in, w_out):
    return pl.pallas_call(
        expert_body,
        in_specs=[IN_VMEM] * 3,
        out_specs=IN_VMEM,
        out_shape=jax.ShapeDtypeStruct(rows.shape, bf16),
        compiler_params=params(12),
        name="expert_rows",
    )(rows, w_in, w_out)


def slice_copies(w1_hbm, w2_hbm, w1, w2, sem):
    tile = w1.shape[1]
    low = pl.multiple_of(lax.axis_index("y") * tile, tile)
    return (
        pltpu.make_async_copy(w1_hbm.at[0, :, pl.ds(low, tile)], w1, sem.at[0]),
        pltpu.make_async_copy(w2_hbm.at[0, pl.ds(low, tile), :], w2, sem.at[1]),
    )


def gather_pieces(piece_refs, both):
    at = 0
    for piece in piece_refs:
        both[at : at + piece.shape[0], :] = piece[...]
        at += piece.shape[0]


def slice_terms(both, w1, w2, act_all, pre_all, loads):
    feat = w1.shape[0]
    rows = both[:, :feat]
    grads = both[:, feat:]
    loads[0].wait()
    act, slope = gelu_parts(jnp.dot(rows, w1[...], preferred_element_type=f32))
    act_all[...] = act.astype(bf16)
    loads[1].wait()
    pre_all[...] = (contract(grads, w2[...], 1, 1) * slope).astype(bf16)


def near_grads_body(count, *refs):
    pieces, (w1_hbm, w2_hbm) = refs[:count], refs[count : count + 2]
    in_hbm, out_hbm, sum_in, sum_out, out_sem, both, act_all, pre_all, w1, w2, sem = refs[count + 2 :]
    feat = w1.shape[0]
    loads = slice_copies(w1_hbm, w2_hbm, w1, w2, sem)
    for load in loads:
        load.start()
    gather_pieces(pieces, both)
    slice_terms(both, w1, w2, act_all, pre_all, loads)
    stores = (
        pltpu.make_async_copy(sum_out, out_hbm, out_sem.at[0]),
        pltpu.make_async_copy(sum_in, in_hbm, out_sem.at[1]),
    )
    sum_out[...] = contract(act_all[...], both[:, feat:], 0, 0)
    stores[0].start()
    sum_in[...] = contract(both[:, :feat], pre_all[...], 0, 0)
    stores[1].start()
    for store in stores:
        store.wait()


def far_grads_body(count, *refs):
    pieces, (w1_hbm, w2_hbm, in_hbm, out_hbm) = refs[:count], refs[count : count + 4]
    keep_in, send_in, keep_out, send_out, *refs = refs[count + 4 :]
    acc_in, acc_out, sum_in, sum_out, in_sem, both, act_all, pre_all, w1, w2, sem = refs
    feat = w1.shape[0]
    xh = lax.axis_index("xh")
    loads = slice_copies(w1_hbm, w2_hbm, w1, w2, sem)
    sums = (
        pltpu.make_async_copy(in_hbm, sum_in, in_sem.at[0]),
        pltpu.make_async_copy(out_hbm, sum_out, in_sem.at[1]),
    )
    for load in loads + sums:
        load.start()
    gather_pieces(pieces, both)
    slice_terms(both, w1, w2, act_all, pre_all, loads)
    part_in = contract(both[:, :feat], pre_all[...], 0, 0)
    sums[0].wait()
    acc_in[...] = (sum_in[...] + part_in).reshape(acc_in.shape)
    send_in[...] = acc_in[:, pl.ds(1 - xh, 1)].reshape(send_in.shape).astype(bf16)
    keep_in[...] = acc_in[:, pl.ds(xh, 1)].reshape(keep_in.shape)
    part_out = contract(act_all[...], both[:, feat:], 0, 0)
    sums[1].wait()
    acc_out[...] = (sum_out[...] + part_out).reshape(acc_out.shape)
    send_out[...] = acc_out[1 - xh].astype(bf16)
    keep_out[...] = acc_out[xh]


def piece_scratch(pieces, tile):
    count = sum(p.shape[0] for p in pieces)
    feat = pieces[0].shape[1] // 2
    return [
        pltpu.VMEM((feat, tile), f32),
        pltpu.VMEM((tile, feat), f32),
        pltpu.SemaphoreType.DMA((2,)),
        pltpu.VMEM((count, 2 * feat), bf16),
        pltpu.VMEM((count, tile), bf16),
        pltpu.VMEM((count, tile), bf16),
        pltpu.VMEM((feat, tile), bf16),
        pltpu.VMEM((tile, feat), bf16),
        pltpu.SemaphoreType.DMA((2,)),
    ]


def near_grads(pieces, w_in, w_out, parts):
    feat, hidden = w_in.shape[1:]
    tile = hidden // parts
    return pl.pallas_call(
        functools.partial(near_grads_body, len(pieces)),
        in_specs=[IN_VMEM] * len(pieces) + [IN_PLACE] * 2,
        out_specs=[IN_PLACE] * 2,
        out_shape=[
            pltpu.HBM((feat, tile), f32),
            pltpu.HBM((tile, feat), f32),
        ],
        scratch_shapes=piece_scratch(pieces, tile),
        compiler_params=params(20),
        name="near_grads",
    )(*pieces, pinned(w_in), pinned(w_out))


def far_grads(pieces, w_in, w_out, sums, parts):
    feat, hidden = w_in.shape[1:]
    tile = hidden // parts
    own = feat // (parts * XH)
    return pl.pallas_call(
        functools.partial(far_grads_body, len(pieces)),
        in_specs=[IN_VMEM] * len(pieces) + [IN_PLACE] * 4,
        out_specs=[IN_VMEM] * 4,
        out_shape=[
            jax.ShapeDtypeStruct((parts, own, tile), f32),
            jax.ShapeDtypeStruct((parts, own, tile), bf16),
            jax.ShapeDtypeStruct((tile // XH, feat), f32),
            jax.ShapeDtypeStruct((tile // XH, feat), bf16),
        ],
        scratch_shapes=[
            pltpu.VMEM((parts, XH, own, tile), f32),
            pltpu.VMEM((XH, tile // XH, feat), f32),
        ]
        + piece_scratch(pieces, tile),
        compiler_params=params(24),
        name="far_grads",
    )(*pieces, pinned(w_in), pinned(w_out), *[pinned(v) for v in sums])


def widen_body(in_ref, out_ref):
    parts, _, tile = in_ref.shape
    for i in range(parts):
        out_ref[0, :, i * tile : (i + 1) * tile] = in_ref[i].astype(f32)


def widen(spread):
    parts, own, tile = spread.shape
    return pl.pallas_call(
        widen_body,
        in_specs=[IN_VMEM],
        out_specs=IN_VMEM,
        out_shape=jax.ShapeDtypeStruct((1, own, parts * tile), f32),
        compiler_params=params(4),
        name="widen",
    )(spread)


def token_logits_body(
    back_ref, x_hbm, g_hbm, disp_ref, comb_ref, gl_ref, slots_ref, router_ref,
    mix, x_ref, g_ref, x_sem, g_sem
):
    experts, images, double = back_ref.shape
    feat = double // 2
    width = GROUP * PATCHES
    rows = GROUP * experts
    total = experts * images
    x_copies = block_copies(x_hbm, x_ref, x_sem)
    g_copies = block_copies(g_hbm, g_ref, g_sem)
    for x_copy, g_copy in zip(x_copies, g_copies):
        g_copy.start()
        x_copy.start()
    mix[...] = jnp.dot(
        swap_matrix(total, images),
        back_ref[...].reshape(total, double),
        preferred_element_type=f32,
    ).astype(bf16)
    image = lane_images(width)

    def picked(both):
        out = jnp.zeros((experts, width), f32)
        for i in range(GROUP):
            out = jnp.where(image == i, both[i * experts : (i + 1) * experts], out)
        return out

    router_sum = None
    for b in range(images // GROUP):
        g_copies[b].wait()
        x_copies[b].wait()
        x = x_ref[b * width : (b + 1) * width, :]
        g = g_ref[b * width : (b + 1) * width, :]
        block = mix[b * rows : (b + 1) * rows, :]
        slots_ref[b] = block[:, feat:]
        grad_comb = picked(contract(block[:, :feat], g, 1, 1))
        grad_disp = picked(contract(block[:, feat:], x, 1, 1))
        dispatch = disp_ref[b]
        combine = comb_ref[b]
        comb_part = combine * (grad_comb - jnp.sum(combine * grad_comb, axis=0, keepdims=True))
        disp_part = dispatch * (
            grad_disp - per_image(dispatch * grad_disp, image, jnp.sum, 0.0)
        )
        grad_logits = (comb_part + disp_part).astype(bf16)
        gl_ref[b] = grad_logits
        part = jnp.dot(grad_logits, x, preferred_element_type=f32)
        router_sum = part if router_sum is None else router_sum + part
    router_ref[...] = router_sum


def token_logits(back, tokens, g_outputs, dispatch, combine):
    experts, images, double = back.shape
    rows, feat = tokens.shape
    steps, _, width = dispatch.shape
    return pl.pallas_call(
        token_logits_body,
        in_specs=[IN_VMEM, IN_PLACE, IN_PLACE, IN_VMEM, IN_VMEM],
        out_specs=[IN_VMEM] * 3,
        out_shape=[
            jax.ShapeDtypeStruct((steps, experts, width), bf16),
            jax.ShapeDtypeStruct((steps, GROUP * experts, feat), bf16),
            jax.ShapeDtypeStruct((experts, feat), f32),
        ],
        scratch_shapes=[
            pltpu.VMEM((experts * images, double), bf16),
            pltpu.VMEM((rows, feat), bf16),
            pltpu.VMEM((rows, feat), bf16),
            pltpu.SemaphoreType.DMA((steps,)),
            pltpu.SemaphoreType.DMA((steps,)),
        ],
        compiler_params=params(20),
        name="token_logits",
    )(back, pinned(tokens), pinned(g_outputs), dispatch, combine)


def token_grads_body(gl_ref, slots_ref, disp_ref, rt_ref, out_ref):
    image = lane_images(gl_ref.shape[2])
    left = jnp.concatenate([per_slot_rows(disp_ref[0], image), gl_ref[0]], axis=0)
    right = jnp.concatenate([slots_ref[0], rt_ref[...]], axis=0)
    out_ref[...] = contract(left, right, 0, 0).astype(bf16)


def token_grads(grad_logits, slots, dispatch, rt):
    steps, experts, width = grad_logits.shape
    feat = slots.shape[2]
    return pl.pallas_call(
        token_grads_body,
        grid=(steps,),
        in_specs=[
            pl.BlockSpec((1, experts, width), lambda i: (i, 0, 0)),
            pl.BlockSpec((1, GROUP * experts, feat), lambda i: (i, 0, 0)),
            pl.BlockSpec((1, experts, width), lambda i: (i, 0, 0)),
            pl.BlockSpec((experts, feat), lambda i: (0, 0)),
        ],
        out_specs=pl.BlockSpec((width, feat), lambda i: (i, 0)),
        out_shape=jax.ShapeDtypeStruct((steps * width, feat), bf16),
        compiler_params=params(12),
        name="token_grads",
    )(grad_logits, slots, dispatch, rt)


def shift(value, axis, by, count):
    return lax.ppermute(value, axis, [(i, (i + by) % count) for i in range(count)])


def axis_sum(value, axis, count):
    return sum([shift(value, axis, by, count) for by in range(1, count)], value)


def solution(mesh):
    dp, experts = mesh.shape["dp"], mesh.shape["expert"]
    ny, nz = dp // XH, experts // 4
    fine = Mesh(
        mesh.devices.reshape(ny, XH, nz, 2, 2), ("y", "xh", "z", "xl", "core")
    )
    dp_axes = ("y", "xh")
    ex_axes = ("z", "xl", "core")

    def over_experts(value):
        return lax.all_to_all(value, ex_axes, split_axis=0, concat_axis=0, tiled=True)

    def on_device(tokens, router, w_in, w_out, g_outputs):
        rt = router.T
        slots, dispatch, combine = token_forward(tokens, rt, g_outputs)
        rows = over_experts(slots).reshape(-1, slots.shape[2])
        mid = rows.shape[0] // 2
        low, high = [
            pltpu.with_memory_space_constraint(v, pltpu.VMEM) for v in (rows[:mid], rows[mid:])
        ]
        right_low = shift(low, "y", 1, ny)
        left_high = shift(high, "y", ny - 1, ny)
        right_high = shift(high, "y", 1, ny)
        left_low = shift(low, "y", ny - 1, ny)
        far_low = shift(right_low, "y", 1, ny)
        far_high = shift(left_high, "y", ny - 1, ny)
        results = expert_rows(rows, w_in, w_out)
        back = over_experts(results.reshape(slots.shape))
        sums = near_grads(
            (rows, right_low, left_high, right_high, left_low), w_in, w_out, ny
        )
        back, sums = lax.optimization_barrier((back, tuple(sums)))
        grad_logits, slot_grads, router_term = token_logits(
            back, tokens, g_outputs, dispatch, combine
        )
        keep_in, send_in, keep_out, send_out = far_grads((far_low, far_high), w_in, w_out, sums, ny)
        came_in = shift(send_in, "xh", 1, XH)
        came_out = shift(send_out, "xh", 1, XH)
        total = axis_sum(axis_sum(router_term, "core", 2), "z", nz)
        total, came_in = lax.optimization_barrier((total, came_in))
        part_in = (keep_in + came_in.astype(f32)).astype(bf16)
        spread = lax.all_to_all(part_in, "y", split_axis=0, concat_axis=0, tiled=True)
        total = axis_sum(axis_sum(total, "y", ny), "xl", 2)
        total, came_out, spread = lax.optimization_barrier((total, came_out, spread))
        grad_first = widen(spread)
        grad_router = axis_sum(total, "xh", XH).T
        grad_second = keep_out + came_out.astype(f32)
        grad_tok = token_grads(grad_logits, slot_grads, dispatch, rt)
        return grad_tok, grad_router, grad_first, grad_second[None]

    return jax.shard_map(
        on_device,
        mesh=fine,
        in_specs=(
            P(dp_axes + ex_axes, None),
            P(),
            P(ex_axes, None, None),
            P(ex_axes, None, None),
            P(dp_axes + ex_axes, None),
        ),
        out_specs=(
            P(dp_axes + ex_axes, None),
            P(),
            P(ex_axes, dp_axes, None),
            P(ex_axes, dp_axes, None),
        ),
        check_vma=False,
    )
```

```python
import functools

import jax
import jax.numpy as jnp
from jax import lax
from jax.experimental import pallas as pl
from jax.experimental.pallas import tpu as pltpu
from jax.sharding import Mesh, PartitionSpec as P

PATCHES = 196
GROUP = 4
XH = 2
MIB = 1024 * 1024
GELU_C = 0.7978845608028654
GELU_A = 0.044715

f32 = jnp.float32
bf16 = jnp.bfloat16


def contract(left, right, left_dim, right_dim):
    return lax.dot_general(
        left, right, (((left_dim,), (right_dim,)), ((), ())), preferred_element_type=f32
    )


def params(mib):
    return pltpu.CompilerParams(vmem_limit_bytes=mib * MIB)


def pinned(value):
    return pltpu.with_memory_space_constraint(value, pltpu.HBM)


IN_VMEM = pl.BlockSpec(memory_space=pltpu.VMEM)
IN_PLACE = pl.BlockSpec(memory_space=pltpu.HBM)


def gelu_parts(x):
    x2 = x * x
    th = jnp.tanh(GELU_C * x * (1.0 + GELU_A * x2))
    cdf = 0.5 + 0.5 * th
    slope = cdf + (0.5 * GELU_C) * x * (1.0 - th * th) * (1.0 + (3.0 * GELU_A) * x2)
    return x * cdf, slope


def lane_images(width):
    lane = lax.broadcasted_iota(jnp.int32, (1, width), 1)
    image = jnp.zeros_like(lane)
    for i in range(1, width // PATCHES):
        image = image + (lane >= i * PATCHES).astype(jnp.int32)
    return image


def per_image(values, image, reduce, start):
    width = values.shape[1]
    out = jnp.zeros_like(values)
    for i in range(GROUP):
        low = i * PATCHES // 128 * 128
        high = min(-(-(i + 1) * PATCHES // 128) * 128, width)
        part = jnp.where(image[:, low:high] == i, values[:, low:high], start)
        own = reduce(part, axis=1, keepdims=True)
        out = jnp.where(image == i, own, out)
    return out


def inverse_sum(values, axis, keepdims):
    return 1.0 / jnp.sum(values, axis=axis, keepdims=keepdims)


def per_slot_rows(weights, image):
    return jnp.concatenate(
        [jnp.where(image == i, weights, 0.0) for i in range(GROUP)], axis=0
    ).astype(bf16)


def swap_matrix(total, inner):
    outer = total // inner
    out_row = lax.broadcasted_iota(jnp.int32, (total, total), 0)
    in_row = lax.broadcasted_iota(jnp.int32, (total, total), 1)
    wanted = (out_row % outer) * inner + out_row // outer
    return (in_row == wanted).astype(f32).astype(bf16)


def block_copies(src, dst, sem):
    width = GROUP * PATCHES
    return [
        pltpu.make_async_copy(
            src.at[pl.ds(b * width, width)], dst.at[pl.ds(b * width, width)], sem.at[b]
        )
        for b in range(src.shape[0] // width)
    ]


def token_forward_body(
    rt_hbm, x_hbm, g_hbm, slots_ref, disp_hbm, comb_hbm,
    rt_ref, disp_ref, comb_ref, x_ref, g_ref, acc, x_sem, g_sem, rt_sem, disp_sem, comb_sem
):
    experts, images, double = slots_ref.shape
    feat = double // 2
    width = GROUP * PATCHES
    steps = images // GROUP
    rows = GROUP * experts
    total = experts * images

    x_copies = block_copies(x_hbm, x_ref, x_sem)
    g_copies = block_copies(g_hbm, g_ref, g_sem)
    rt_copy = pltpu.make_async_copy(rt_hbm, rt_ref, rt_sem)
    for copy in [rt_copy] + x_copies + g_copies:
        copy.start()
    weight_copies = [
        pltpu.make_async_copy(disp_ref, disp_hbm, disp_sem),
        pltpu.make_async_copy(comb_ref, comb_hbm, comb_sem),
    ]
    image = lane_images(width)
    rt_copy.wait()
    rt = rt_ref[...]
    spread = {}
    for first in range(0, steps, 2):
        pair = (first, first + 1)
        logits, own = {}, {}
        for b in pair:
            x_copies[b].wait()
        for b in pair:
            logits[b] = contract(rt, x_ref[b * width : (b + 1) * width, :], 1, 1)
        for b in pair:
            top = per_image(logits[b], image, jnp.max, -jnp.inf)
            raised = jnp.exp(logits[b] - top)
            dispatch = raised * per_image(raised, image, inverse_sum, 0.0)
            raised_e = jnp.exp(logits[b] - jnp.max(logits[b], axis=0, keepdims=True))
            combine = raised_e * inverse_sum(raised_e, axis=0, keepdims=True)
            disp_ref[b] = dispatch
            comb_ref[b] = combine
            spread[b] = per_slot_rows(combine, image)
            own[b] = per_slot_rows(dispatch, image)
        for b in pair:
            acc[b * rows : (b + 1) * rows, :feat] = jnp.dot(
                own[b], x_ref[b * width : (b + 1) * width, :], preferred_element_type=f32
            ).astype(bf16)
    for copy in weight_copies:
        copy.start()
    for b in range(steps):
        g_copies[b].wait()
    for b in range(steps):
        acc[b * rows : (b + 1) * rows, feat:] = jnp.dot(
            spread[b], g_ref[b * width : (b + 1) * width, :], preferred_element_type=f32
        ).astype(bf16)
    slots_ref[...] = (
        jnp.dot(swap_matrix(total, experts), acc[...], preferred_element_type=f32)
        .astype(bf16)
        .reshape(experts, images, double)
    )
    for copy in weight_copies:
        copy.wait()


def token_forward(tokens, rt, g_outputs):
    rows, feat = tokens.shape
    experts = rt.shape[0]
    images = rows // PATCHES
    width = GROUP * PATCHES
    steps = rows // width
    return pl.pallas_call(
        token_forward_body,
        in_specs=[IN_PLACE] * 3,
        out_specs=[IN_VMEM, IN_PLACE, IN_PLACE],
        out_shape=[
            jax.ShapeDtypeStruct((experts, images, 2 * feat), bf16),
            pltpu.HBM((steps, experts, width), f32),
            pltpu.HBM((steps, experts, width), f32),
        ],
        scratch_shapes=[
            pltpu.VMEM((experts, feat), bf16),
            pltpu.VMEM((steps, experts, width), f32),
            pltpu.VMEM((steps, experts, width), f32),
            pltpu.VMEM((rows, feat), bf16),
            pltpu.VMEM((rows, feat), bf16),
            pltpu.VMEM((experts * images, 2 * feat), bf16),
            pltpu.SemaphoreType.DMA((steps,)),
            pltpu.SemaphoreType.DMA((steps,)),
            pltpu.SemaphoreType.DMA(()),
            pltpu.SemaphoreType.DMA(()),
            pltpu.SemaphoreType.DMA(()),
        ],
        compiler_params=params(20),
        name="token_forward",
    )(pinned(rt), pinned(tokens), pinned(g_outputs))


def hidden_terms(rows, grads, w1, w2):
    act, slope = gelu_parts(jnp.dot(rows, w1, preferred_element_type=f32))
    return act.astype(bf16), (contract(grads, w2, 1, 1) * slope).astype(bf16)


def expert_body(
    rows_ref, w1_ref, w2_ref, out_hbm, act_hbm, pre_hbm, out_ref, act_ref, pre_ref, sem
):
    feat = w1_ref.shape[1]
    hidden = w1_ref.shape[2]
    tile = act_ref.shape[1]
    part_at = lax.axis_index("y")
    rows = rows_ref[:, :feat]
    grads = rows_ref[:, feat:]
    made, back = None, None
    stores = [
        pltpu.make_async_copy(src, dst, sem.at[k])
        for k, (src, dst) in enumerate(
            ((act_ref, act_hbm), (pre_ref, pre_hbm), (out_ref, out_hbm))
        )
    ]
    for i in range(hidden // tile):
        w1 = w1_ref[0, :, i * tile : (i + 1) * tile]
        w2 = w2_ref[0, i * tile : (i + 1) * tile, :]
        act, grad_pre = hidden_terms(rows, grads, w1, w2)

        @pl.when(part_at == i)
        def _():
            act_ref[...] = act
            pre_ref[...] = grad_pre

        if i == hidden // tile - 1:
            stores[0].start()
            stores[1].start()
        part = jnp.dot(act, w2, preferred_element_type=f32)
        made = part if made is None else made + part
        part = contract(grad_pre, w1, 1, 1)
        back = part if back is None else back + part
    out_ref[:, :feat] = made.astype(bf16)
    out_ref[:, feat:] = back.astype(bf16)
    stores[2].start()
    for store in stores:
        store.wait()


def expert_rows(rows, w_in, w_out, parts):
    tile = w_in.shape[2] // parts
    shapes = [rows.shape, (rows.shape[0], tile), (rows.shape[0], tile)]
    return pl.pallas_call(
        expert_body,
        in_specs=[IN_VMEM] * 3,
        out_specs=[IN_PLACE] * 3,
        out_shape=[pltpu.HBM(shape, bf16) for shape in shapes],
        scratch_shapes=[pltpu.VMEM(shape, bf16) for shape in shapes]
        + [pltpu.SemaphoreType.DMA((3,))],
        compiler_params=params(12),
        name="expert_rows",
    )(rows, w_in, w_out)


def slice_copies(w1_hbm, w2_hbm, w1, w2, sem):
    tile = w1.shape[1]
    low = pl.multiple_of(lax.axis_index("y") * tile, tile)
    return (
        pltpu.make_async_copy(w1_hbm.at[0, :, pl.ds(low, tile)], w1, sem.at[0]),
        pltpu.make_async_copy(w2_hbm.at[0, pl.ds(low, tile), :], w2, sem.at[1]),
    )


def stacked_copies(sources, out, sem):
    copies, at = [], 0
    for k, source in enumerate(sources):
        rows = source.shape[0]
        copies.append(pltpu.make_async_copy(source, out.at[pl.ds(at, rows)], sem.at[k]))
        at += rows
    return copies


def join(pieces, low, high, out):
    at = 0
    for piece in pieces:
        out[at : at + piece.shape[0], :] = piece[:, low:high]
        at += piece.shape[0]


def near_terms_body(
    right_ref, left_ref, w1_hbm, w2_hbm, act_hbm, pre_hbm, act, pre, both, w1, w2, sem, out_sem
):
    feat = w1.shape[0]
    loads = slice_copies(w1_hbm, w2_hbm, w1, w2, sem)
    for load in loads:
        load.start()
    join((right_ref, left_ref), 0, 2 * feat, both)
    for load in loads:
        load.wait()
    act[...], pre[...] = hidden_terms(both[:, :feat], both[:, feat:], w1[...], w2[...])
    stores = (
        pltpu.make_async_copy(act, act_hbm, out_sem.at[0]),
        pltpu.make_async_copy(pre, pre_hbm, out_sem.at[1]),
    )
    for store in stores:
        store.start()
    for store in stores:
        store.wait()


def near_terms(right, left, w_in, w_out, parts):
    feat, hidden = w_in.shape[1:]
    tile = hidden // parts
    count = right.shape[0] + left.shape[0]
    return pl.pallas_call(
        near_terms_body,
        in_specs=[IN_VMEM] * 2 + [IN_PLACE] * 2,
        out_specs=[IN_PLACE] * 2,
        out_shape=[pltpu.HBM((count, tile), bf16)] * 2,
        scratch_shapes=[
            pltpu.VMEM((count, tile), bf16),
            pltpu.VMEM((count, tile), bf16),
            pltpu.VMEM((count, 2 * feat), bf16),
            pltpu.VMEM((feat, tile), bf16),
            pltpu.VMEM((tile, feat), bf16),
            pltpu.SemaphoreType.DMA((2,)),
            pltpu.SemaphoreType.DMA((2,)),
        ],
        compiler_params=params(16),
        name="near_terms",
    )(right, left, pinned(w_in), pinned(w_out))


def first_grads_body(
    own_ref, right_ref, left_ref, far_a, far_b, pre_own, pre_near, w1_hbm, w2_hbm,
    keep_ref, send_ref, act_far, rows, pre, far, acc, w1, w2, sem, pre_sem
):
    feat = w1.shape[0]
    xh = lax.axis_index("xh")
    loads = slice_copies(w1_hbm, w2_hbm, w1, w2, sem)
    terms = stacked_copies((pre_own, pre_near), pre, pre_sem)
    for load in terms + list(loads):
        load.start()
    join((own_ref, right_ref, left_ref), 0, feat, rows)
    join((far_a, far_b), 0, 2 * feat, far)
    for load in terms:
        load.wait()
    total = contract(rows[...], pre[...], 0, 0)
    for load in loads:
        load.wait()
    act, pre_far = hidden_terms(far[:, :feat], far[:, feat:], w1[...], w2[...])
    act_far[...] = act
    acc[...] = (total + contract(far[:, :feat], pre_far, 0, 0)).reshape(acc.shape)
    send_ref[...] = acc[:, pl.ds(1 - xh, 1)].reshape(send_ref.shape).astype(bf16)
    keep_ref[...] = acc[:, pl.ds(xh, 1)].reshape(keep_ref.shape)


def first_grads(pieces, pre_own, pre_near, w_in, w_out, parts):
    feat, hidden = w_in.shape[1:]
    tile = hidden // parts
    own = feat // (parts * XH)
    near_count = sum(p.shape[0] for p in pieces[:3])
    far_count = sum(p.shape[0] for p in pieces[3:])
    return pl.pallas_call(
        first_grads_body,
        in_specs=[IN_VMEM] * 5 + [IN_PLACE] * 4,
        out_specs=[IN_VMEM] * 3,
        out_shape=[
            jax.ShapeDtypeStruct((parts, own, tile), f32),
            jax.ShapeDtypeStruct((parts, own, tile), bf16),
            jax.ShapeDtypeStruct((far_count, tile), bf16),
        ],
        scratch_shapes=[
            pltpu.VMEM((near_count, feat), bf16),
            pltpu.VMEM((near_count, tile), bf16),
            pltpu.VMEM((far_count, 2 * feat), bf16),
            pltpu.VMEM((parts, XH, own, tile), f32),
            pltpu.VMEM((feat, tile), bf16),
            pltpu.VMEM((tile, feat), bf16),
            pltpu.SemaphoreType.DMA((2,)),
            pltpu.SemaphoreType.DMA((2,)),
        ],
        compiler_params=params(20),
        name="first_grads",
    )(*pieces, pinned(pre_own), pinned(pre_near), pinned(w_in), pinned(w_out))


def second_grads_body(
    own_ref, right_ref, left_ref, far_a, far_b, act_own, act_near, act_far,
    keep_ref, send_ref, grads, act, sem
):
    feat = grads.shape[1]
    tile = keep_ref.shape[0]
    xh = lax.axis_index("xh")
    terms = stacked_copies((act_own, act_near), act, sem)
    for load in terms:
        load.start()
    join((own_ref, right_ref, left_ref, far_a, far_b), feat, 2 * feat, grads)
    act[act.shape[0] - act_far.shape[0] :, :] = act_far[...]
    for load in terms:
        load.wait()

    def rows_of(part):
        low = pl.multiple_of(part * tile, tile)
        return contract(act[:, pl.ds(low, tile)], grads[...], 0, 0)

    send_ref[...] = rows_of(1 - xh).astype(bf16)
    keep_ref[...] = rows_of(xh)


def second_grads(pieces, acts):
    feat = pieces[0].shape[1] // 2
    count = sum(p.shape[0] for p in pieces)
    width = acts[0].shape[1]
    tile = width // XH
    return pl.pallas_call(
        second_grads_body,
        in_specs=[IN_VMEM] * 5 + [IN_PLACE] * 2 + [IN_VMEM],
        out_specs=[IN_VMEM] * 2,
        out_shape=[
            jax.ShapeDtypeStruct((tile, feat), f32),
            jax.ShapeDtypeStruct((tile, feat), bf16),
        ],
        scratch_shapes=[
            pltpu.VMEM((count, feat), bf16),
            pltpu.VMEM((count, width), bf16),
            pltpu.SemaphoreType.DMA((2,)),
        ],
        compiler_params=params(12),
        name="second_grads",
    )(*pieces, pinned(acts[0]), pinned(acts[1]), acts[2])


def widen_body(in_ref, out_ref):
    parts, _, tile = in_ref.shape
    for i in range(parts):
        out_ref[0, :, i * tile : (i + 1) * tile] = in_ref[i].astype(f32)


def widen(spread):
    parts, own, tile = spread.shape
    return pl.pallas_call(
        widen_body,
        in_specs=[IN_VMEM],
        out_specs=IN_VMEM,
        out_shape=jax.ShapeDtypeStruct((1, own, parts * tile), f32),
        compiler_params=params(4),
        name="widen",
    )(spread)


def token_logits_body(
    back_ref, x_hbm, g_hbm, disp_hbm, comb_hbm, gl_ref, slots_ref, router_ref,
    mix, disp_ref, comb_ref, x_ref, g_ref, x_sem, g_sem, weight_sem
):
    experts, images, double = back_ref.shape
    feat = double // 2
    width = GROUP * PATCHES
    rows = GROUP * experts
    total = experts * images
    x_copies = block_copies(x_hbm, x_ref, x_sem)
    g_copies = block_copies(g_hbm, g_ref, g_sem)
    for x_copy, g_copy in zip(x_copies, g_copies):
        g_copy.start()
        x_copy.start()
    weight_copies = [
        pltpu.make_async_copy(disp_hbm, disp_ref, weight_sem.at[0]),
        pltpu.make_async_copy(comb_hbm, comb_ref, weight_sem.at[1]),
    ]
    for copy in weight_copies:
        copy.start()
    mix[...] = jnp.dot(
        swap_matrix(total, images),
        back_ref[...].reshape(total, double),
        preferred_element_type=f32,
    ).astype(bf16)
    image = lane_images(width)

    def picked(both):
        out = both[:experts]
        for i in range(1, GROUP):
            out = jnp.where(image == i, both[i * experts : (i + 1) * experts], out)
        return out

    for copy in weight_copies:
        copy.wait()
    router_sum = None
    for first in range(0, images // GROUP, 2):
        pair = (first, first + 1)
        grad_comb, grad_disp, grad_logits = {}, {}, {}
        for b in pair:
            g_copies[b].wait()
            x_copies[b].wait()
        for b in pair:
            block = mix[b * rows : (b + 1) * rows, :]
            slots_ref[b] = block[:, feat:]
            g = g_ref[b * width : (b + 1) * width, :]
            grad_comb[b] = picked(contract(block[:, :feat], g, 1, 1))
            x = x_ref[b * width : (b + 1) * width, :]
            grad_disp[b] = picked(contract(block[:, feat:], x, 1, 1))
        for b in pair:
            both = comb_ref[b] * grad_comb[b]
            comb_part = both - comb_ref[b] * jnp.sum(both, axis=0, keepdims=True)
            both = disp_ref[b] * grad_disp[b]
            disp_part = both - disp_ref[b] * per_image(both, image, jnp.sum, 0.0)
            grad_logits[b] = (comb_part + disp_part).astype(bf16)
            gl_ref[b] = grad_logits[b]
        for b in pair:
            part = jnp.dot(
                grad_logits[b], x_ref[b * width : (b + 1) * width, :], preferred_element_type=f32
            )
            router_sum = part if router_sum is None else router_sum + part
    router_ref[...] = router_sum


def token_logits(back, tokens, g_outputs, dispatch, combine):
    experts, images, double = back.shape
    rows, feat = tokens.shape
    steps, _, width = dispatch.shape
    return pl.pallas_call(
        token_logits_body,
        in_specs=[IN_VMEM] + [IN_PLACE] * 4,
        out_specs=[IN_VMEM] * 3,
        out_shape=[
            jax.ShapeDtypeStruct((steps, experts, width), bf16),
            jax.ShapeDtypeStruct((steps, GROUP * experts, feat), bf16),
            jax.ShapeDtypeStruct((experts, feat), f32),
        ],
        scratch_shapes=[
            pltpu.VMEM((experts * images, double), bf16),
            pltpu.VMEM(dispatch.shape, f32),
            pltpu.VMEM(combine.shape, f32),
            pltpu.VMEM((rows, feat), bf16),
            pltpu.VMEM((rows, feat), bf16),
            pltpu.SemaphoreType.DMA((steps,)),
            pltpu.SemaphoreType.DMA((steps,)),
            pltpu.SemaphoreType.DMA((2,)),
        ],
        compiler_params=params(20),
        name="token_logits",
    )(back, *[pinned(v) for v in (tokens, g_outputs, dispatch, combine)])


def token_grads_body(gl_ref, slots_ref, disp_ref, rt_ref, out_ref):
    image = lane_images(gl_ref.shape[2])
    left = jnp.concatenate([per_slot_rows(disp_ref[0], image), gl_ref[0]], axis=0)
    right = jnp.concatenate([slots_ref[0], rt_ref[...]], axis=0)
    out_ref[...] = contract(left, right, 0, 0).astype(bf16)


def token_grads(grad_logits, slots, dispatch, rt):
    steps, experts, width = grad_logits.shape
    feat = slots.shape[2]
    return pl.pallas_call(
        token_grads_body,
        grid=(steps,),
        in_specs=[
            pl.BlockSpec((1, experts, width), lambda i: (i, 0, 0)),
            pl.BlockSpec((1, GROUP * experts, feat), lambda i: (i, 0, 0)),
            pl.BlockSpec((1, experts, width), lambda i: (i, 0, 0)),
            pl.BlockSpec((experts, feat), lambda i: (0, 0)),
        ],
        out_specs=pl.BlockSpec((width, feat), lambda i: (i, 0)),
        out_shape=jax.ShapeDtypeStruct((steps * width, feat), bf16),
        compiler_params=params(12),
        name="token_grads",
    )(grad_logits, slots, dispatch, rt)


def shift(value, axis, by, count):
    return lax.ppermute(value, axis, [(i, (i + by) % count) for i in range(count)])


def axis_sum(value, axis, count):
    return sum([shift(value, axis, by, count) for by in range(1, count)], value)


def solution(mesh):
    dp, experts = mesh.shape["dp"], mesh.shape["expert"]
    ny, nz = dp // XH, experts // 4
    fine = Mesh(
        mesh.devices.reshape(ny, XH, nz, 2, 2), ("y", "xh", "z", "xl", "core")
    )
    dp_axes = ("y", "xh")
    ex_axes = ("z", "xl", "core")

    def over_experts(value):
        return lax.all_to_all(value, ex_axes, split_axis=0, concat_axis=0, tiled=True)

    def on_device(tokens, router, w_in, w_out, g_outputs):
        rt = router.T
        slots, dispatch, combine = token_forward(tokens, rt, g_outputs)
        rows = over_experts(slots).reshape(-1, slots.shape[2])
        mid = rows.shape[0] // 2
        right = shift(rows, "y", 1, ny)
        left = shift(rows, "y", ny - 1, ny)
        results, act_own, pre_own = expert_rows(rows, w_in, w_out, ny)
        back = over_experts(results.reshape(slots.shape))
        far_a = shift(right[:mid], "y", 1, ny)
        far_b = shift(left[mid:], "y", ny - 1, ny)
        act_near, pre_near = near_terms(right, left, w_in, w_out, ny)
        back, act_near, pre_near = lax.optimization_barrier((back, act_near, pre_near))
        grad_logits, slot_grads, router_term = token_logits(
            back, tokens, g_outputs, dispatch, combine
        )
        pieces = (rows, right, left, far_a, far_b)
        keep_in, send_in, act_far = first_grads(pieces, pre_own, pre_near, w_in, w_out, ny)
        keep_out, send_out = second_grads(pieces, (act_own, act_near, act_far))
        came_in = shift(send_in, "xh", 1, XH)
        came_out = shift(send_out, "xh", 1, XH)
        total = axis_sum(router_term, ("xh", "xl"), 2 * XH)
        total, keep_out = lax.optimization_barrier((total, keep_out))
        total = axis_sum(axis_sum(total, "core", 2), "y", ny)
        total, came_in = lax.optimization_barrier((total, came_in))
        part_in = (keep_in + came_in.astype(f32)).astype(bf16)
        spread = lax.all_to_all(part_in, "y", split_axis=0, concat_axis=0, tiled=True)
        grad_router = axis_sum(total, "z", nz).T
        grad_second = keep_out + came_out.astype(f32)
        grad_first = widen(spread)
        grad_tok = token_grads(grad_logits, slot_grads, dispatch, rt)
        return grad_tok, grad_router, grad_first, grad_second[None]

    return jax.shard_map(
        on_device,
        mesh=fine,
        in_specs=(
            P(dp_axes + ex_axes, None),
            P(),
            P(ex_axes, None, None),
            P(ex_axes, None, None),
            P(dp_axes + ex_axes, None),
        ),
        out_specs=(
            P(dp_axes + ex_axes, None),
            P(),
            P(ex_axes, dp_axes, None),
            P(ex_axes, dp_axes, None),
        ),
        check_vma=False,
    )
```

```python
import functools

import jax
import jax.numpy as jnp
from jax import lax
from jax.experimental import pallas as pl
from jax.experimental.pallas import tpu as pltpu
from jax.sharding import Mesh, PartitionSpec as P

PATCHES = 196
GROUP = 4
XH = 2
MIB = 1024 * 1024
GELU_C = 0.7978845608028654
GELU_A = 0.044715

f32 = jnp.float32
bf16 = jnp.bfloat16


def contract(left, right, left_dim, right_dim):
    return lax.dot_general(
        left, right, (((left_dim,), (right_dim,)), ((), ())), preferred_element_type=f32
    )


def params(mib):
    return pltpu.CompilerParams(vmem_limit_bytes=mib * MIB)


def pinned(value):
    return pltpu.with_memory_space_constraint(value, pltpu.HBM)


IN_VMEM = pl.BlockSpec(memory_space=pltpu.VMEM)
IN_PLACE = pl.BlockSpec(memory_space=pltpu.HBM)


def gelu_parts(x):
    x2 = x * x
    th = jnp.tanh(GELU_C * x * (1.0 + GELU_A * x2))
    cdf = 0.5 + 0.5 * th
    slope = cdf + (0.5 * GELU_C) * x * (1.0 - th * th) * (1.0 + (3.0 * GELU_A) * x2)
    return x * cdf, slope


def lane_images(width):
    lane = lax.broadcasted_iota(jnp.int32, (1, width), 1)
    image = jnp.zeros_like(lane)
    for i in range(1, width // PATCHES):
        image = image + (lane >= i * PATCHES).astype(jnp.int32)
    return image


def per_image(values, image, reduce, start):
    width = values.shape[1]
    out = jnp.zeros_like(values)
    for i in range(GROUP):
        low = i * PATCHES // 128 * 128
        high = min(-(-(i + 1) * PATCHES // 128) * 128, width)
        part = jnp.where(image[:, low:high] == i, values[:, low:high], start)
        own = reduce(part, axis=1, keepdims=True)
        out = jnp.where(image == i, own, out)
    return out


def inverse_sum(values, axis, keepdims):
    return 1.0 / jnp.sum(values, axis=axis, keepdims=keepdims)


def per_slot_rows(weights, image):
    return jnp.concatenate(
        [jnp.where(image == i, weights, 0.0) for i in range(GROUP)], axis=0
    ).astype(bf16)


def swap_matrix(total, inner):
    outer = total // inner
    out_row = lax.broadcasted_iota(jnp.int32, (total, total), 0)
    in_row = lax.broadcasted_iota(jnp.int32, (total, total), 1)
    wanted = (out_row % outer) * inner + out_row // outer
    return (in_row == wanted).astype(f32).astype(bf16)


def block_copies(src, dst, sem):
    width = GROUP * PATCHES
    return [
        pltpu.make_async_copy(
            src.at[pl.ds(b * width, width)], dst.at[pl.ds(b * width, width)], sem.at[b]
        )
        for b in range(src.shape[0] // width)
    ]


def token_forward_body(
    rt_hbm, x_hbm, g_hbm, slots_ref, disp_hbm, comb_hbm,
    rt_ref, disp_ref, comb_ref, x_ref, g_ref, acc, x_sem, g_sem, rt_sem, disp_sem, comb_sem
):
    experts, images, double = slots_ref.shape
    feat = double // 2
    width = GROUP * PATCHES
    steps = images // GROUP
    rows = GROUP * experts
    total = experts * images

    x_copies = block_copies(x_hbm, x_ref, x_sem)
    g_copies = block_copies(g_hbm, g_ref, g_sem)
    rt_copy = pltpu.make_async_copy(rt_hbm, rt_ref, rt_sem)
    for copy in [rt_copy] + x_copies + g_copies:
        copy.start()
    weight_copies = [
        pltpu.make_async_copy(disp_ref, disp_hbm, disp_sem),
        pltpu.make_async_copy(comb_ref, comb_hbm, comb_sem),
    ]
    image = lane_images(width)
    rt_copy.wait()
    rt = rt_ref[...]
    spread = {}
    for first in range(0, steps, 2):
        pair = (first, first + 1)
        logits, own = {}, {}
        for b in pair:
            x_copies[b].wait()
        for b in pair:
            logits[b] = contract(rt, x_ref[b * width : (b + 1) * width, :], 1, 1)
        for b in pair:
            top = per_image(logits[b], image, jnp.max, -jnp.inf)
            raised = jnp.exp(logits[b] - top)
            dispatch = raised * per_image(raised, image, inverse_sum, 0.0)
            raised_e = jnp.exp(logits[b] - jnp.max(logits[b], axis=0, keepdims=True))
            combine = raised_e * inverse_sum(raised_e, axis=0, keepdims=True)
            disp_ref[b] = dispatch
            comb_ref[b] = combine
            spread[b] = per_slot_rows(combine, image)
            own[b] = per_slot_rows(dispatch, image)
        for b in pair:
            acc[b * rows : (b + 1) * rows, :feat] = jnp.dot(
                own[b], x_ref[b * width : (b + 1) * width, :], preferred_element_type=f32
            ).astype(bf16)
    for copy in weight_copies:
        copy.start()
    for b in range(steps):
        g_copies[b].wait()
    for b in range(steps):
        acc[b * rows : (b + 1) * rows, feat:] = jnp.dot(
            spread[b], g_ref[b * width : (b + 1) * width, :], preferred_element_type=f32
        ).astype(bf16)
    slots_ref[...] = (
        jnp.dot(swap_matrix(total, experts), acc[...], preferred_element_type=f32)
        .astype(bf16)
        .reshape(experts, images, double)
    )
    for copy in weight_copies:
        copy.wait()


def token_forward(tokens, rt, g_outputs):
    rows, feat = tokens.shape
    experts = rt.shape[0]
    images = rows // PATCHES
    width = GROUP * PATCHES
    steps = rows // width
    return pl.pallas_call(
        token_forward_body,
        in_specs=[IN_PLACE] * 3,
        out_specs=[IN_VMEM, IN_PLACE, IN_PLACE],
        out_shape=[
            jax.ShapeDtypeStruct((experts, images, 2 * feat), bf16),
            pltpu.HBM((steps, experts, width), f32),
            pltpu.HBM((steps, experts, width), f32),
        ],
        scratch_shapes=[
            pltpu.VMEM((experts, feat), bf16),
            pltpu.VMEM((steps, experts, width), f32),
            pltpu.VMEM((steps, experts, width), f32),
            pltpu.VMEM((rows, feat), bf16),
            pltpu.VMEM((rows, feat), bf16),
            pltpu.VMEM((experts * images, 2 * feat), bf16),
            pltpu.SemaphoreType.DMA((steps,)),
            pltpu.SemaphoreType.DMA((steps,)),
            pltpu.SemaphoreType.DMA(()),
            pltpu.SemaphoreType.DMA(()),
            pltpu.SemaphoreType.DMA(()),
        ],
        compiler_params=params(20),
        name="token_forward",
    )(pinned(rt), pinned(tokens), pinned(g_outputs))


def hidden_terms(rows, grads, w1, w2):
    act, slope = gelu_parts(jnp.dot(rows, w1, preferred_element_type=f32))
    return act.astype(bf16), (contract(grads, w2, 1, 1) * slope).astype(bf16)


def expert_body(
    rows_ref, w1_ref, w2_ref, out_hbm, act_hbm, pre_hbm, out_ref, act_ref, pre_ref, sem
):
    feat = w1_ref.shape[1]
    hidden = w1_ref.shape[2]
    tile = act_ref.shape[1]
    part_at = lax.axis_index("y")
    rows = rows_ref[:, :feat]
    grads = rows_ref[:, feat:]
    made, back = None, None
    stores = [
        pltpu.make_async_copy(src, dst, sem.at[k])
        for k, (src, dst) in enumerate(
            ((act_ref, act_hbm), (pre_ref, pre_hbm), (out_ref, out_hbm))
        )
    ]
    for i in range(hidden // tile):
        w1 = w1_ref[0, :, i * tile : (i + 1) * tile]
        w2 = w2_ref[0, i * tile : (i + 1) * tile, :]
        act, grad_pre = hidden_terms(rows, grads, w1, w2)

        @pl.when(part_at == i)
        def _():
            act_ref[...] = act
            pre_ref[...] = grad_pre

        if i == hidden // tile - 1:
            stores[0].start()
            stores[1].start()
        part = jnp.dot(act, w2, preferred_element_type=f32)
        made = part if made is None else made + part
        part = contract(grad_pre, w1, 1, 1)
        back = part if back is None else back + part
    out_ref[:, :feat] = made.astype(bf16)
    out_ref[:, feat:] = back.astype(bf16)
    stores[2].start()
    for store in stores:
        store.wait()


def expert_rows(rows, w_in, w_out, parts):
    tile = w_in.shape[2] // parts
    shapes = [rows.shape, (rows.shape[0], tile), (rows.shape[0], tile)]
    return pl.pallas_call(
        expert_body,
        in_specs=[IN_VMEM] * 3,
        out_specs=[IN_PLACE] * 3,
        out_shape=[pltpu.HBM(shape, bf16) for shape in shapes],
        scratch_shapes=[pltpu.VMEM(shape, bf16) for shape in shapes]
        + [pltpu.SemaphoreType.DMA((3,))],
        compiler_params=params(12),
        name="expert_rows",
    )(rows, w_in, w_out)


def slice_copies(w1_hbm, w2_hbm, w1, w2, sem):
    tile = w1.shape[1]
    low = pl.multiple_of(lax.axis_index("y") * tile, tile)
    return (
        pltpu.make_async_copy(w1_hbm.at[0, :, pl.ds(low, tile)], w1, sem.at[0]),
        pltpu.make_async_copy(w2_hbm.at[0, pl.ds(low, tile), :], w2, sem.at[1]),
    )


def stacked_copies(sources, out, sem):
    copies, at = [], 0
    for k, source in enumerate(sources):
        rows = source.shape[0]
        copies.append(pltpu.make_async_copy(source, out.at[pl.ds(at, rows)], sem.at[k]))
        at += rows
    return copies


def join(pieces, low, high, out):
    at = 0
    for piece in pieces:
        out[at : at + piece.shape[0], :] = piece[:, low:high]
        at += piece.shape[0]


def near_terms_body(
    right_ref, left_ref, w1_hbm, w2_hbm, act_hbm, pre_hbm, act, pre, both, w1, w2, sem, out_sem
):
    feat = w1.shape[0]
    loads = slice_copies(w1_hbm, w2_hbm, w1, w2, sem)
    for load in loads:
        load.start()
    join((right_ref, left_ref), 0, 2 * feat, both)
    for load in loads:
        load.wait()
    act[...], pre[...] = hidden_terms(both[:, :feat], both[:, feat:], w1[...], w2[...])
    stores = (
        pltpu.make_async_copy(act, act_hbm, out_sem.at[0]),
        pltpu.make_async_copy(pre, pre_hbm, out_sem.at[1]),
    )
    for store in stores:
        store.start()
    for store in stores:
        store.wait()


def near_terms(right, left, w_in, w_out, parts):
    feat, hidden = w_in.shape[1:]
    tile = hidden // parts
    count = right.shape[0] + left.shape[0]
    return pl.pallas_call(
        near_terms_body,
        in_specs=[IN_VMEM] * 2 + [IN_PLACE] * 2,
        out_specs=[IN_PLACE] * 2,
        out_shape=[pltpu.HBM((count, tile), bf16)] * 2,
        scratch_shapes=[
            pltpu.VMEM((count, tile), bf16),
            pltpu.VMEM((count, tile), bf16),
            pltpu.VMEM((count, 2 * feat), bf16),
            pltpu.VMEM((feat, tile), bf16),
            pltpu.VMEM((tile, feat), bf16),
            pltpu.SemaphoreType.DMA((2,)),
            pltpu.SemaphoreType.DMA((2,)),
        ],
        compiler_params=params(16),
        name="near_terms",
    )(right, left, pinned(w_in), pinned(w_out))


def first_grads_body(
    own_ref, right_ref, left_ref, far_a, far_b, pre_own, pre_near, w1_hbm, w2_hbm,
    keep_ref, send_ref, act_far, rows, pre, far, acc, w1, w2, sem, pre_sem
):
    feat = w1.shape[0]
    xh = lax.axis_index("xh")
    loads = slice_copies(w1_hbm, w2_hbm, w1, w2, sem)
    terms = stacked_copies((pre_own, pre_near), pre, pre_sem)
    for load in terms + list(loads):
        load.start()
    join((own_ref, right_ref, left_ref), 0, feat, rows)
    join((far_a, far_b), 0, 2 * feat, far)
    for load in terms:
        load.wait()
    total = contract(rows[...], pre[...], 0, 0)
    for load in loads:
        load.wait()
    act, pre_far = hidden_terms(far[:, :feat], far[:, feat:], w1[...], w2[...])
    act_far[...] = act
    acc[...] = (total + contract(far[:, :feat], pre_far, 0, 0)).reshape(acc.shape)
    send_ref[...] = acc[:, pl.ds(1 - xh, 1)].reshape(send_ref.shape).astype(bf16)
    keep_ref[...] = acc[:, pl.ds(xh, 1)].reshape(keep_ref.shape)


def first_grads(pieces, pre_own, pre_near, w_in, w_out, parts):
    feat, hidden = w_in.shape[1:]
    tile = hidden // parts
    own = feat // (parts * XH)
    near_count = sum(p.shape[0] for p in pieces[:3])
    far_count = sum(p.shape[0] for p in pieces[3:])
    return pl.pallas_call(
        first_grads_body,
        in_specs=[IN_VMEM] * 5 + [IN_PLACE] * 4,
        out_specs=[IN_VMEM] * 3,
        out_shape=[
            jax.ShapeDtypeStruct((parts, own, tile), f32),
            jax.ShapeDtypeStruct((parts, own, tile), bf16),
            jax.ShapeDtypeStruct((far_count, tile), bf16),
        ],
        scratch_shapes=[
            pltpu.VMEM((near_count, feat), bf16),
            pltpu.VMEM((near_count, tile), bf16),
            pltpu.VMEM((far_count, 2 * feat), bf16),
            pltpu.VMEM((parts, XH, own, tile), f32),
            pltpu.VMEM((feat, tile), bf16),
            pltpu.VMEM((tile, feat), bf16),
            pltpu.SemaphoreType.DMA((2,)),
            pltpu.SemaphoreType.DMA((2,)),
        ],
        compiler_params=params(20),
        name="first_grads",
    )(*pieces, pinned(pre_own), pinned(pre_near), pinned(w_in), pinned(w_out))


def second_grads_body(
    own_ref, right_ref, left_ref, far_a, far_b, act_own, act_near, act_far,
    keep_ref, send_ref, grads, act, sem
):
    feat = grads.shape[1]
    tile = keep_ref.shape[0]
    xh = lax.axis_index("xh")
    terms = stacked_copies((act_own, act_near), act, sem)
    for load in terms:
        load.start()
    join((own_ref, right_ref, left_ref, far_a, far_b), feat, 2 * feat, grads)
    act[act.shape[0] - act_far.shape[0] :, :] = act_far[...]
    for load in terms:
        load.wait()

    def rows_of(part):
        low = pl.multiple_of(part * tile, tile)
        return contract(act[:, pl.ds(low, tile)], grads[...], 0, 0)

    send_ref[...] = rows_of(1 - xh).astype(bf16)
    keep_ref[...] = rows_of(xh)


def second_grads(pieces, acts):
    feat = pieces[0].shape[1] // 2
    count = sum(p.shape[0] for p in pieces)
    width = acts[0].shape[1]
    tile = width // XH
    return pl.pallas_call(
        second_grads_body,
        in_specs=[IN_VMEM] * 5 + [IN_PLACE] * 2 + [IN_VMEM],
        out_specs=[IN_VMEM] * 2,
        out_shape=[
            jax.ShapeDtypeStruct((tile, feat), f32),
            jax.ShapeDtypeStruct((tile, feat), bf16),
        ],
        scratch_shapes=[
            pltpu.VMEM((count, feat), bf16),
            pltpu.VMEM((count, width), bf16),
            pltpu.SemaphoreType.DMA((2,)),
        ],
        compiler_params=params(12),
        name="second_grads",
    )(*pieces, pinned(acts[0]), pinned(acts[1]), acts[2])


def widen_body(in_ref, out_ref):
    parts, _, tile = in_ref.shape
    for i in range(parts):
        out_ref[0, :, i * tile : (i + 1) * tile] = in_ref[i].astype(f32)


def widen(spread):
    parts, own, tile = spread.shape
    return pl.pallas_call(
        widen_body,
        in_specs=[IN_VMEM],
        out_specs=IN_VMEM,
        out_shape=jax.ShapeDtypeStruct((1, own, parts * tile), f32),
        compiler_params=params(4),
        name="widen",
    )(spread)


def token_logits_body(
    back_ref, x_hbm, g_hbm, disp_hbm, comb_hbm, gl_ref, slots_ref, router_ref,
    mix, disp_ref, comb_ref, x_ref, g_ref, x_sem, g_sem, weight_sem
):
    experts, images, double = back_ref.shape
    feat = double // 2
    width = GROUP * PATCHES
    rows = GROUP * experts
    total = experts * images
    x_copies = block_copies(x_hbm, x_ref, x_sem)
    g_copies = block_copies(g_hbm, g_ref, g_sem)
    for x_copy, g_copy in zip(x_copies, g_copies):
        g_copy.start()
        x_copy.start()
    weight_copies = [
        pltpu.make_async_copy(disp_hbm, disp_ref, weight_sem.at[0]),
        pltpu.make_async_copy(comb_hbm, comb_ref, weight_sem.at[1]),
    ]
    for copy in weight_copies:
        copy.start()
    mix[...] = jnp.dot(
        swap_matrix(total, images),
        back_ref[...].reshape(total, double),
        preferred_element_type=f32,
    ).astype(bf16)
    image = lane_images(width)

    def picked(both):
        out = both[:experts]
        for i in range(1, GROUP):
            out = jnp.where(image == i, both[i * experts : (i + 1) * experts], out)
        return out

    for copy in weight_copies:
        copy.wait()
    router_sum = None
    for first in range(0, images // GROUP, 2):
        pair = (first, first + 1)
        grad_comb, grad_disp, grad_logits = {}, {}, {}
        for b in pair:
            g_copies[b].wait()
            x_copies[b].wait()
        for b in pair:
            block = mix[b * rows : (b + 1) * rows, :]
            slots_ref[b] = block[:, feat:]
            g = g_ref[b * width : (b + 1) * width, :]
            grad_comb[b] = picked(contract(block[:, :feat], g, 1, 1))
            x = x_ref[b * width : (b + 1) * width, :]
            grad_disp[b] = picked(contract(block[:, feat:], x, 1, 1))
        for b in pair:
            both = comb_ref[b] * grad_comb[b]
            comb_part = both - comb_ref[b] * jnp.sum(both, axis=0, keepdims=True)
            both = disp_ref[b] * grad_disp[b]
            disp_part = both - disp_ref[b] * per_image(both, image, jnp.sum, 0.0)
            grad_logits[b] = (comb_part + disp_part).astype(bf16)
            gl_ref[b] = grad_logits[b]
        for b in pair:
            part = jnp.dot(
                grad_logits[b], x_ref[b * width : (b + 1) * width, :], preferred_element_type=f32
            )
            router_sum = part if router_sum is None else router_sum + part
    router_ref[...] = router_sum


def token_logits(back, tokens, g_outputs, dispatch, combine):
    experts, images, double = back.shape
    rows, feat = tokens.shape
    steps, _, width = dispatch.shape
    return pl.pallas_call(
        token_logits_body,
        in_specs=[IN_VMEM] + [IN_PLACE] * 4,
        out_specs=[IN_VMEM] * 3,
        out_shape=[
            jax.ShapeDtypeStruct((steps, experts, width), bf16),
            jax.ShapeDtypeStruct((steps, GROUP * experts, feat), bf16),
            jax.ShapeDtypeStruct((experts, feat), f32),
        ],
        scratch_shapes=[
            pltpu.VMEM((experts * images, double), bf16),
            pltpu.VMEM(dispatch.shape, f32),
            pltpu.VMEM(combine.shape, f32),
            pltpu.VMEM((rows, feat), bf16),
            pltpu.VMEM((rows, feat), bf16),
            pltpu.SemaphoreType.DMA((steps,)),
            pltpu.SemaphoreType.DMA((steps,)),
            pltpu.SemaphoreType.DMA((2,)),
        ],
        compiler_params=params(20),
        name="token_logits",
    )(back, *[pinned(v) for v in (tokens, g_outputs, dispatch, combine)])


def token_grads_body(gl_ref, slots_ref, disp_ref, rt_ref, out_ref):
    image = lane_images(gl_ref.shape[2])
    left = jnp.concatenate([per_slot_rows(disp_ref[0], image), gl_ref[0]], axis=0)
    right = jnp.concatenate([slots_ref[0], rt_ref[...]], axis=0)
    out_ref[...] = contract(left, right, 0, 0).astype(bf16)


def token_grads(grad_logits, slots, dispatch, rt):
    steps, experts, width = grad_logits.shape
    feat = slots.shape[2]
    return pl.pallas_call(
        token_grads_body,
        grid=(steps,),
        in_specs=[
            pl.BlockSpec((1, experts, width), lambda i: (i, 0, 0)),
            pl.BlockSpec((1, GROUP * experts, feat), lambda i: (i, 0, 0)),
            pl.BlockSpec((1, experts, width), lambda i: (i, 0, 0)),
            pl.BlockSpec((experts, feat), lambda i: (0, 0)),
        ],
        out_specs=pl.BlockSpec((width, feat), lambda i: (i, 0)),
        out_shape=jax.ShapeDtypeStruct((steps * width, feat), bf16),
        compiler_params=params(12),
        name="token_grads",
    )(grad_logits, slots, dispatch, rt)


def shift(value, axis, by, count):
    return lax.ppermute(value, axis, [(i, (i + by) % count) for i in range(count)])


def axis_sum(value, axis, count):
    return sum([shift(value, axis, by, count) for by in range(1, count)], value)


def solution(mesh):
    dp, experts = mesh.shape["dp"], mesh.shape["expert"]
    ny, nz = dp // XH, experts // 4
    fine = Mesh(
        mesh.devices.reshape(ny, XH, nz, 2, 2), ("y", "xh", "z", "xl", "core")
    )
    dp_axes = ("y", "xh")
    ex_axes = ("z", "xl", "core")

    def over_experts(value):
        return lax.all_to_all(value, ex_axes, split_axis=0, concat_axis=0, tiled=True)

    def on_device(tokens, router, w_in, w_out, g_outputs):
        rt = router.T
        slots, dispatch, combine = token_forward(tokens, rt, g_outputs)
        rows = over_experts(slots).reshape(-1, slots.shape[2])
        mid = rows.shape[0] // 2
        right = shift(rows, "y", 1, ny)
        left = shift(rows, "y", ny - 1, ny)
        results, act_own, pre_own = expert_rows(rows, w_in, w_out, ny)
        back = over_experts(results.reshape(slots.shape))
        far_a = shift(right[:mid], "y", 1, ny)
        far_b = shift(left[mid:], "y", ny - 1, ny)
        act_near, pre_near = near_terms(right, left, w_in, w_out, ny)
        back, act_near, pre_near = lax.optimization_barrier((back, act_near, pre_near))
        grad_logits, slot_grads, router_term = token_logits(
            back, tokens, g_outputs, dispatch, combine
        )
        far_a, far_b, router_term = lax.optimization_barrier((far_a, far_b, router_term))
        pieces = (rows, right, left, far_a, far_b)
        keep_in, send_in, act_far = first_grads(pieces, pre_own, pre_near, w_in, w_out, ny)
        keep_out, send_out = second_grads(pieces, (act_own, act_near, act_far))
        total = axis_sum(router_term, "xh", XH)
        total, send_in = lax.optimization_barrier((total, send_in))
        came_in = shift(send_in, "xh", 1, XH)
        total = axis_sum(axis_sum(total, "core", 2), "y", ny)
        total, keep_out, send_out = lax.optimization_barrier((total, keep_out, send_out))
        total = axis_sum(total, "z", nz)
        came_in, send_out = lax.optimization_barrier((came_in, send_out))
        came_out = shift(send_out, "xh", 1, XH)
        part_in = (keep_in + came_in.astype(f32)).astype(bf16)
        total, part_in, grad_logits = lax.optimization_barrier((total, part_in, grad_logits))
        spread = lax.all_to_all(part_in, "y", split_axis=0, concat_axis=0, tiled=True)
        grad_router = axis_sum(total, "xl", 2).T
        grad_second = keep_out + came_out.astype(f32)
        grad_first = widen(spread)
        grad_tok = token_grads(grad_logits, slot_grads, dispatch, rt)
        return grad_tok, grad_router, grad_first, grad_second[None]

    return jax.shard_map(
        on_device,
        mesh=fine,
        in_specs=(
            P(dp_axes + ex_axes, None),
            P(),
            P(ex_axes, None, None),
            P(ex_axes, None, None),
            P(dp_axes + ex_axes, None),
        ),
        out_specs=(
            P(dp_axes + ex_axes, None),
            P(),
            P(ex_axes, dp_axes, None),
            P(ex_axes, dp_axes, None),
        ),
        check_vma=False,
    )
```

```python
import functools

import jax
import jax.numpy as jnp
from jax import lax
from jax.experimental import pallas as pl
from jax.experimental.pallas import tpu as pltpu
from jax.sharding import Mesh, PartitionSpec as P

PATCHES = 196
GROUP = 4
XH = 2
MIB = 1024 * 1024
GELU_C = 0.7978845608028654
GELU_A = 0.044715

f32 = jnp.float32
bf16 = jnp.bfloat16


def contract(left, right, left_dim, right_dim):
    return lax.dot_general(
        left, right, (((left_dim,), (right_dim,)), ((), ())), preferred_element_type=f32
    )


def params(mib):
    return pltpu.CompilerParams(vmem_limit_bytes=mib * MIB)


def pinned(value):
    return pltpu.with_memory_space_constraint(value, pltpu.HBM)


IN_VMEM = pl.BlockSpec(memory_space=pltpu.VMEM)
IN_PLACE = pl.BlockSpec(memory_space=pltpu.HBM)


def gelu_parts(x):
    x2 = x * x
    th = jnp.tanh(GELU_C * x * (1.0 + GELU_A * x2))
    cdf = 0.5 + 0.5 * th
    slope = cdf + (0.5 * GELU_C) * x * (1.0 - th * th) * (1.0 + (3.0 * GELU_A) * x2)
    return x * cdf, slope


def lane_images(width):
    lane = lax.broadcasted_iota(jnp.int32, (1, width), 1)
    image = jnp.zeros_like(lane)
    for i in range(1, width // PATCHES):
        image = image + (lane >= i * PATCHES).astype(jnp.int32)
    return image


def per_image(values, image, reduce, start):
    width = values.shape[1]
    out = jnp.zeros_like(values)
    for i in range(GROUP):
        low = i * PATCHES // 128 * 128
        high = min(-(-(i + 1) * PATCHES // 128) * 128, width)
        part = jnp.where(image[:, low:high] == i, values[:, low:high], start)
        own = reduce(part, axis=1, keepdims=True)
        out = jnp.where(image == i, own, out)
    return out


def inverse_sum(values, axis, keepdims):
    return 1.0 / jnp.sum(values, axis=axis, keepdims=keepdims)


def per_slot_rows(weights, image):
    return jnp.concatenate(
        [jnp.where(image == i, weights, 0.0) for i in range(GROUP)], axis=0
    ).astype(bf16)


def swap_matrix(total, inner):
    outer = total // inner
    out_row = lax.broadcasted_iota(jnp.int32, (total, total), 0)
    in_row = lax.broadcasted_iota(jnp.int32, (total, total), 1)
    wanted = (out_row % outer) * inner + out_row // outer
    return (in_row == wanted).astype(f32).astype(bf16)


def block_copies(src, dst, sem):
    width = GROUP * PATCHES
    return [
        pltpu.make_async_copy(
            src.at[pl.ds(b * width, width)], dst.at[pl.ds(b * width, width)], sem.at[b]
        )
        for b in range(src.shape[0] // width)
    ]


def token_forward_body(
    rt_hbm, x_hbm, g_hbm, slots_ref, disp_hbm, comb_hbm,
    rt_ref, disp_ref, comb_ref, x_ref, g_ref, acc, x_sem, g_sem, rt_sem, disp_sem, comb_sem
):
    experts, images, double = slots_ref.shape
    feat = double // 2
    width = GROUP * PATCHES
    steps = images // GROUP
    rows = GROUP * experts
    total = experts * images

    x_copies = block_copies(x_hbm, x_ref, x_sem)
    g_copies = block_copies(g_hbm, g_ref, g_sem)
    rt_copy = pltpu.make_async_copy(rt_hbm, rt_ref, rt_sem)
    for copy in [rt_copy] + x_copies:
        copy.start()
    weight_copies = [
        pltpu.make_async_copy(disp_ref, disp_hbm, disp_sem),
        pltpu.make_async_copy(comb_ref, comb_hbm, comb_sem),
    ]
    image = lane_images(width)
    rt_copy.wait()
    rt = rt_ref[...]
    spread = {}
    for first in range(0, steps, 2):
        pair = (first, first + 1)
        logits, own = {}, {}
        for b in pair:
            x_copies[b].wait()
        for b in pair:
            g_copies[b].start()
        for b in pair:
            logits[b] = contract(rt, x_ref[b * width : (b + 1) * width, :], 1, 1)
        for b in pair:
            top = per_image(logits[b], image, jnp.max, -jnp.inf)
            raised = jnp.exp(logits[b] - top)
            dispatch = raised * per_image(raised, image, inverse_sum, 0.0)
            raised_e = jnp.exp(logits[b] - jnp.max(logits[b], axis=0, keepdims=True))
            combine = raised_e * inverse_sum(raised_e, axis=0, keepdims=True)
            disp_ref[b] = dispatch
            comb_ref[b] = combine
            spread[b] = per_slot_rows(combine, image)
            own[b] = per_slot_rows(dispatch, image)
        for b in pair:
            acc[b * rows : (b + 1) * rows, :feat] = jnp.dot(
                own[b], x_ref[b * width : (b + 1) * width, :], preferred_element_type=f32
            ).astype(bf16)
    for copy in weight_copies:
        copy.start()
    for b in range(steps):
        g_copies[b].wait()
    for b in range(steps):
        acc[b * rows : (b + 1) * rows, feat:] = jnp.dot(
            spread[b], g_ref[b * width : (b + 1) * width, :], preferred_element_type=f32
        ).astype(bf16)
    slots_ref[...] = (
        jnp.dot(swap_matrix(total, experts), acc[...], preferred_element_type=f32)
        .astype(bf16)
        .reshape(experts, images, double)
    )
    for copy in weight_copies:
        copy.wait()


def token_forward(tokens, rt, g_outputs):
    rows, feat = tokens.shape
    experts = rt.shape[0]
    images = rows // PATCHES
    width = GROUP * PATCHES
    steps = rows // width
    return pl.pallas_call(
        token_forward_body,
        in_specs=[IN_PLACE] * 3,
        out_specs=[IN_VMEM, IN_PLACE, IN_PLACE],
        out_shape=[
            jax.ShapeDtypeStruct((experts, images, 2 * feat), bf16),
            pltpu.HBM((steps, experts, width), f32),
            pltpu.HBM((steps, experts, width), f32),
        ],
        scratch_shapes=[
            pltpu.VMEM((experts, feat), bf16),
            pltpu.VMEM((steps, experts, width), f32),
            pltpu.VMEM((steps, experts, width), f32),
            pltpu.VMEM((rows, feat), bf16),
            pltpu.VMEM((rows, feat), bf16),
            pltpu.VMEM((experts * images, 2 * feat), bf16),
            pltpu.SemaphoreType.DMA((steps,)),
            pltpu.SemaphoreType.DMA((steps,)),
            pltpu.SemaphoreType.DMA(()),
            pltpu.SemaphoreType.DMA(()),
            pltpu.SemaphoreType.DMA(()),
        ],
        compiler_params=params(20),
        name="token_forward",
    )(pinned(rt), pinned(tokens), pinned(g_outputs))


def hidden_terms(rows, grads, w1, w2):
    act, slope = gelu_parts(jnp.dot(rows, w1, preferred_element_type=f32))
    return act.astype(bf16), (contract(grads, w2, 1, 1) * slope).astype(bf16)


def expert_body(
    rows_ref, w1_ref, w2_ref, out_hbm, act_hbm, pre_hbm, out_ref, act_ref, pre_ref, sem
):
    feat = w1_ref.shape[1]
    hidden = w1_ref.shape[2]
    tile = act_ref.shape[1]
    part_at = lax.axis_index("y")
    rows = rows_ref[:, :feat]
    grads = rows_ref[:, feat:]
    made, back = None, None
    stores = [
        pltpu.make_async_copy(src, dst, sem.at[k])
        for k, (src, dst) in enumerate(
            ((act_ref, act_hbm), (pre_ref, pre_hbm), (out_ref, out_hbm))
        )
    ]
    for i in range(hidden // tile):
        w1 = w1_ref[0, :, i * tile : (i + 1) * tile]
        w2 = w2_ref[0, i * tile : (i + 1) * tile, :]
        act, grad_pre = hidden_terms(rows, grads, w1, w2)

        @pl.when(part_at == i)
        def _():
            act_ref[...] = act
            pre_ref[...] = grad_pre

        if i == hidden // tile - 1:
            stores[0].start()
            stores[1].start()
        part = jnp.dot(act, w2, preferred_element_type=f32)
        made = part if made is None else made + part
        part = contract(grad_pre, w1, 1, 1)
        back = part if back is None else back + part
    out_ref[:, :feat] = made.astype(bf16)
    out_ref[:, feat:] = back.astype(bf16)
    stores[2].start()
    for store in stores:
        store.wait()


def expert_rows(rows, w_in, w_out, parts):
    tile = w_in.shape[2] // parts
    shapes = [rows.shape, (rows.shape[0], tile), (rows.shape[0], tile)]
    return pl.pallas_call(
        expert_body,
        in_specs=[IN_VMEM] * 3,
        out_specs=[IN_PLACE] * 3,
        out_shape=[pltpu.HBM(shape, bf16) for shape in shapes],
        scratch_shapes=[pltpu.VMEM(shape, bf16) for shape in shapes]
        + [pltpu.SemaphoreType.DMA((3,))],
        compiler_params=params(12),
        name="expert_rows",
    )(rows, w_in, w_out)


def slice_copies(w1_hbm, w2_hbm, w1, w2, sem):
    tile = w1.shape[1]
    low = pl.multiple_of(lax.axis_index("y") * tile, tile)
    return (
        pltpu.make_async_copy(w1_hbm.at[0, :, pl.ds(low, tile)], w1, sem.at[0]),
        pltpu.make_async_copy(w2_hbm.at[0, pl.ds(low, tile), :], w2, sem.at[1]),
    )


def stacked_copies(sources, out, sem):
    copies, at = [], 0
    for k, source in enumerate(sources):
        rows = source.shape[0]
        copies.append(pltpu.make_async_copy(source, out.at[pl.ds(at, rows)], sem.at[k]))
        at += rows
    return copies


def join(pieces, low, high, out):
    at = 0
    for piece in pieces:
        out[at : at + piece.shape[0], :] = piece[:, low:high]
        at += piece.shape[0]


def near_terms_body(
    right_ref, left_ref, w1_hbm, w2_hbm, act_hbm, pre_hbm, act, pre, both, w1, w2, sem, out_sem
):
    feat = w1.shape[0]
    loads = slice_copies(w1_hbm, w2_hbm, w1, w2, sem)
    for load in loads:
        load.start()
    join((right_ref, left_ref), 0, 2 * feat, both)
    for load in loads:
        load.wait()
    act[...], pre[...] = hidden_terms(both[:, :feat], both[:, feat:], w1[...], w2[...])
    stores = (
        pltpu.make_async_copy(act, act_hbm, out_sem.at[0]),
        pltpu.make_async_copy(pre, pre_hbm, out_sem.at[1]),
    )
    for store in stores:
        store.start()
    for store in stores:
        store.wait()


def near_terms(right, left, w_in, w_out, parts):
    feat, hidden = w_in.shape[1:]
    tile = hidden // parts
    count = right.shape[0] + left.shape[0]
    return pl.pallas_call(
        near_terms_body,
        in_specs=[IN_VMEM] * 2 + [IN_PLACE] * 2,
        out_specs=[IN_PLACE] * 2,
        out_shape=[pltpu.HBM((count, tile), bf16)] * 2,
        scratch_shapes=[
            pltpu.VMEM((count, tile), bf16),
            pltpu.VMEM((count, tile), bf16),
            pltpu.VMEM((count, 2 * feat), bf16),
            pltpu.VMEM((feat, tile), bf16),
            pltpu.VMEM((tile, feat), bf16),
            pltpu.SemaphoreType.DMA((2,)),
            pltpu.SemaphoreType.DMA((2,)),
        ],
        compiler_params=params(16),
        name="near_terms",
    )(right, left, pinned(w_in), pinned(w_out))


def first_grads_body(
    own_ref, right_ref, left_ref, far_ref, pre_own, pre_near, w1_hbm, w2_hbm,
    terms_hbm, act_hbm, terms_ref, act_far, rows, pre, w1, w2, sem, pre_sem, out_sem
):
    feat = w1.shape[0]
    loads = slice_copies(w1_hbm, w2_hbm, w1, w2, sem)
    terms = stacked_copies((pre_own, pre_near), pre, pre_sem)
    for load in terms + list(loads):
        load.start()
    join((own_ref, right_ref, left_ref), 0, feat, rows)
    for load in terms:
        load.wait()
    total = contract(rows[...], pre[...], 0, 0)
    for load in loads:
        load.wait()
    act, pre_far = hidden_terms(far_ref[:, :feat], far_ref[:, feat:], w1[...], w2[...])
    act_far[...] = act
    stores = [
        pltpu.make_async_copy(act_far, act_hbm, out_sem.at[0]),
        pltpu.make_async_copy(terms_ref, terms_hbm, out_sem.at[1]),
    ]
    stores[0].start()
    total = total + contract(far_ref[:, :feat], pre_far, 0, 0)
    terms_ref[...] = total.astype(bf16).reshape(terms_ref.shape)
    stores[1].start()
    for store in stores:
        store.wait()


def first_grads(pieces, pre_own, pre_near, w_in, w_out, parts):
    feat, hidden = w_in.shape[1:]
    tile = hidden // parts
    own = feat // (parts * XH)
    near_count = sum(p.shape[0] for p in pieces[:3])
    return pl.pallas_call(
        first_grads_body,
        in_specs=[IN_VMEM] * 4 + [IN_PLACE] * 4,
        out_specs=[IN_PLACE] * 2,
        out_shape=[
            pltpu.HBM((parts * XH, own, tile), bf16),
            pltpu.HBM((pieces[3].shape[0], tile), bf16),
        ],
        scratch_shapes=[
            pltpu.VMEM((parts * XH, own, tile), bf16),
            pltpu.VMEM((pieces[3].shape[0], tile), bf16),
            pltpu.VMEM((near_count, feat), bf16),
            pltpu.VMEM((near_count, tile), bf16),
            pltpu.VMEM((feat, tile), bf16),
            pltpu.VMEM((tile, feat), bf16),
            pltpu.SemaphoreType.DMA((2,)),
            pltpu.SemaphoreType.DMA((2,)),
            pltpu.SemaphoreType.DMA((2,)),
        ],
        compiler_params=params(20),
        name="first_grads",
    )(*pieces, pinned(pre_own), pinned(pre_near), pinned(w_in), pinned(w_out))


def second_grads_body(
    own_ref, right_ref, left_ref, far_hbm, act_own, act_near, act_far,
    keep_ref, send_ref, grads, act, sem
):
    feat = grads.shape[1]
    tile = keep_ref.shape[0]
    xh = lax.axis_index("xh")
    terms = stacked_copies((act_own, act_near, act_far), act, sem)
    far = far_hbm.shape[0]
    terms.append(
        pltpu.make_async_copy(
            far_hbm.at[:, pl.ds(feat, feat)], grads.at[pl.ds(grads.shape[0] - far, far)], sem.at[3]
        )
    )
    for load in terms:
        load.start()
    join((own_ref, right_ref, left_ref), feat, 2 * feat, grads)
    for load in terms:
        load.wait()

    def rows_of(part):
        low = pl.multiple_of(part * tile, tile)
        return contract(act[:, pl.ds(low, tile)], grads[...], 0, 0)

    send_ref[...] = rows_of(1 - xh).astype(bf16)
    keep_ref[...] = rows_of(xh)


def second_grads(pieces, acts):
    feat = pieces[0].shape[1] // 2
    count = sum(p.shape[0] for p in pieces)
    width = acts[0].shape[1]
    tile = width // XH
    return pl.pallas_call(
        second_grads_body,
        in_specs=[IN_VMEM] * 3 + [IN_PLACE] * 4,
        out_specs=[IN_VMEM] * 2,
        out_shape=[
            jax.ShapeDtypeStruct((tile, feat), f32),
            jax.ShapeDtypeStruct((tile, feat), bf16),
        ],
        scratch_shapes=[
            pltpu.VMEM((count, feat), bf16),
            pltpu.VMEM((count, width), bf16),
            pltpu.SemaphoreType.DMA((4,)),
        ],
        compiler_params=params(12),
        name="second_grads",
    )(*pieces[:3], *[pinned(v) for v in (pieces[3],) + tuple(acts)])


def sum_pairs_body(in_ref, out_ref):
    count, _, tile = in_ref.shape
    for i in range(count // XH):
        terms = [in_ref[XH * i + k].astype(f32) for k in range(XH)]
        out_ref[0, :, i * tile : (i + 1) * tile] = sum(terms[1:], terms[0])


def sum_pairs(spread):
    count, own, tile = spread.shape
    return pl.pallas_call(
        sum_pairs_body,
        in_specs=[IN_VMEM],
        out_specs=IN_VMEM,
        out_shape=jax.ShapeDtypeStruct((1, own, count // XH * tile), f32),
        compiler_params=params(4),
        name="sum_pairs",
    )(spread)


def token_logits_body(
    back_ref, x_hbm, g_hbm, disp_hbm, comb_hbm, gl_ref, slots_ref, router_ref,
    mix, disp_ref, comb_ref, x_ref, g_ref, x_sem, g_sem, weight_sem
):
    experts, images, double = back_ref.shape
    feat = double // 2
    width = GROUP * PATCHES
    rows = GROUP * experts
    total = experts * images
    x_copies = block_copies(x_hbm, x_ref, x_sem)
    g_copies = block_copies(g_hbm, g_ref, g_sem)
    weight_copies = [
        pltpu.make_async_copy(disp_hbm, disp_ref, weight_sem.at[0]),
        pltpu.make_async_copy(comb_hbm, comb_ref, weight_sem.at[1]),
    ]
    for copy in g_copies[:2] + x_copies[:2] + weight_copies:
        copy.start()
    mix[...] = jnp.dot(
        swap_matrix(total, images),
        back_ref[...].reshape(total, double),
        preferred_element_type=f32,
    ).astype(bf16)
    image = lane_images(width)

    def picked(both):
        out = both[:experts]
        for i in range(1, GROUP):
            out = jnp.where(image == i, both[i * experts : (i + 1) * experts], out)
        return out

    for copy in weight_copies:
        copy.wait()
    router_sum = None
    for first in range(0, images // GROUP, 2):
        pair = (first, first + 1)
        grad_comb, grad_disp, grad_logits = {}, {}, {}
        for b in pair:
            g_copies[b].wait()
            x_copies[b].wait()
        if first == 0:
            for copy in g_copies[2:] + x_copies[2:]:
                copy.start()
        for b in pair:
            block = mix[b * rows : (b + 1) * rows, :]
            slots_ref[b] = block[:, feat:]
            g = g_ref[b * width : (b + 1) * width, :]
            grad_comb[b] = picked(contract(block[:, :feat], g, 1, 1))
            x = x_ref[b * width : (b + 1) * width, :]
            grad_disp[b] = picked(contract(block[:, feat:], x, 1, 1))
        for b in pair:
            both = comb_ref[b] * grad_comb[b]
            comb_part = both - comb_ref[b] * jnp.sum(both, axis=0, keepdims=True)
            both = disp_ref[b] * grad_disp[b]
            disp_part = both - disp_ref[b] * per_image(both, image, jnp.sum, 0.0)
            grad_logits[b] = (comb_part + disp_part).astype(bf16)
            gl_ref[b] = grad_logits[b]
        for b in pair:
            part = jnp.dot(
                grad_logits[b], x_ref[b * width : (b + 1) * width, :], preferred_element_type=f32
            )
            router_sum = part if router_sum is None else router_sum + part
    router_ref[...] = router_sum


def token_logits(back, tokens, g_outputs, dispatch, combine):
    experts, images, double = back.shape
    rows, feat = tokens.shape
    steps, _, width = dispatch.shape
    return pl.pallas_call(
        token_logits_body,
        in_specs=[IN_VMEM] + [IN_PLACE] * 4,
        out_specs=[IN_VMEM] * 3,
        out_shape=[
            jax.ShapeDtypeStruct((steps, experts, width), bf16),
            jax.ShapeDtypeStruct((steps, GROUP * experts, feat), bf16),
            jax.ShapeDtypeStruct((experts, feat), f32),
        ],
        scratch_shapes=[
            pltpu.VMEM((experts * images, double), bf16),
            pltpu.VMEM(dispatch.shape, f32),
            pltpu.VMEM(combine.shape, f32),
            pltpu.VMEM((rows, feat), bf16),
            pltpu.VMEM((rows, feat), bf16),
            pltpu.SemaphoreType.DMA((steps,)),
            pltpu.SemaphoreType.DMA((steps,)),
            pltpu.SemaphoreType.DMA((2,)),
        ],
        compiler_params=params(20),
        name="token_logits",
    )(back, *[pinned(v) for v in (tokens, g_outputs, dispatch, combine)])


def token_grads_body(gl_ref, slots_ref, disp_ref, rt_ref, out_ref):
    image = lane_images(gl_ref.shape[2])
    left = jnp.concatenate([per_slot_rows(disp_ref[0], image), gl_ref[0]], axis=0)
    right = jnp.concatenate([slots_ref[0], rt_ref[...]], axis=0)
    out_ref[...] = contract(left, right, 0, 0).astype(bf16)


def token_grads(grad_logits, slots, dispatch, rt):
    steps, experts, width = grad_logits.shape
    feat = slots.shape[2]
    return pl.pallas_call(
        token_grads_body,
        grid=(steps,),
        in_specs=[
            pl.BlockSpec((1, experts, width), lambda i: (i, 0, 0)),
            pl.BlockSpec((1, GROUP * experts, feat), lambda i: (i, 0, 0)),
            pl.BlockSpec((1, experts, width), lambda i: (i, 0, 0)),
            pl.BlockSpec((experts, feat), lambda i: (0, 0)),
        ],
        out_specs=pl.BlockSpec((width, feat), lambda i: (i, 0)),
        out_shape=jax.ShapeDtypeStruct((steps * width, feat), bf16),
        compiler_params=params(12),
        name="token_grads",
    )(grad_logits, slots, dispatch, rt)


def shift(value, axis, by, count):
    return lax.ppermute(value, axis, [(i, (i + by) % count) for i in range(count)])


def axis_sum(value, axis, count):
    return sum([shift(value, axis, by, count) for by in range(1, count)], value)


def solution(mesh):
    dp, experts = mesh.shape["dp"], mesh.shape["expert"]
    ny, nz = dp // XH, experts // 4
    fine = Mesh(
        mesh.devices.reshape(ny, XH, nz, 2, 2), ("y", "xh", "z", "xl", "core")
    )
    dp_axes = ("y", "xh")
    ex_axes = ("z", "xl", "core")

    def over_experts(value):
        return lax.all_to_all(value, ex_axes, split_axis=0, concat_axis=0, tiled=True)

    def on_device(tokens, router, w_in, w_out, g_outputs):
        rt = router.T
        slots, dispatch, combine = token_forward(tokens, rt, g_outputs)
        rows = over_experts(slots).reshape(-1, slots.shape[2])
        right = shift(rows, "y", 1, ny)
        left = shift(rows, "y", ny - 1, ny)
        results, act_own, pre_own = expert_rows(rows, w_in, w_out, ny)
        rows, results = lax.optimization_barrier((rows, results))
        far = shift(rows, "y", ny // 2, ny)
        back = over_experts(results.reshape(slots.shape))
        act_near, pre_near = near_terms(right, left, w_in, w_out, ny)
        back, act_near, pre_near = lax.optimization_barrier((back, act_near, pre_near))
        grad_logits, slot_grads, router_term = token_logits(
            back, tokens, g_outputs, dispatch, combine
        )
        far, router_term = lax.optimization_barrier((far, router_term))
        pieces = (rows, right, left, far)
        terms_in, act_far = first_grads(pieces, pre_own, pre_near, w_in, w_out, ny)
        total = axis_sum(router_term, "xh", XH)
        total, terms_in = lax.optimization_barrier((total, terms_in))
        spread = lax.all_to_all(terms_in, dp_axes, split_axis=0, concat_axis=0, tiled=True)
        keep_out, send_out = second_grads(pieces, (act_own, act_near, act_far))
        came_out = shift(send_out, "xh", 1, XH)
        total = axis_sum(axis_sum(total, "core", 2), "z", nz)
        total, keep_out, send_out = lax.optimization_barrier((total, keep_out, send_out))
        total, spread = lax.optimization_barrier((axis_sum(total, "y", ny), spread))
        grad_first = sum_pairs(spread)
        grad_router = axis_sum(total, "xl", 2).T
        grad_second = keep_out + came_out.astype(f32)
        grad_tok = token_grads(grad_logits, slot_grads, dispatch, rt)
        return grad_tok, grad_router, grad_first, grad_second[None]

    return jax.shard_map(
        on_device,
        mesh=fine,
        in_specs=(
            P(dp_axes + ex_axes, None),
            P(),
            P(ex_axes, None, None),
            P(ex_axes, None, None),
            P(dp_axes + ex_axes, None),
        ),
        out_specs=(
            P(dp_axes + ex_axes, None),
            P(),
            P(ex_axes, dp_axes, None),
            P(ex_axes, dp_axes, None),
        ),
        check_vma=False,
    )
```

```python
import functools

import jax
import jax.numpy as jnp
from jax import lax
from jax.experimental import pallas as pl
from jax.experimental.pallas import tpu as pltpu
from jax.sharding import Mesh, PartitionSpec as P

PATCHES = 196
GROUP = 4
XH = 2
MIB = 1024 * 1024
GELU_C = 0.7978845608028654
GELU_A = 0.044715

f32 = jnp.float32
bf16 = jnp.bfloat16


def contract(left, right, left_dim, right_dim):
    return lax.dot_general(
        left, right, (((left_dim,), (right_dim,)), ((), ())), preferred_element_type=f32
    )


def params(mib):
    return pltpu.CompilerParams(vmem_limit_bytes=mib * MIB)


def pinned(value):
    return pltpu.with_memory_space_constraint(value, pltpu.HBM)


IN_VMEM = pl.BlockSpec(memory_space=pltpu.VMEM)
IN_PLACE = pl.BlockSpec(memory_space=pltpu.HBM)


def gelu_parts(x):
    x2 = x * x
    th = jnp.tanh(GELU_C * x * (1.0 + GELU_A * x2))
    cdf = 0.5 + 0.5 * th
    slope = cdf + (0.5 * GELU_C) * x * (1.0 - th * th) * (1.0 + (3.0 * GELU_A) * x2)
    return x * cdf, slope


def lane_images(width):
    lane = lax.broadcasted_iota(jnp.int32, (1, width), 1)
    image = jnp.zeros_like(lane)
    for i in range(1, width // PATCHES):
        image = image + (lane >= i * PATCHES).astype(jnp.int32)
    return image


def per_image(values, image, reduce, start):
    width = values.shape[1]
    out = jnp.zeros_like(values)
    for i in range(GROUP):
        low = i * PATCHES // 128 * 128
        high = min(-(-(i + 1) * PATCHES // 128) * 128, width)
        part = jnp.where(image[:, low:high] == i, values[:, low:high], start)
        own = reduce(part, axis=1, keepdims=True)
        out = jnp.where(image == i, own, out)
    return out


def inverse_sum(values, axis, keepdims):
    return 1.0 / jnp.sum(values, axis=axis, keepdims=keepdims)


def per_slot_rows(weights, image):
    return jnp.concatenate(
        [jnp.where(image == i, weights, 0.0) for i in range(GROUP)], axis=0
    ).astype(bf16)


def swap_matrix(total, inner):
    outer = total // inner
    out_row = lax.broadcasted_iota(jnp.int32, (total, total), 0)
    in_row = lax.broadcasted_iota(jnp.int32, (total, total), 1)
    wanted = (out_row % outer) * inner + out_row // outer
    return (in_row == wanted).astype(f32).astype(bf16)


def block_copies(src, dst, sem):
    width = GROUP * PATCHES
    return [
        pltpu.make_async_copy(
            src.at[pl.ds(b * width, width)], dst.at[pl.ds(b * width, width)], sem.at[b]
        )
        for b in range(src.shape[0] // width)
    ]


def token_forward_body(
    rt_hbm, x_hbm, g_hbm, slots_ref, disp_hbm, comb_hbm,
    rt_ref, disp_ref, comb_ref, x_ref, g_ref, acc, x_sem, g_sem, rt_sem, disp_sem, comb_sem
):
    experts, images, double = slots_ref.shape
    feat = double // 2
    width = GROUP * PATCHES
    steps = images // GROUP
    rows = GROUP * experts
    total = experts * images

    x_copies = block_copies(x_hbm, x_ref, x_sem)
    g_copies = block_copies(g_hbm, g_ref, g_sem)
    rt_copy = pltpu.make_async_copy(rt_hbm, rt_ref, rt_sem)
    for copy in [rt_copy] + x_copies + g_copies:
        copy.start()
    weight_copies = [
        pltpu.make_async_copy(disp_ref, disp_hbm, disp_sem),
        pltpu.make_async_copy(comb_ref, comb_hbm, comb_sem),
    ]
    image = lane_images(width)
    rt_copy.wait()
    rt = rt_ref[...]
    spread = {}
    for first in range(0, steps, 2):
        pair = (first, first + 1)
        logits, own = {}, {}
        for b in pair:
            x_copies[b].wait()
        for b in pair:
            logits[b] = contract(rt, x_ref[b * width : (b + 1) * width, :], 1, 1)
        for b in pair:
            top = per_image(logits[b], image, jnp.max, -jnp.inf)
            raised = jnp.exp(logits[b] - top)
            dispatch = raised * per_image(raised, image, inverse_sum, 0.0)
            raised_e = jnp.exp(logits[b] - jnp.max(logits[b], axis=0, keepdims=True))
            combine = raised_e * inverse_sum(raised_e, axis=0, keepdims=True)
            disp_ref[b] = dispatch
            comb_ref[b] = combine
            spread[b] = per_slot_rows(combine, image)
            own[b] = per_slot_rows(dispatch, image)
        for b in pair:
            acc[b * rows : (b + 1) * rows, :feat] = jnp.dot(
                own[b], x_ref[b * width : (b + 1) * width, :], preferred_element_type=f32
            ).astype(bf16)
    for copy in weight_copies:
        copy.start()
    for b in range(steps):
        g_copies[b].wait()
    for b in range(steps):
        acc[b * rows : (b + 1) * rows, feat:] = jnp.dot(
            spread[b], g_ref[b * width : (b + 1) * width, :], preferred_element_type=f32
        ).astype(bf16)
    slots_ref[...] = (
        jnp.dot(swap_matrix(total, experts), acc[...], preferred_element_type=f32)
        .astype(bf16)
        .reshape(experts, images, double)
    )
    for copy in weight_copies:
        copy.wait()


def token_forward(tokens, rt, g_outputs):
    rows, feat = tokens.shape
    experts = rt.shape[0]
    images = rows // PATCHES
    width = GROUP * PATCHES
    steps = rows // width
    return pl.pallas_call(
        token_forward_body,
        in_specs=[IN_PLACE] * 3,
        out_specs=[IN_VMEM, IN_PLACE, IN_PLACE],
        out_shape=[
            jax.ShapeDtypeStruct((experts, images, 2 * feat), bf16),
            pltpu.HBM((steps, experts, width), f32),
            pltpu.HBM((steps, experts, width), f32),
        ],
        scratch_shapes=[
            pltpu.VMEM((experts, feat), bf16),
            pltpu.VMEM((steps, experts, width), f32),
            pltpu.VMEM((steps, experts, width), f32),
            pltpu.VMEM((rows, feat), bf16),
            pltpu.VMEM((rows, feat), bf16),
            pltpu.VMEM((experts * images, 2 * feat), bf16),
            pltpu.SemaphoreType.DMA((steps,)),
            pltpu.SemaphoreType.DMA((steps,)),
            pltpu.SemaphoreType.DMA(()),
            pltpu.SemaphoreType.DMA(()),
            pltpu.SemaphoreType.DMA(()),
        ],
        compiler_params=params(20),
        name="token_forward",
    )(pinned(rt), pinned(tokens), pinned(g_outputs))


def hidden_terms(rows, grads, w1, w2):
    act, slope = gelu_parts(jnp.dot(rows, w1, preferred_element_type=f32))
    return act.astype(bf16), (contract(grads, w2, 1, 1) * slope).astype(bf16)


def expert_body(
    rows_ref, w1_ref, w2_ref, out_hbm, act_hbm, pre_hbm, out_ref, act_ref, pre_ref, sem
):
    feat = w1_ref.shape[1]
    hidden = w1_ref.shape[2]
    tile = act_ref.shape[1]
    part_at = lax.axis_index("y")
    rows = rows_ref[:, :feat]
    grads = rows_ref[:, feat:]
    made, back = None, None
    stores = [
        pltpu.make_async_copy(src, dst, sem.at[k])
        for k, (src, dst) in enumerate(
            ((act_ref, act_hbm), (pre_ref, pre_hbm), (out_ref, out_hbm))
        )
    ]
    for i in range(hidden // tile):
        w1 = w1_ref[0, :, i * tile : (i + 1) * tile]
        w2 = w2_ref[0, i * tile : (i + 1) * tile, :]
        act, grad_pre = hidden_terms(rows, grads, w1, w2)

        @pl.when(part_at == i)
        def _():
            act_ref[...] = act
            pre_ref[...] = grad_pre

        if i == hidden // tile - 1:
            stores[0].start()
            stores[1].start()
        part = jnp.dot(act, w2, preferred_element_type=f32)
        made = part if made is None else made + part
        part = contract(grad_pre, w1, 1, 1)
        back = part if back is None else back + part
    out_ref[:, :feat] = made.astype(bf16)
    out_ref[:, feat:] = back.astype(bf16)
    stores[2].start()
    for store in stores:
        store.wait()


def expert_rows(rows, w_in, w_out, parts):
    tile = w_in.shape[2] // parts
    shapes = [rows.shape, (rows.shape[0], tile), (rows.shape[0], tile)]
    return pl.pallas_call(
        expert_body,
        in_specs=[IN_VMEM] * 3,
        out_specs=[IN_PLACE] * 3,
        out_shape=[pltpu.HBM(shape, bf16) for shape in shapes],
        scratch_shapes=[pltpu.VMEM(shape, bf16) for shape in shapes]
        + [pltpu.SemaphoreType.DMA((3,))],
        compiler_params=params(12),
        name="expert_rows",
    )(rows, w_in, w_out)


def slice_copies(w1_hbm, w2_hbm, w1, w2, sem):
    tile = w1.shape[1]
    low = pl.multiple_of(lax.axis_index("y") * tile, tile)
    return (
        pltpu.make_async_copy(w1_hbm.at[0, :, pl.ds(low, tile)], w1, sem.at[0]),
        pltpu.make_async_copy(w2_hbm.at[0, pl.ds(low, tile), :], w2, sem.at[1]),
    )


def stacked_copies(sources, out, sem):
    copies, at = [], 0
    for k, source in enumerate(sources):
        rows = source.shape[0]
        copies.append(pltpu.make_async_copy(source, out.at[pl.ds(at, rows)], sem.at[k]))
        at += rows
    return copies


def join(pieces, low, high, out):
    at = 0
    for piece in pieces:
        out[at : at + piece.shape[0], :] = piece[:, low:high]
        at += piece.shape[0]


def near_terms_body(
    right_ref, left_ref, w1_hbm, w2_hbm, act_hbm, pre_hbm, act, pre, both, w1, w2, sem, out_sem
):
    feat = w1.shape[0]
    loads = slice_copies(w1_hbm, w2_hbm, w1, w2, sem)
    for load in loads:
        load.start()
    join((right_ref, left_ref), 0, 2 * feat, both)
    for load in loads:
        load.wait()
    act[...], pre[...] = hidden_terms(both[:, :feat], both[:, feat:], w1[...], w2[...])
    stores = (
        pltpu.make_async_copy(act, act_hbm, out_sem.at[0]),
        pltpu.make_async_copy(pre, pre_hbm, out_sem.at[1]),
    )
    for store in stores:
        store.start()
    for store in stores:
        store.wait()


def near_terms(right, left, w_in, w_out, parts):
    feat, hidden = w_in.shape[1:]
    tile = hidden // parts
    count = right.shape[0] + left.shape[0]
    return pl.pallas_call(
        near_terms_body,
        in_specs=[IN_VMEM] * 2 + [IN_PLACE] * 2,
        out_specs=[IN_PLACE] * 2,
        out_shape=[pltpu.HBM((count, tile), bf16)] * 2,
        scratch_shapes=[
            pltpu.VMEM((count, tile), bf16),
            pltpu.VMEM((count, tile), bf16),
            pltpu.VMEM((count, 2 * feat), bf16),
            pltpu.VMEM((feat, tile), bf16),
            pltpu.VMEM((tile, feat), bf16),
            pltpu.SemaphoreType.DMA((2,)),
            pltpu.SemaphoreType.DMA((2,)),
        ],
        compiler_params=params(16),
        name="near_terms",
    )(right, left, pinned(w_in), pinned(w_out))


def first_grads_body(
    own_ref, right_ref, left_ref, far_a, far_b, pre_own, pre_near, w1_hbm, w2_hbm,
    keep_ref, send_ref, act_far, rows, pre, far, w1, w2, sem, pre_sem
):
    feat = w1.shape[0]
    xh = lax.axis_index("xh")
    loads = slice_copies(w1_hbm, w2_hbm, w1, w2, sem)
    terms = stacked_copies((pre_own, pre_near), pre, pre_sem)
    for load in terms + list(loads):
        load.start()
    join((own_ref, right_ref, left_ref), 0, feat, rows)
    join((far_a, far_b), 0, 2 * feat, far)
    for load in terms:
        load.wait()
    total = contract(rows[...], pre[...], 0, 0)
    for load in loads:
        load.wait()
    act, pre_far = hidden_terms(far[:, :feat], far[:, feat:], w1[...], w2[...])
    act_far[...] = act
    total = total + contract(far[:, :feat], pre_far, 0, 0)
    parts, own, _ = keep_ref.shape
    for i in range(parts):
        low = total[XH * i * own : (XH * i + 1) * own]
        high = total[(XH * i + 1) * own : XH * (i + 1) * own]
        send_ref[i] = jnp.where(xh == 0, high, low).astype(bf16)
        keep_ref[i] = jnp.where(xh == 0, low, high)


def first_grads(pieces, pre_own, pre_near, w_in, w_out, parts):
    feat, hidden = w_in.shape[1:]
    tile = hidden // parts
    own = feat // (parts * XH)
    near_count = sum(p.shape[0] for p in pieces[:3])
    far_count = sum(p.shape[0] for p in pieces[3:])
    return pl.pallas_call(
        first_grads_body,
        in_specs=[IN_VMEM] * 5 + [IN_PLACE] * 4,
        out_specs=[IN_VMEM] * 3,
        out_shape=[
            jax.ShapeDtypeStruct((parts, own, tile), f32),
            jax.ShapeDtypeStruct((parts, own, tile), bf16),
            jax.ShapeDtypeStruct((far_count, tile), bf16),
        ],
        scratch_shapes=[
            pltpu.VMEM((near_count, feat), bf16),
            pltpu.VMEM((near_count, tile), bf16),
            pltpu.VMEM((far_count, 2 * feat), bf16),
            pltpu.VMEM((feat, tile), bf16),
            pltpu.VMEM((tile, feat), bf16),
            pltpu.SemaphoreType.DMA((2,)),
            pltpu.SemaphoreType.DMA((2,)),
        ],
        compiler_params=params(20),
        name="first_grads",
    )(*pieces, pinned(pre_own), pinned(pre_near), pinned(w_in), pinned(w_out))


def second_grads_body(
    own_ref, right_ref, left_ref, far_a, far_b, act_own, act_near, act_far,
    keep_ref, send_ref, grads, act, sem
):
    feat = grads.shape[1]
    tile = keep_ref.shape[0]
    xh = lax.axis_index("xh")
    terms = stacked_copies((act_own, act_near), act, sem)
    for load in terms:
        load.start()
    join((own_ref, right_ref, left_ref, far_a, far_b), feat, 2 * feat, grads)
    act[act.shape[0] - act_far.shape[0] :, :] = act_far[...]
    for load in terms:
        load.wait()

    def rows_of(part):
        low = pl.multiple_of(part * tile, tile)
        return contract(act[:, pl.ds(low, tile)], grads[...], 0, 0)

    send_ref[...] = rows_of(1 - xh).astype(bf16)
    keep_ref[...] = rows_of(xh)


def second_grads(pieces, acts):
    feat = pieces[0].shape[1] // 2
    count = sum(p.shape[0] for p in pieces)
    width = acts[0].shape[1]
    tile = width // XH
    return pl.pallas_call(
        second_grads_body,
        in_specs=[IN_VMEM] * 5 + [IN_PLACE] * 2 + [IN_VMEM],
        out_specs=[IN_VMEM] * 2,
        out_shape=[
            jax.ShapeDtypeStruct((tile, feat), f32),
            jax.ShapeDtypeStruct((tile, feat), bf16),
        ],
        scratch_shapes=[
            pltpu.VMEM((count, feat), bf16),
            pltpu.VMEM((count, width), bf16),
            pltpu.SemaphoreType.DMA((2,)),
        ],
        compiler_params=params(12),
        name="second_grads",
    )(*pieces, pinned(acts[0]), pinned(acts[1]), acts[2])


def finish_body(spread_ref, keep_ref, came_ref, first_ref, second_ref):
    parts, _, tile = spread_ref.shape
    for i in range(parts):
        first_ref[0, :, i * tile : (i + 1) * tile] = spread_ref[i].astype(f32)
    second_ref[0] = keep_ref[...] + came_ref[...].astype(f32)


def finish(spread, keep, came):
    parts, own, tile = spread.shape
    return pl.pallas_call(
        finish_body,
        in_specs=[IN_VMEM] * 3,
        out_specs=[IN_VMEM] * 2,
        out_shape=[
            jax.ShapeDtypeStruct((1, own, parts * tile), f32),
            jax.ShapeDtypeStruct((1,) + keep.shape, f32),
        ],
        compiler_params=params(8),
        name="finish",
    )(spread, keep, came)


def token_logits_body(
    back_ref, x_hbm, g_hbm, disp_hbm, comb_hbm, gl_ref, slots_ref, router_ref,
    mix, disp_ref, comb_ref, x_ref, g_ref, x_sem, g_sem, weight_sem
):
    experts, images, double = back_ref.shape
    feat = double // 2
    width = GROUP * PATCHES
    rows = GROUP * experts
    total = experts * images
    x_copies = block_copies(x_hbm, x_ref, x_sem)
    g_copies = block_copies(g_hbm, g_ref, g_sem)
    for x_copy, g_copy in zip(x_copies, g_copies):
        g_copy.start()
        x_copy.start()
    weight_copies = [
        pltpu.make_async_copy(disp_hbm, disp_ref, weight_sem.at[0]),
        pltpu.make_async_copy(comb_hbm, comb_ref, weight_sem.at[1]),
    ]
    for copy in weight_copies:
        copy.start()
    mix[...] = jnp.dot(
        swap_matrix(total, images),
        back_ref[...].reshape(total, double),
        preferred_element_type=f32,
    ).astype(bf16)
    image = lane_images(width)

    def picked(both):
        out = both[:experts]
        for i in range(1, GROUP):
            out = jnp.where(image == i, both[i * experts : (i + 1) * experts], out)
        return out

    for copy in weight_copies:
        copy.wait()
    router_sum = None
    for first in range(0, images // GROUP, 2):
        pair = (first, first + 1)
        grad_comb, grad_disp, grad_logits = {}, {}, {}
        for b in pair:
            g_copies[b].wait()
            x_copies[b].wait()
        for b in pair:
            block = mix[b * rows : (b + 1) * rows, :]
            slots_ref[b] = block[:, feat:]
            g = g_ref[b * width : (b + 1) * width, :]
            grad_comb[b] = picked(contract(block[:, :feat], g, 1, 1))
            x = x_ref[b * width : (b + 1) * width, :]
            grad_disp[b] = picked(contract(block[:, feat:], x, 1, 1))
        for b in pair:
            both = comb_ref[b] * grad_comb[b]
            comb_part = both - comb_ref[b] * jnp.sum(both, axis=0, keepdims=True)
            both = disp_ref[b] * grad_disp[b]
            disp_part = both - disp_ref[b] * per_image(both, image, jnp.sum, 0.0)
            grad_logits[b] = (comb_part + disp_part).astype(bf16)
            gl_ref[b] = grad_logits[b]
        for b in pair:
            part = jnp.dot(
                grad_logits[b], x_ref[b * width : (b + 1) * width, :], preferred_element_type=f32
            )
            router_sum = part if router_sum is None else router_sum + part
    router_ref[...] = router_sum


def token_logits(back, tokens, g_outputs, dispatch, combine):
    experts, images, double = back.shape
    rows, feat = tokens.shape
    steps, _, width = dispatch.shape
    return pl.pallas_call(
        token_logits_body,
        in_specs=[IN_VMEM] + [IN_PLACE] * 4,
        out_specs=[IN_VMEM] * 3,
        out_shape=[
            jax.ShapeDtypeStruct((steps, experts, width), bf16),
            jax.ShapeDtypeStruct((steps, GROUP * experts, feat), bf16),
            jax.ShapeDtypeStruct((experts, feat), f32),
        ],
        scratch_shapes=[
            pltpu.VMEM((experts * images, double), bf16),
            pltpu.VMEM(dispatch.shape, f32),
            pltpu.VMEM(combine.shape, f32),
            pltpu.VMEM((rows, feat), bf16),
            pltpu.VMEM((rows, feat), bf16),
            pltpu.SemaphoreType.DMA((steps,)),
            pltpu.SemaphoreType.DMA((steps,)),
            pltpu.SemaphoreType.DMA((2,)),
        ],
        compiler_params=params(20),
        name="token_logits",
    )(back, *[pinned(v) for v in (tokens, g_outputs, dispatch, combine)])


def token_grads_body(gl_ref, slots_ref, disp_ref, rt_ref, out_ref):
    image = lane_images(gl_ref.shape[2])
    left = jnp.concatenate([per_slot_rows(disp_ref[0], image), gl_ref[0]], axis=0)
    right = jnp.concatenate([slots_ref[0], rt_ref[...]], axis=0)
    out_ref[...] = contract(left, right, 0, 0).astype(bf16)


def token_grads(grad_logits, slots, dispatch, rt):
    steps, experts, width = grad_logits.shape
    feat = slots.shape[2]
    return pl.pallas_call(
        token_grads_body,
        grid=(steps,),
        in_specs=[
            pl.BlockSpec((1, experts, width), lambda i: (i, 0, 0)),
            pl.BlockSpec((1, GROUP * experts, feat), lambda i: (i, 0, 0)),
            pl.BlockSpec((1, experts, width), lambda i: (i, 0, 0)),
            pl.BlockSpec((experts, feat), lambda i: (0, 0)),
        ],
        out_specs=pl.BlockSpec((width, feat), lambda i: (i, 0)),
        out_shape=jax.ShapeDtypeStruct((steps * width, feat), bf16),
        compiler_params=params(12),
        name="token_grads",
    )(grad_logits, slots, dispatch, rt)


def shift(value, axis, by, count):
    return lax.ppermute(value, axis, [(i, (i + by) % count) for i in range(count)])


def axis_sum(value, axis, count):
    return sum([shift(value, axis, by, count) for by in range(1, count)], value)


def solution(mesh):
    dp, experts = mesh.shape["dp"], mesh.shape["expert"]
    ny, nz = dp // XH, experts // 4
    fine = Mesh(
        mesh.devices.reshape(ny, XH, nz, 2, 2), ("y", "xh", "z", "xl", "core")
    )
    dp_axes = ("y", "xh")
    ex_axes = ("z", "xl", "core")

    def over_experts(value):
        return lax.all_to_all(value, ex_axes, split_axis=0, concat_axis=0, tiled=True)

    def on_device(tokens, router, w_in, w_out, g_outputs):
        rt = router.T
        slots, dispatch, combine = token_forward(tokens, rt, g_outputs)
        rows = over_experts(slots).reshape(-1, slots.shape[2])
        mid = rows.shape[0] // 2
        right = shift(rows, "y", 1, ny)
        left = shift(rows, "y", ny - 1, ny)
        results, act_own, pre_own = expert_rows(rows, w_in, w_out, ny)
        back = over_experts(results.reshape(slots.shape))
        far_a = shift(right[:mid], "y", 1, ny)
        far_b = shift(left[mid:], "y", ny - 1, ny)
        act_near, pre_near = near_terms(right, left, w_in, w_out, ny)
        back, act_near, pre_near = lax.optimization_barrier((back, act_near, pre_near))
        grad_logits, slot_grads, router_term = token_logits(
            back, tokens, g_outputs, dispatch, combine
        )
        far_a, far_b, router_term = lax.optimization_barrier((far_a, far_b, router_term))
        pieces = (rows, right, left, far_a, far_b)
        keep_in, send_in, act_far = first_grads(pieces, pre_own, pre_near, w_in, w_out, ny)
        keep_out, send_out = second_grads(pieces, (act_own, act_near, act_far))
        total = axis_sum(router_term, "xh", XH)
        total, send_in = lax.optimization_barrier((total, send_in))
        came_in = shift(send_in, "xh", 1, XH)
        total = axis_sum(axis_sum(total, "core", 2), "xl", 2)
        total, keep_out, send_out = lax.optimization_barrier((total, keep_out, send_out))
        total = axis_sum(total, "y", ny)
        came_in, send_out = lax.optimization_barrier((came_in, send_out))
        came_out = shift(send_out, "xh", 1, XH)
        part_in = (keep_in + came_in.astype(f32)).astype(bf16)
        total, part_in, grad_logits = lax.optimization_barrier((total, part_in, grad_logits))
        spread = lax.all_to_all(part_in, "y", split_axis=0, concat_axis=0, tiled=True)
        grad_router = axis_sum(total, "z", nz).T
        grad_first, grad_second = finish(spread, keep_out, came_out)
        grad_tok = token_grads(grad_logits, slot_grads, dispatch, rt)
        return grad_tok, grad_router, grad_first, grad_second

    return jax.shard_map(
        on_device,
        mesh=fine,
        in_specs=(
            P(dp_axes + ex_axes, None),
            P(),
            P(ex_axes, None, None),
            P(ex_axes, None, None),
            P(dp_axes + ex_axes, None),
        ),
        out_specs=(
            P(dp_axes + ex_axes, None),
            P(),
            P(ex_axes, dp_axes, None),
            P(ex_axes, dp_axes, None),
        ),
        check_vma=False,
    )
```

```python
import functools

import jax
import jax.numpy as jnp
from jax import lax
from jax.experimental import pallas as pl
from jax.experimental.pallas import tpu as pltpu
from jax.sharding import Mesh, PartitionSpec as P

PATCHES = 196
GROUP = 4
XH = 2
MIB = 1024 * 1024
GELU_C = 0.7978845608028654
GELU_A = 0.044715

f32 = jnp.float32
bf16 = jnp.bfloat16


def contract(left, right, left_dim, right_dim):
    return lax.dot_general(
        left, right, (((left_dim,), (right_dim,)), ((), ())), preferred_element_type=f32
    )


def params(mib):
    return pltpu.CompilerParams(vmem_limit_bytes=mib * MIB)


def pinned(value):
    return pltpu.with_memory_space_constraint(value, pltpu.HBM)


IN_VMEM = pl.BlockSpec(memory_space=pltpu.VMEM)
IN_PLACE = pl.BlockSpec(memory_space=pltpu.HBM)


def gelu_parts(x):
    x2 = x * x
    th = jnp.tanh(GELU_C * x * (1.0 + GELU_A * x2))
    cdf = 0.5 + 0.5 * th
    slope = cdf + (0.5 * GELU_C) * x * (1.0 - th * th) * (1.0 + (3.0 * GELU_A) * x2)
    return x * cdf, slope


def lane_images(width):
    lane = lax.broadcasted_iota(jnp.int32, (1, width), 1)
    image = jnp.zeros_like(lane)
    for i in range(1, width // PATCHES):
        image = image + (lane >= i * PATCHES).astype(jnp.int32)
    return image


def per_image(values, image, reduce, start):
    width = values.shape[1]
    out = jnp.zeros_like(values)
    for i in range(GROUP):
        low = i * PATCHES // 128 * 128
        high = min(-(-(i + 1) * PATCHES // 128) * 128, width)
        part = jnp.where(image[:, low:high] == i, values[:, low:high], start)
        own = reduce(part, axis=1, keepdims=True)
        out = jnp.where(image == i, own, out)
    return out


def inverse_sum(values, axis, keepdims):
    return 1.0 / jnp.sum(values, axis=axis, keepdims=keepdims)


def per_slot_rows(weights, image):
    return jnp.concatenate(
        [jnp.where(image == i, weights, 0.0) for i in range(GROUP)], axis=0
    ).astype(bf16)


def swap_matrix(total, inner):
    outer = total // inner
    out_row = lax.broadcasted_iota(jnp.int32, (total, total), 0)
    in_row = lax.broadcasted_iota(jnp.int32, (total, total), 1)
    wanted = (out_row % outer) * inner + out_row // outer
    return (in_row == wanted).astype(f32).astype(bf16)


def block_copies(src, dst, sem):
    width = GROUP * PATCHES
    return [
        pltpu.make_async_copy(
            src.at[pl.ds(b * width, width)], dst.at[pl.ds(b * width, width)], sem.at[b]
        )
        for b in range(src.shape[0] // width)
    ]


def token_forward_body(
    rt_hbm, x_hbm, g_hbm, slots_ref, disp_hbm, comb_hbm,
    rt_ref, disp_ref, comb_ref, x_ref, g_ref, acc, x_sem, g_sem, rt_sem, disp_sem, comb_sem
):
    experts, images, double = slots_ref.shape
    feat = double // 2
    width = GROUP * PATCHES
    steps = images // GROUP
    rows = GROUP * experts
    total = experts * images

    x_copies = block_copies(x_hbm, x_ref, x_sem)
    g_copies = block_copies(g_hbm, g_ref, g_sem)
    rt_copy = pltpu.make_async_copy(rt_hbm, rt_ref, rt_sem)
    for copy in [rt_copy] + x_copies + g_copies:
        copy.start()
    weight_copies = [
        pltpu.make_async_copy(disp_ref, disp_hbm, disp_sem),
        pltpu.make_async_copy(comb_ref, comb_hbm, comb_sem),
    ]
    image = lane_images(width)
    rt_copy.wait()
    rt = rt_ref[...]
    spread = {}
    for first in range(0, steps, 2):
        pair = (first, first + 1)
        logits, own = {}, {}
        for b in pair:
            x_copies[b].wait()
        for b in pair:
            logits[b] = contract(rt, x_ref[b * width : (b + 1) * width, :], 1, 1)
        for b in pair:
            top = per_image(logits[b], image, jnp.max, -jnp.inf)
            raised = jnp.exp(logits[b] - top)
            dispatch = raised * per_image(raised, image, inverse_sum, 0.0)
            raised_e = jnp.exp(logits[b] - jnp.max(logits[b], axis=0, keepdims=True))
            combine = raised_e * inverse_sum(raised_e, axis=0, keepdims=True)
            disp_ref[b] = dispatch
            comb_ref[b] = combine
            spread[b] = per_slot_rows(combine, image)
            own[b] = per_slot_rows(dispatch, image)
        for b in pair:
            acc[b * rows : (b + 1) * rows, :feat] = jnp.dot(
                own[b], x_ref[b * width : (b + 1) * width, :], preferred_element_type=f32
            ).astype(bf16)
    for copy in weight_copies:
        copy.start()
    for b in range(steps):
        g_copies[b].wait()
    for b in range(steps):
        acc[b * rows : (b + 1) * rows, feat:] = jnp.dot(
            spread[b], g_ref[b * width : (b + 1) * width, :], preferred_element_type=f32
        ).astype(bf16)
    slots_ref[...] = (
        jnp.dot(swap_matrix(total, experts), acc[...], preferred_element_type=f32)
        .astype(bf16)
        .reshape(experts, images, double)
    )
    for copy in weight_copies:
        copy.wait()


def token_forward(tokens, rt, g_outputs):
    rows, feat = tokens.shape
    experts = rt.shape[0]
    images = rows // PATCHES
    width = GROUP * PATCHES
    steps = rows // width
    return pl.pallas_call(
        token_forward_body,
        in_specs=[IN_PLACE] * 3,
        out_specs=[IN_VMEM, IN_PLACE, IN_PLACE],
        out_shape=[
            jax.ShapeDtypeStruct((experts, images, 2 * feat), bf16),
            pltpu.HBM((steps, experts, width), f32),
            pltpu.HBM((steps, experts, width), f32),
        ],
        scratch_shapes=[
            pltpu.VMEM((experts, feat), bf16),
            pltpu.VMEM((steps, experts, width), f32),
            pltpu.VMEM((steps, experts, width), f32),
            pltpu.VMEM((rows, feat), bf16),
            pltpu.VMEM((rows, feat), bf16),
            pltpu.VMEM((experts * images, 2 * feat), bf16),
            pltpu.SemaphoreType.DMA((steps,)),
            pltpu.SemaphoreType.DMA((steps,)),
            pltpu.SemaphoreType.DMA(()),
            pltpu.SemaphoreType.DMA(()),
            pltpu.SemaphoreType.DMA(()),
        ],
        compiler_params=params(20),
        name="token_forward",
    )(pinned(rt), pinned(tokens), pinned(g_outputs))


def hidden_terms(rows, grads, w1, w2):
    act, slope = gelu_parts(jnp.dot(rows, w1, preferred_element_type=f32))
    return act.astype(bf16), (contract(grads, w2, 1, 1) * slope).astype(bf16)


def expert_body(
    rows_ref, w1_ref, w2_ref, out_hbm, act_hbm, pre_hbm, out_ref, act_ref, pre_ref, sem
):
    feat = w1_ref.shape[1]
    hidden = w1_ref.shape[2]
    tile = act_ref.shape[1]
    part_at = lax.axis_index("y")
    rows = rows_ref[:, :feat]
    grads = rows_ref[:, feat:]
    made, back = None, None
    stores = [
        pltpu.make_async_copy(src, dst, sem.at[k])
        for k, (src, dst) in enumerate(
            ((act_ref, act_hbm), (pre_ref, pre_hbm), (out_ref, out_hbm))
        )
    ]
    for i in range(hidden // tile):
        w1 = w1_ref[0, :, i * tile : (i + 1) * tile]
        w2 = w2_ref[0, i * tile : (i + 1) * tile, :]
        act, grad_pre = hidden_terms(rows, grads, w1, w2)

        @pl.when(part_at == i)
        def _():
            act_ref[...] = act
            pre_ref[...] = grad_pre

        if i == hidden // tile - 1:
            stores[0].start()
            stores[1].start()
        part = jnp.dot(act, w2, preferred_element_type=f32)
        made = part if made is None else made + part
        part = contract(grad_pre, w1, 1, 1)
        back = part if back is None else back + part
    out_ref[:, :feat] = made.astype(bf16)
    out_ref[:, feat:] = back.astype(bf16)
    stores[2].start()
    for store in stores:
        store.wait()


def expert_rows(rows, w_in, w_out, parts):
    tile = w_in.shape[2] // parts
    shapes = [rows.shape, (rows.shape[0], tile), (rows.shape[0], tile)]
    return pl.pallas_call(
        expert_body,
        in_specs=[IN_VMEM] * 3,
        out_specs=[IN_PLACE] * 3,
        out_shape=[pltpu.HBM(shape, bf16) for shape in shapes],
        scratch_shapes=[pltpu.VMEM(shape, bf16) for shape in shapes]
        + [pltpu.SemaphoreType.DMA((3,))],
        compiler_params=params(12),
        name="expert_rows",
    )(rows, w_in, w_out)


def slice_copies(w1_hbm, w2_hbm, w1, w2, sem):
    tile = w1.shape[1]
    low = pl.multiple_of(lax.axis_index("y") * tile, tile)
    return (
        pltpu.make_async_copy(w1_hbm.at[0, :, pl.ds(low, tile)], w1, sem.at[0]),
        pltpu.make_async_copy(w2_hbm.at[0, pl.ds(low, tile), :], w2, sem.at[1]),
    )


def stacked_copies(sources, out, sem):
    copies, at = [], 0
    for k, source in enumerate(sources):
        rows = source.shape[0]
        copies.append(pltpu.make_async_copy(source, out.at[pl.ds(at, rows)], sem.at[k]))
        at += rows
    return copies


def join(pieces, low, high, out):
    at = 0
    for piece in pieces:
        out[at : at + piece.shape[0], :] = piece[:, low:high]
        at += piece.shape[0]


def near_terms_body(
    right_ref, left_ref, w1_hbm, w2_hbm, act_hbm, pre_hbm, act, pre, both, w1, w2, sem, out_sem
):
    feat = w1.shape[0]
    loads = slice_copies(w1_hbm, w2_hbm, w1, w2, sem)
    for load in loads:
        load.start()
    join((right_ref, left_ref), 0, 2 * feat, both)
    for load in loads:
        load.wait()
    act[...], pre[...] = hidden_terms(both[:, :feat], both[:, feat:], w1[...], w2[...])
    stores = (
        pltpu.make_async_copy(act, act_hbm, out_sem.at[0]),
        pltpu.make_async_copy(pre, pre_hbm, out_sem.at[1]),
    )
    for store in stores:
        store.start()
    for store in stores:
        store.wait()


def near_terms(right, left, w_in, w_out, parts):
    feat, hidden = w_in.shape[1:]
    tile = hidden // parts
    count = right.shape[0] + left.shape[0]
    return pl.pallas_call(
        near_terms_body,
        in_specs=[IN_VMEM] * 2 + [IN_PLACE] * 2,
        out_specs=[IN_PLACE] * 2,
        out_shape=[pltpu.HBM((count, tile), bf16)] * 2,
        scratch_shapes=[
            pltpu.VMEM((count, tile), bf16),
            pltpu.VMEM((count, tile), bf16),
            pltpu.VMEM((count, 2 * feat), bf16),
            pltpu.VMEM((feat, tile), bf16),
            pltpu.VMEM((tile, feat), bf16),
            pltpu.SemaphoreType.DMA((2,)),
            pltpu.SemaphoreType.DMA((2,)),
        ],
        compiler_params=params(16),
        name="near_terms",
    )(right, left, pinned(w_in), pinned(w_out))


def first_grads_body(
    own_ref, right_ref, left_ref, far_a, far_b, pre_own, pre_near, w1_hbm, w2_hbm,
    keep_ref, send_ref, act_far, rows, pre, far, w1, w2, sem, pre_sem
):
    feat = w1.shape[0]
    xh = lax.axis_index("xh")
    loads = slice_copies(w1_hbm, w2_hbm, w1, w2, sem)
    terms = stacked_copies((pre_own, pre_near), pre, pre_sem)
    for load in terms + list(loads):
        load.start()
    join((own_ref, right_ref, left_ref), 0, feat, rows)
    join((far_a, far_b), 0, 2 * feat, far)
    for load in terms:
        load.wait()
    total = contract(rows[...], pre[...], 0, 0)
    for load in loads:
        load.wait()
    act, pre_far = hidden_terms(far[:, :feat], far[:, feat:], w1[...], w2[...])
    act_far[...] = act
    total = total + contract(far[:, :feat], pre_far, 0, 0)
    parts, own, _ = keep_ref.shape
    for i in range(parts):
        low = total[XH * i * own : (XH * i + 1) * own]
        high = total[(XH * i + 1) * own : XH * (i + 1) * own]
        send_ref[i] = jnp.where(xh == 0, high, low).astype(bf16)
        keep_ref[i] = jnp.where(xh == 0, low, high)


def first_grads(pieces, pre_own, pre_near, w_in, w_out, parts):
    feat, hidden = w_in.shape[1:]
    tile = hidden // parts
    own = feat // (parts * XH)
    near_count = sum(p.shape[0] for p in pieces[:3])
    far_count = sum(p.shape[0] for p in pieces[3:])
    return pl.pallas_call(
        first_grads_body,
        in_specs=[IN_VMEM] * 5 + [IN_PLACE] * 4,
        out_specs=[IN_VMEM] * 3,
        out_shape=[
            jax.ShapeDtypeStruct((parts, own, tile), f32),
            jax.ShapeDtypeStruct((parts, own, tile), bf16),
            jax.ShapeDtypeStruct((far_count, tile), bf16),
        ],
        scratch_shapes=[
            pltpu.VMEM((near_count, feat), bf16),
            pltpu.VMEM((near_count, tile), bf16),
            pltpu.VMEM((far_count, 2 * feat), bf16),
            pltpu.VMEM((feat, tile), bf16),
            pltpu.VMEM((tile, feat), bf16),
            pltpu.SemaphoreType.DMA((2,)),
            pltpu.SemaphoreType.DMA((2,)),
        ],
        compiler_params=params(20),
        name="first_grads",
    )(*pieces, pinned(pre_own), pinned(pre_near), pinned(w_in), pinned(w_out))


def second_grads_body(
    own_ref, right_ref, left_ref, far_a, far_b, act_own, act_near, act_far,
    keep_ref, send_ref, grads, act, sem
):
    feat = grads.shape[1]
    tile = keep_ref.shape[0]
    xh = lax.axis_index("xh")
    terms = stacked_copies((act_own, act_near), act, sem)
    for load in terms:
        load.start()
    join((own_ref, right_ref, left_ref, far_a, far_b), feat, 2 * feat, grads)
    act[act.shape[0] - act_far.shape[0] :, :] = act_far[...]
    for load in terms:
        load.wait()

    def rows_of(part):
        low = pl.multiple_of(part * tile, tile)
        return contract(act[:, pl.ds(low, tile)], grads[...], 0, 0)

    send_ref[...] = rows_of(1 - xh).astype(bf16)
    keep_ref[...] = rows_of(xh)


def second_grads(pieces, acts):
    feat = pieces[0].shape[1] // 2
    count = sum(p.shape[0] for p in pieces)
    width = acts[0].shape[1]
    tile = width // XH
    return pl.pallas_call(
        second_grads_body,
        in_specs=[IN_VMEM] * 5 + [IN_PLACE] * 2 + [IN_VMEM],
        out_specs=[IN_VMEM] * 2,
        out_shape=[
            jax.ShapeDtypeStruct((tile, feat), f32),
            jax.ShapeDtypeStruct((tile, feat), bf16),
        ],
        scratch_shapes=[
            pltpu.VMEM((count, feat), bf16),
            pltpu.VMEM((count, width), bf16),
            pltpu.SemaphoreType.DMA((2,)),
        ],
        compiler_params=params(12),
        name="second_grads",
    )(*pieces, pinned(acts[0]), pinned(acts[1]), acts[2])


def finish_body(spread_ref, keep_ref, came_ref, first_ref, second_ref):
    parts, _, tile = spread_ref.shape
    for i in range(parts):
        first_ref[0, :, i * tile : (i + 1) * tile] = spread_ref[i].astype(f32)
    second_ref[0] = keep_ref[...] + came_ref[...].astype(f32)


def finish(spread, keep, came):
    parts, own, tile = spread.shape
    return pl.pallas_call(
        finish_body,
        in_specs=[IN_VMEM] * 3,
        out_specs=[IN_VMEM] * 2,
        out_shape=[
            jax.ShapeDtypeStruct((1, own, parts * tile), f32),
            jax.ShapeDtypeStruct((1,) + keep.shape, f32),
        ],
        compiler_params=params(8),
        name="finish",
    )(spread, keep, came)


def token_logits_body(
    back_ref, x_hbm, g_hbm, disp_hbm, comb_hbm, gl_ref, slots_ref, router_ref,
    mix, disp_ref, comb_ref, x_ref, g_ref, x_sem, g_sem, weight_sem
):
    experts, images, double = back_ref.shape
    feat = double // 2
    width = GROUP * PATCHES
    rows = GROUP * experts
    total = experts * images
    x_copies = block_copies(x_hbm, x_ref, x_sem)
    g_copies = block_copies(g_hbm, g_ref, g_sem)
    for x_copy, g_copy in zip(x_copies, g_copies):
        g_copy.start()
        x_copy.start()
    weight_copies = [
        pltpu.make_async_copy(disp_hbm, disp_ref, weight_sem.at[0]),
        pltpu.make_async_copy(comb_hbm, comb_ref, weight_sem.at[1]),
    ]
    for copy in weight_copies:
        copy.start()
    mix[...] = jnp.dot(
        swap_matrix(total, images),
        back_ref[...].reshape(total, double),
        preferred_element_type=f32,
    ).astype(bf16)
    image = lane_images(width)

    def picked(both):
        out = both[:experts]
        for i in range(1, GROUP):
            out = jnp.where(image == i, both[i * experts : (i + 1) * experts], out)
        return out

    for copy in weight_copies:
        copy.wait()
    router_sum = None
    for first in range(0, images // GROUP, 2):
        pair = (first, first + 1)
        grad_comb, grad_disp, grad_logits = {}, {}, {}
        for b in pair:
            g_copies[b].wait()
            x_copies[b].wait()
        for b in pair:
            block = mix[b * rows : (b + 1) * rows, :]
            slots_ref[b] = block[:, feat:]
            g = g_ref[b * width : (b + 1) * width, :]
            grad_comb[b] = picked(contract(block[:, :feat], g, 1, 1))
            x = x_ref[b * width : (b + 1) * width, :]
            grad_disp[b] = picked(contract(block[:, feat:], x, 1, 1))
        for b in pair:
            both = comb_ref[b] * grad_comb[b]
            comb_part = both - comb_ref[b] * jnp.sum(both, axis=0, keepdims=True)
            both = disp_ref[b] * grad_disp[b]
            disp_part = both - disp_ref[b] * per_image(both, image, jnp.sum, 0.0)
            grad_logits[b] = (comb_part + disp_part).astype(bf16)
            gl_ref[b] = grad_logits[b]
        for b in pair:
            part = jnp.dot(
                grad_logits[b], x_ref[b * width : (b + 1) * width, :], preferred_element_type=f32
            )
            router_sum = part if router_sum is None else router_sum + part
    router_ref[...] = router_sum


def token_logits(back, tokens, g_outputs, dispatch, combine):
    experts, images, double = back.shape
    rows, feat = tokens.shape
    steps, _, width = dispatch.shape
    return pl.pallas_call(
        token_logits_body,
        in_specs=[IN_VMEM] + [IN_PLACE] * 4,
        out_specs=[IN_VMEM] * 3,
        out_shape=[
            jax.ShapeDtypeStruct((steps, experts, width), bf16),
            jax.ShapeDtypeStruct((steps, GROUP * experts, feat), bf16),
            jax.ShapeDtypeStruct((experts, feat), f32),
        ],
        scratch_shapes=[
            pltpu.VMEM((experts * images, double), bf16),
            pltpu.VMEM(dispatch.shape, f32),
            pltpu.VMEM(combine.shape, f32),
            pltpu.VMEM((rows, feat), bf16),
            pltpu.VMEM((rows, feat), bf16),
            pltpu.SemaphoreType.DMA((steps,)),
            pltpu.SemaphoreType.DMA((steps,)),
            pltpu.SemaphoreType.DMA((2,)),
        ],
        compiler_params=params(20),
        name="token_logits",
    )(back, *[pinned(v) for v in (tokens, g_outputs, dispatch, combine)])


def token_grads_body(gl_ref, slots_ref, disp_ref, rt_ref, out_ref):
    image = lane_images(gl_ref.shape[2])
    left = jnp.concatenate([per_slot_rows(disp_ref[0], image), gl_ref[0]], axis=0)
    right = jnp.concatenate([slots_ref[0], rt_ref[...]], axis=0)
    out_ref[...] = contract(left, right, 0, 0).astype(bf16)


def token_grads(grad_logits, slots, dispatch, rt):
    steps, experts, width = grad_logits.shape
    feat = slots.shape[2]
    return pl.pallas_call(
        token_grads_body,
        grid=(steps,),
        in_specs=[
            pl.BlockSpec((1, experts, width), lambda i: (i, 0, 0)),
            pl.BlockSpec((1, GROUP * experts, feat), lambda i: (i, 0, 0)),
            pl.BlockSpec((1, experts, width), lambda i: (i, 0, 0)),
            pl.BlockSpec((experts, feat), lambda i: (0, 0)),
        ],
        out_specs=pl.BlockSpec((width, feat), lambda i: (i, 0)),
        out_shape=jax.ShapeDtypeStruct((steps * width, feat), bf16),
        compiler_params=params(12),
        name="token_grads",
    )(grad_logits, slots, dispatch, rt)


def shift(value, axis, by, count):
    return lax.ppermute(value, axis, [(i, (i + by) % count) for i in range(count)])


def axis_sum(value, axis, count):
    return sum([shift(value, axis, by, count) for by in range(1, count)], value)


def solution(mesh):
    dp, experts = mesh.shape["dp"], mesh.shape["expert"]
    ny, nz = dp // XH, experts // 4
    fine = Mesh(
        mesh.devices.reshape(ny, XH, nz, 2, 2), ("y", "xh", "z", "xl", "core")
    )
    dp_axes = ("y", "xh")
    ex_axes = ("z", "xl", "core")

    def over_experts(value):
        return lax.all_to_all(value, ex_axes, split_axis=0, concat_axis=0, tiled=True)

    def on_device(tokens, router, w_in, w_out, g_outputs):
        rt = router.T
        slots, dispatch, combine = token_forward(tokens, rt, g_outputs)
        rows = over_experts(slots).reshape(-1, slots.shape[2])
        mid = rows.shape[0] // 2
        right = shift(rows, "y", 1, ny)
        left = shift(rows, "y", ny - 1, ny)
        results, act_own, pre_own = expert_rows(rows, w_in, w_out, ny)
        back = over_experts(results.reshape(slots.shape))
        far_a = shift(right[:mid], "y", 1, ny)
        far_b = shift(left[mid:], "y", ny - 1, ny)
        act_near, pre_near = near_terms(right, left, w_in, w_out, ny)
        back, act_near, pre_near = lax.optimization_barrier((back, act_near, pre_near))
        grad_logits, slot_grads, router_term = token_logits(
            back, tokens, g_outputs, dispatch, combine
        )
        far_a, far_b, router_term = lax.optimization_barrier((far_a, far_b, router_term))
        pieces = (rows, right, left, far_a, far_b)
        keep_in, send_in, act_far = first_grads(pieces, pre_own, pre_near, w_in, w_out, ny)
        keep_out, send_out = second_grads(pieces, (act_own, act_near, act_far))
        came_in = shift(send_in, "xh", 1, XH)
        came_out = shift(send_out, "xh", 1, XH)
        total = axis_sum(router_term, ("xh", "xl"), 2 * XH)
        total, keep_out = lax.optimization_barrier((total, keep_out))
        total = axis_sum(axis_sum(total, "core", 2), "y", ny)
        part_in = (keep_in + came_in.astype(f32)).astype(bf16)
        total, part_in, grad_logits = lax.optimization_barrier((total, part_in, grad_logits))
        spread = lax.all_to_all(part_in, "y", split_axis=0, concat_axis=0, tiled=True)
        grad_router = axis_sum(total, "z", nz).T
        grad_first, grad_second = finish(spread, keep_out, came_out)
        grad_tok = token_grads(grad_logits, slot_grads, dispatch, rt)
        return grad_tok, grad_router, grad_first, grad_second

    return jax.shard_map(
        on_device,
        mesh=fine,
        in_specs=(
            P(dp_axes + ex_axes, None),
            P(),
            P(ex_axes, None, None),
            P(ex_axes, None, None),
            P(dp_axes + ex_axes, None),
        ),
        out_specs=(
            P(dp_axes + ex_axes, None),
            P(),
            P(ex_axes, dp_axes, None),
            P(ex_axes, dp_axes, None),
        ),
        check_vma=False,
    )
```

```python
import functools

import jax
import jax.numpy as jnp
from jax import lax
from jax.experimental import pallas as pl
from jax.experimental.pallas import tpu as pltpu
from jax.sharding import Mesh, PartitionSpec as P

PATCHES = 196
GROUP = 4
XH = 2
MIB = 1024 * 1024
GELU_C = 0.7978845608028654
GELU_A = 0.044715

f32 = jnp.float32
bf16 = jnp.bfloat16


def contract(left, right, left_dim, right_dim):
    return lax.dot_general(
        left, right, (((left_dim,), (right_dim,)), ((), ())), preferred_element_type=f32
    )


def params(mib):
    return pltpu.CompilerParams(vmem_limit_bytes=mib * MIB)


def pinned(value):
    return pltpu.with_memory_space_constraint(value, pltpu.HBM)


IN_VMEM = pl.BlockSpec(memory_space=pltpu.VMEM)
IN_PLACE = pl.BlockSpec(memory_space=pltpu.HBM)


def gelu_parts(x):
    x2 = x * x
    th = jnp.tanh(GELU_C * x * (1.0 + GELU_A * x2))
    cdf = 0.5 + 0.5 * th
    slope = cdf + (0.5 * GELU_C) * x * (1.0 - th * th) * (1.0 + (3.0 * GELU_A) * x2)
    return x * cdf, slope


def lane_images(width):
    lane = lax.broadcasted_iota(jnp.int32, (1, width), 1)
    image = jnp.zeros_like(lane)
    for i in range(1, width // PATCHES):
        image = image + (lane >= i * PATCHES).astype(jnp.int32)
    return image


def per_image(values, image, reduce, start):
    width = values.shape[1]
    out = jnp.zeros_like(values)
    for i in range(GROUP):
        low = i * PATCHES // 128 * 128
        high = min(-(-(i + 1) * PATCHES // 128) * 128, width)
        part = jnp.where(image[:, low:high] == i, values[:, low:high], start)
        own = reduce(part, axis=1, keepdims=True)
        out = jnp.where(image == i, own, out)
    return out


def inverse_sum(values, axis, keepdims):
    return 1.0 / jnp.sum(values, axis=axis, keepdims=keepdims)


def per_slot_rows(weights, image):
    return jnp.concatenate(
        [jnp.where(image == i, weights, 0.0) for i in range(GROUP)], axis=0
    ).astype(bf16)


def swap_matrix(total, inner):
    outer = total // inner
    out_row = lax.broadcasted_iota(jnp.int32, (total, total), 0)
    in_row = lax.broadcasted_iota(jnp.int32, (total, total), 1)
    wanted = (out_row % outer) * inner + out_row // outer
    return (in_row == wanted).astype(f32).astype(bf16)


def block_copies(src, dst, sem):
    width = GROUP * PATCHES
    return [
        pltpu.make_async_copy(
            src.at[pl.ds(b * width, width)], dst.at[pl.ds(b * width, width)], sem.at[b]
        )
        for b in range(src.shape[0] // width)
    ]


def token_forward_body(
    rt_hbm, x_hbm, g_hbm, slots_ref, disp_hbm, comb_hbm,
    rt_ref, disp_ref, comb_ref, x_ref, g_ref, acc, x_sem, g_sem, rt_sem, disp_sem, comb_sem
):
    experts, images, double = slots_ref.shape
    feat = double // 2
    width = GROUP * PATCHES
    steps = images // GROUP
    rows = GROUP * experts
    total = experts * images

    x_copies = block_copies(x_hbm, x_ref, x_sem)
    g_copies = block_copies(g_hbm, g_ref, g_sem)
    rt_copy = pltpu.make_async_copy(rt_hbm, rt_ref, rt_sem)
    for copy in [rt_copy] + x_copies + g_copies:
        copy.start()
    weight_copies = [
        pltpu.make_async_copy(disp_ref, disp_hbm, disp_sem),
        pltpu.make_async_copy(comb_ref, comb_hbm, comb_sem),
    ]
    image = lane_images(width)
    rt_copy.wait()
    rt = rt_ref[...]
    spread = {}
    for first in range(0, steps, 2):
        pair = (first, first + 1)
        logits, own = {}, {}
        for b in pair:
            x_copies[b].wait()
        for b in pair:
            logits[b] = contract(rt, x_ref[b * width : (b + 1) * width, :], 1, 1)
        for b in pair:
            top = per_image(logits[b], image, jnp.max, -jnp.inf)
            raised = jnp.exp(logits[b] - top)
            dispatch = raised * per_image(raised, image, inverse_sum, 0.0)
            raised_e = jnp.exp(logits[b] - jnp.max(logits[b], axis=0, keepdims=True))
            combine = raised_e * inverse_sum(raised_e, axis=0, keepdims=True)
            disp_ref[b] = dispatch
            comb_ref[b] = combine
            spread[b] = per_slot_rows(combine, image)
            own[b] = per_slot_rows(dispatch, image)
        for b in pair:
            acc[b * rows : (b + 1) * rows, :feat] = jnp.dot(
                own[b], x_ref[b * width : (b + 1) * width, :], preferred_element_type=f32
            ).astype(bf16)
    for copy in weight_copies:
        copy.start()
    for b in range(steps):
        g_copies[b].wait()
    for b in range(steps):
        acc[b * rows : (b + 1) * rows, feat:] = jnp.dot(
            spread[b], g_ref[b * width : (b + 1) * width, :], preferred_element_type=f32
        ).astype(bf16)
    slots_ref[...] = (
        jnp.dot(swap_matrix(total, experts), acc[...], preferred_element_type=f32)
        .astype(bf16)
        .reshape(experts, images, double)
    )
    for copy in weight_copies:
        copy.wait()


def token_forward(tokens, rt, g_outputs):
    rows, feat = tokens.shape
    experts = rt.shape[0]
    images = rows // PATCHES
    width = GROUP * PATCHES
    steps = rows // width
    return pl.pallas_call(
        token_forward_body,
        in_specs=[IN_PLACE] * 3,
        out_specs=[IN_VMEM, IN_PLACE, IN_PLACE],
        out_shape=[
            jax.ShapeDtypeStruct((experts, images, 2 * feat), bf16),
            pltpu.HBM((steps, experts, width), f32),
            pltpu.HBM((steps, experts, width), f32),
        ],
        scratch_shapes=[
            pltpu.VMEM((experts, feat), bf16),
            pltpu.VMEM((steps, experts, width), f32),
            pltpu.VMEM((steps, experts, width), f32),
            pltpu.VMEM((rows, feat), bf16),
            pltpu.VMEM((rows, feat), bf16),
            pltpu.VMEM((experts * images, 2 * feat), bf16),
            pltpu.SemaphoreType.DMA((steps,)),
            pltpu.SemaphoreType.DMA((steps,)),
            pltpu.SemaphoreType.DMA(()),
            pltpu.SemaphoreType.DMA(()),
            pltpu.SemaphoreType.DMA(()),
        ],
        compiler_params=params(20),
        name="token_forward",
    )(pinned(rt), pinned(tokens), pinned(g_outputs))


def hidden_terms(rows, grads, w1, w2):
    act, slope = gelu_parts(jnp.dot(rows, w1, preferred_element_type=f32))
    return act.astype(bf16), (contract(grads, w2, 1, 1) * slope).astype(bf16)


def expert_body(
    rows_ref, w1_ref, w2_ref, out_hbm, act_hbm, pre_hbm, out_ref, act_ref, pre_ref, sem
):
    feat = w1_ref.shape[1]
    hidden = w1_ref.shape[2]
    tile = act_ref.shape[1]
    part_at = lax.axis_index("y")
    rows = rows_ref[:, :feat]
    grads = rows_ref[:, feat:]
    made, back = None, None
    stores = [
        pltpu.make_async_copy(src, dst, sem.at[k])
        for k, (src, dst) in enumerate(
            (
                (act_ref, act_hbm),
                (pre_ref, pre_hbm),
                (out_ref.at[:, pl.ds(0, feat)], out_hbm.at[:, pl.ds(0, feat)]),
                (out_ref.at[:, pl.ds(feat, feat)], out_hbm.at[:, pl.ds(feat, feat)]),
            )
        )
    ]
    for i in range(hidden // tile):
        w1 = w1_ref[0, :, i * tile : (i + 1) * tile]
        w2 = w2_ref[0, i * tile : (i + 1) * tile, :]
        act, grad_pre = hidden_terms(rows, grads, w1, w2)

        @pl.when(part_at == i)
        def _():
            act_ref[...] = act
            pre_ref[...] = grad_pre

        if i == hidden // tile - 1:
            stores[0].start()
            stores[1].start()
        part = jnp.dot(act, w2, preferred_element_type=f32)
        made = part if made is None else made + part
        if i == hidden // tile - 1:
            out_ref[:, :feat] = made.astype(bf16)
            stores[2].start()
        part = contract(grad_pre, w1, 1, 1)
        back = part if back is None else back + part
    out_ref[:, feat:] = back.astype(bf16)
    stores[3].start()
    for store in stores:
        store.wait()


def expert_rows(rows, w_in, w_out, parts):
    tile = w_in.shape[2] // parts
    shapes = [rows.shape, (rows.shape[0], tile), (rows.shape[0], tile)]
    return pl.pallas_call(
        expert_body,
        in_specs=[IN_VMEM] * 3,
        out_specs=[IN_PLACE] * 3,
        out_shape=[pltpu.HBM(shape, bf16) for shape in shapes],
        scratch_shapes=[pltpu.VMEM(shape, bf16) for shape in shapes]
        + [pltpu.SemaphoreType.DMA((4,))],
        compiler_params=params(12),
        name="expert_rows",
    )(rows, w_in, w_out)


def slice_copies(w1_hbm, w2_hbm, w1, w2, sem):
    tile = w1.shape[1]
    low = pl.multiple_of(lax.axis_index("y") * tile, tile)
    return (
        pltpu.make_async_copy(w1_hbm.at[0, :, pl.ds(low, tile)], w1, sem.at[0]),
        pltpu.make_async_copy(w2_hbm.at[0, pl.ds(low, tile), :], w2, sem.at[1]),
    )


def stacked_copies(sources, out, sem):
    copies, at = [], 0
    for k, source in enumerate(sources):
        rows = source.shape[0]
        copies.append(pltpu.make_async_copy(source, out.at[pl.ds(at, rows)], sem.at[k]))
        at += rows
    return copies


def join(pieces, low, high, out):
    at = 0
    for piece in pieces:
        out[at : at + piece.shape[0], :] = piece[:, low:high]
        at += piece.shape[0]


def near_terms_body(
    right_ref, left_ref, w1_hbm, w2_hbm, act_hbm, pre_hbm, act, pre, both, w1, w2, sem, out_sem
):
    feat = w1.shape[0]
    loads = slice_copies(w1_hbm, w2_hbm, w1, w2, sem)
    for load in loads:
        load.start()
    join((right_ref, left_ref), 0, 2 * feat, both)
    for load in loads:
        load.wait()
    act[...], pre[...] = hidden_terms(both[:, :feat], both[:, feat:], w1[...], w2[...])
    stores = (
        pltpu.make_async_copy(act, act_hbm, out_sem.at[0]),
        pltpu.make_async_copy(pre, pre_hbm, out_sem.at[1]),
    )
    for store in stores:
        store.start()
    for store in stores:
        store.wait()


def near_terms(right, left, w_in, w_out, parts):
    feat, hidden = w_in.shape[1:]
    tile = hidden // parts
    count = right.shape[0] + left.shape[0]
    return pl.pallas_call(
        near_terms_body,
        in_specs=[IN_VMEM] * 2 + [IN_PLACE] * 2,
        out_specs=[IN_PLACE] * 2,
        out_shape=[pltpu.HBM((count, tile), bf16)] * 2,
        scratch_shapes=[
            pltpu.VMEM((count, tile), bf16),
            pltpu.VMEM((count, tile), bf16),
            pltpu.VMEM((count, 2 * feat), bf16),
            pltpu.VMEM((feat, tile), bf16),
            pltpu.VMEM((tile, feat), bf16),
            pltpu.SemaphoreType.DMA((2,)),
            pltpu.SemaphoreType.DMA((2,)),
        ],
        compiler_params=params(16),
        name="near_terms",
    )(right, left, pinned(w_in), pinned(w_out))


def first_grads_body(
    own_ref, right_ref, left_ref, far_a, far_b, pre_own, pre_near, w1_hbm, w2_hbm,
    keep_ref, send_ref, act_far, rows, pre, far, w1, w2, sem, pre_sem
):
    feat = w1.shape[0]
    xh = lax.axis_index("xh")
    loads = slice_copies(w1_hbm, w2_hbm, w1, w2, sem)
    terms = stacked_copies((pre_own, pre_near), pre, pre_sem)
    for load in terms + list(loads):
        load.start()
    join((own_ref, right_ref, left_ref), 0, feat, rows)
    join((far_a, far_b), 0, 2 * feat, far)
    for load in terms:
        load.wait()
    total = contract(rows[...], pre[...], 0, 0)
    for load in loads:
        load.wait()
    act, pre_far = hidden_terms(far[:, :feat], far[:, feat:], w1[...], w2[...])
    act_far[...] = act
    total = total + contract(far[:, :feat], pre_far, 0, 0)
    parts, own, _ = keep_ref.shape
    for i in range(parts):
        low = total[XH * i * own : (XH * i + 1) * own]
        high = total[(XH * i + 1) * own : XH * (i + 1) * own]
        send_ref[i] = jnp.where(xh == 0, high, low).astype(bf16)
        keep_ref[i] = jnp.where(xh == 0, low, high)


def first_grads(pieces, pre_own, pre_near, w_in, w_out, parts):
    feat, hidden = w_in.shape[1:]
    tile = hidden // parts
    own = feat // (parts * XH)
    near_count = sum(p.shape[0] for p in pieces[:3])
    far_count = sum(p.shape[0] for p in pieces[3:])
    return pl.pallas_call(
        first_grads_body,
        in_specs=[IN_VMEM] * 5 + [IN_PLACE] * 4,
        out_specs=[IN_VMEM] * 3,
        out_shape=[
            jax.ShapeDtypeStruct((parts, own, tile), f32),
            jax.ShapeDtypeStruct((parts, own, tile), bf16),
            jax.ShapeDtypeStruct((far_count, tile), bf16),
        ],
        scratch_shapes=[
            pltpu.VMEM((near_count, feat), bf16),
            pltpu.VMEM((near_count, tile), bf16),
            pltpu.VMEM((far_count, 2 * feat), bf16),
            pltpu.VMEM((feat, tile), bf16),
            pltpu.VMEM((tile, feat), bf16),
            pltpu.SemaphoreType.DMA((2,)),
            pltpu.SemaphoreType.DMA((2,)),
        ],
        compiler_params=params(20),
        name="first_grads",
    )(*pieces, pinned(pre_own), pinned(pre_near), pinned(w_in), pinned(w_out))


def second_grads_body(
    own_ref, right_ref, left_ref, far_a, far_b, act_own, act_near, act_far,
    keep_ref, send_ref, grads, act, sem
):
    feat = grads.shape[1]
    tile = keep_ref.shape[0]
    xh = lax.axis_index("xh")
    terms = stacked_copies((act_own, act_near), act, sem)
    for load in terms:
        load.start()
    join((own_ref, right_ref, left_ref, far_a, far_b), feat, 2 * feat, grads)
    act[act.shape[0] - act_far.shape[0] :, :] = act_far[...]
    for load in terms:
        load.wait()

    def rows_of(part):
        low = pl.multiple_of(part * tile, tile)
        return contract(act[:, pl.ds(low, tile)], grads[...], 0, 0)

    send_ref[...] = rows_of(1 - xh).astype(bf16)
    keep_ref[...] = rows_of(xh)


def second_grads(pieces, acts):
    feat = pieces[0].shape[1] // 2
    count = sum(p.shape[0] for p in pieces)
    width = acts[0].shape[1]
    tile = width // XH
    return pl.pallas_call(
        second_grads_body,
        in_specs=[IN_VMEM] * 5 + [IN_PLACE] * 2 + [IN_VMEM],
        out_specs=[IN_VMEM] * 2,
        out_shape=[
            jax.ShapeDtypeStruct((tile, feat), f32),
            jax.ShapeDtypeStruct((tile, feat), bf16),
        ],
        scratch_shapes=[
            pltpu.VMEM((count, feat), bf16),
            pltpu.VMEM((count, width), bf16),
            pltpu.SemaphoreType.DMA((2,)),
        ],
        compiler_params=params(12),
        name="second_grads",
    )(*pieces, pinned(acts[0]), pinned(acts[1]), acts[2])


def finish_body(spread_ref, keep_ref, came_ref, first_ref, second_ref):
    parts, _, tile = spread_ref.shape
    for i in range(parts):
        first_ref[0, :, i * tile : (i + 1) * tile] = spread_ref[i].astype(f32)
    second_ref[0] = keep_ref[...] + came_ref[...].astype(f32)


def finish(spread, keep, came):
    parts, own, tile = spread.shape
    return pl.pallas_call(
        finish_body,
        in_specs=[IN_VMEM] * 3,
        out_specs=[IN_VMEM] * 2,
        out_shape=[
            jax.ShapeDtypeStruct((1, own, parts * tile), f32),
            jax.ShapeDtypeStruct((1,) + keep.shape, f32),
        ],
        compiler_params=params(8),
        name="finish",
    )(spread, keep, came)


def token_logits_body(
    back_ref, x_hbm, g_hbm, disp_hbm, comb_hbm, gl_ref, slots_ref, router_ref,
    mix, disp_ref, comb_ref, x_ref, g_ref, x_sem, g_sem, weight_sem
):
    experts, images, double = back_ref.shape
    feat = double // 2
    width = GROUP * PATCHES
    rows = GROUP * experts
    total = experts * images
    x_copies = block_copies(x_hbm, x_ref, x_sem)
    g_copies = block_copies(g_hbm, g_ref, g_sem)
    for x_copy, g_copy in zip(x_copies, g_copies):
        g_copy.start()
        x_copy.start()
    weight_copies = [
        pltpu.make_async_copy(disp_hbm, disp_ref, weight_sem.at[0]),
        pltpu.make_async_copy(comb_hbm, comb_ref, weight_sem.at[1]),
    ]
    for copy in weight_copies:
        copy.start()
    mix[...] = jnp.dot(
        swap_matrix(total, images),
        back_ref[...].reshape(total, double),
        preferred_element_type=f32,
    ).astype(bf16)
    image = lane_images(width)

    def picked(both):
        out = both[:experts]
        for i in range(1, GROUP):
            out = jnp.where(image == i, both[i * experts : (i + 1) * experts], out)
        return out

    for copy in weight_copies:
        copy.wait()
    router_sum = None
    for first in range(0, images // GROUP, 2):
        pair = (first, first + 1)
        grad_comb, grad_disp, grad_logits = {}, {}, {}
        for b in pair:
            g_copies[b].wait()
            x_copies[b].wait()
        for b in pair:
            block = mix[b * rows : (b + 1) * rows, :]
            slots_ref[b] = block[:, feat:]
            g = g_ref[b * width : (b + 1) * width, :]
            grad_comb[b] = picked(contract(block[:, :feat], g, 1, 1))
            x = x_ref[b * width : (b + 1) * width, :]
            grad_disp[b] = picked(contract(block[:, feat:], x, 1, 1))
        for b in pair:
            both = comb_ref[b] * grad_comb[b]
            comb_part = both - comb_ref[b] * jnp.sum(both, axis=0, keepdims=True)
            both = disp_ref[b] * grad_disp[b]
            disp_part = both - disp_ref[b] * per_image(both, image, jnp.sum, 0.0)
            grad_logits[b] = (comb_part + disp_part).astype(bf16)
            gl_ref[b] = grad_logits[b]
        for b in pair:
            part = jnp.dot(
                grad_logits[b], x_ref[b * width : (b + 1) * width, :], preferred_element_type=f32
            )
            router_sum = part if router_sum is None else router_sum + part
    router_ref[...] = router_sum


def token_logits(back, tokens, g_outputs, dispatch, combine):
    experts, images, double = back.shape
    rows, feat = tokens.shape
    steps, _, width = dispatch.shape
    return pl.pallas_call(
        token_logits_body,
        in_specs=[IN_VMEM] + [IN_PLACE] * 4,
        out_specs=[IN_VMEM] * 3,
        out_shape=[
            jax.ShapeDtypeStruct((steps, experts, width), bf16),
            jax.ShapeDtypeStruct((steps, GROUP * experts, feat), bf16),
            jax.ShapeDtypeStruct((experts, feat), f32),
        ],
        scratch_shapes=[
            pltpu.VMEM((experts * images, double), bf16),
            pltpu.VMEM(dispatch.shape, f32),
            pltpu.VMEM(combine.shape, f32),
            pltpu.VMEM((rows, feat), bf16),
            pltpu.VMEM((rows, feat), bf16),
            pltpu.SemaphoreType.DMA((steps,)),
            pltpu.SemaphoreType.DMA((steps,)),
            pltpu.SemaphoreType.DMA((2,)),
        ],
        compiler_params=params(20),
        name="token_logits",
    )(back, *[pinned(v) for v in (tokens, g_outputs, dispatch, combine)])


def token_grads_body(gl_ref, slots_ref, disp_ref, rt_ref, out_hbm, out, sem):
    steps, _, width = gl_ref.shape
    image = lane_images(width)
    stores = []
    for b in range(steps):
        left = jnp.concatenate([per_slot_rows(disp_ref[b], image), gl_ref[b]], axis=0)
        right = jnp.concatenate([slots_ref[b], rt_ref[...]], axis=0)
        out[b * width : (b + 1) * width, :] = contract(left, right, 0, 0).astype(bf16)
        at = pl.ds(b * width, width)
        stores.append(pltpu.make_async_copy(out.at[at], out_hbm.at[at], sem.at[b]))
        stores[b].start()
    for store in stores:
        store.wait()


def token_grads(grad_logits, slots, dispatch, rt):
    steps, _, width = grad_logits.shape
    shape = (steps * width, slots.shape[2])
    return pl.pallas_call(
        token_grads_body,
        in_specs=[IN_VMEM] * 4,
        out_specs=IN_PLACE,
        out_shape=pltpu.HBM(shape, bf16),
        scratch_shapes=[pltpu.VMEM(shape, bf16), pltpu.SemaphoreType.DMA((steps,))],
        compiler_params=params(12),
        name="token_grads",
    )(grad_logits, slots, dispatch, rt)


def shift(value, axis, by, count):
    return lax.ppermute(value, axis, [(i, (i + by) % count) for i in range(count)])


def axis_sum(value, axis, count):
    return sum([shift(value, axis, by, count) for by in range(1, count)], value)


def solution(mesh):
    dp, experts = mesh.shape["dp"], mesh.shape["expert"]
    ny, nz = dp // XH, experts // 4
    fine = Mesh(
        mesh.devices.reshape(ny, XH, nz, 2, 2), ("y", "xh", "z", "xl", "core")
    )
    dp_axes = ("y", "xh")
    ex_axes = ("z", "xl", "core")

    def over_experts(value):
        return lax.all_to_all(value, ex_axes, split_axis=0, concat_axis=0, tiled=True)

    def on_device(tokens, router, w_in, w_out, g_outputs):
        rt = router.T
        slots, dispatch, combine = token_forward(tokens, rt, g_outputs)
        rows = over_experts(slots).reshape(-1, slots.shape[2])
        mid = rows.shape[0] // 2
        right = shift(rows, "y", 1, ny)
        left = shift(rows, "y", ny - 1, ny)
        results, act_own, pre_own = expert_rows(rows, w_in, w_out, ny)
        back = over_experts(results.reshape(slots.shape))
        far_a = shift(right[:mid], "y", 1, ny)
        far_b = shift(left[mid:], "y", ny - 1, ny)
        act_near, pre_near = near_terms(right, left, w_in, w_out, ny)
        back, act_near, pre_near = lax.optimization_barrier((back, act_near, pre_near))
        grad_logits, slot_grads, router_term = token_logits(
            back, tokens, g_outputs, dispatch, combine
        )
        far_a, far_b, router_term = lax.optimization_barrier((far_a, far_b, router_term))
        pieces = (rows, right, left, far_a, far_b)
        keep_in, send_in, act_far = first_grads(pieces, pre_own, pre_near, w_in, w_out, ny)
        keep_out, send_out = second_grads(pieces, (act_own, act_near, act_far))
        came_in = shift(send_in, "xh", 1, XH)
        came_out = shift(send_out, "xh", 1, XH)
        total = axis_sum(router_term, ("xh", "xl"), 2 * XH)
        total, keep_out = lax.optimization_barrier((total, keep_out))
        total = axis_sum(axis_sum(total, "core", 2), "y", ny)
        part_in = (keep_in + came_in.astype(f32)).astype(bf16)
        grad_tok = token_grads(grad_logits, slot_grads, dispatch, rt)
        total, part_in, grad_tok = lax.optimization_barrier((total, part_in, grad_tok))
        spread = lax.all_to_all(part_in, "y", split_axis=0, concat_axis=0, tiled=True)
        grad_router = axis_sum(total, "z", nz).T
        grad_first, grad_second = finish(spread, keep_out, came_out)
        return grad_tok, grad_router, grad_first, grad_second

    return jax.shard_map(
        on_device,
        mesh=fine,
        in_specs=(
            P(dp_axes + ex_axes, None),
            P(),
            P(ex_axes, None, None),
            P(ex_axes, None, None),
            P(dp_axes + ex_axes, None),
        ),
        out_specs=(
            P(dp_axes + ex_axes, None),
            P(),
            P(ex_axes, dp_axes, None),
            P(ex_axes, dp_axes, None),
        ),
        check_vma=False,
    )
```

```python
import functools

import jax
import jax.numpy as jnp
from jax import lax
from jax.experimental import pallas as pl
from jax.experimental.pallas import tpu as pltpu
from jax.sharding import Mesh, PartitionSpec as P

PATCHES = 196
GROUP = 4
XH = 2
MIB = 1024 * 1024
GELU_C = 0.7978845608028654
GELU_A = 0.044715

f32 = jnp.float32
bf16 = jnp.bfloat16


def contract(left, right, left_dim, right_dim):
    return lax.dot_general(
        left, right, (((left_dim,), (right_dim,)), ((), ())), preferred_element_type=f32
    )


def params(mib):
    return pltpu.CompilerParams(vmem_limit_bytes=mib * MIB)


def pinned(value):
    return pltpu.with_memory_space_constraint(value, pltpu.HBM)


IN_VMEM = pl.BlockSpec(memory_space=pltpu.VMEM)
IN_PLACE = pl.BlockSpec(memory_space=pltpu.HBM)


def gelu_parts(x):
    x2 = x * x
    th = jnp.tanh(GELU_C * x * (1.0 + GELU_A * x2))
    cdf = 0.5 + 0.5 * th
    slope = cdf + (0.5 * GELU_C) * x * (1.0 - th * th) * (1.0 + (3.0 * GELU_A) * x2)
    return x * cdf, slope


def lane_images(width):
    lane = lax.broadcasted_iota(jnp.int32, (1, width), 1)
    image = jnp.zeros_like(lane)
    for i in range(1, width // PATCHES):
        image = image + (lane >= i * PATCHES).astype(jnp.int32)
    return image


def per_image(values, image, reduce, start):
    width = values.shape[1]
    out = jnp.zeros_like(values)
    for i in range(GROUP):
        low = i * PATCHES // 128 * 128
        high = min(-(-(i + 1) * PATCHES // 128) * 128, width)
        part = jnp.where(image[:, low:high] == i, values[:, low:high], start)
        own = reduce(part, axis=1, keepdims=True)
        out = jnp.where(image == i, own, out)
    return out


def inverse_sum(values, axis, keepdims):
    return 1.0 / jnp.sum(values, axis=axis, keepdims=keepdims)


def per_slot_rows(weights, image):
    return jnp.concatenate(
        [jnp.where(image == i, weights, 0.0) for i in range(GROUP)], axis=0
    ).astype(bf16)


def swap_matrix(total, inner):
    outer = total // inner
    out_row = lax.broadcasted_iota(jnp.int32, (total, total), 0)
    in_row = lax.broadcasted_iota(jnp.int32, (total, total), 1)
    wanted = (out_row % outer) * inner + out_row // outer
    return (in_row == wanted).astype(f32).astype(bf16)


def block_copies(src, dst, sem):
    width = GROUP * PATCHES
    return [
        pltpu.make_async_copy(
            src.at[pl.ds(b * width, width)], dst.at[pl.ds(b * width, width)], sem.at[b]
        )
        for b in range(src.shape[0] // width)
    ]


def token_forward_body(
    rt_hbm, x_hbm, g_hbm, slots_ref, disp_hbm, comb_hbm,
    rt_ref, disp_ref, comb_ref, x_ref, g_ref, acc, x_sem, g_sem, rt_sem, disp_sem, comb_sem
):
    experts, images, double = slots_ref.shape
    feat = double // 2
    width = GROUP * PATCHES
    steps = images // GROUP
    rows = GROUP * experts
    total = experts * images

    x_copies = block_copies(x_hbm, x_ref, x_sem)
    g_copies = block_copies(g_hbm, g_ref, g_sem)
    rt_copy = pltpu.make_async_copy(rt_hbm, rt_ref, rt_sem)
    for copy in [rt_copy] + x_copies + g_copies:
        copy.start()
    weight_copies = [
        pltpu.make_async_copy(disp_ref, disp_hbm, disp_sem),
        pltpu.make_async_copy(comb_ref, comb_hbm, comb_sem),
    ]
    image = lane_images(width)
    rt_copy.wait()
    rt = rt_ref[...]
    spread = {}
    for first in range(0, steps, 2):
        pair = (first, first + 1)
        logits, own = {}, {}
        for b in pair:
            x_copies[b].wait()
        for b in pair:
            logits[b] = contract(rt, x_ref[b * width : (b + 1) * width, :], 1, 1)
        for b in pair:
            top = per_image(logits[b], image, jnp.max, -jnp.inf)
            raised = jnp.exp(logits[b] - top)
            dispatch = raised * per_image(raised, image, inverse_sum, 0.0)
            raised_e = jnp.exp(logits[b] - jnp.max(logits[b], axis=0, keepdims=True))
            combine = raised_e * inverse_sum(raised_e, axis=0, keepdims=True)
            disp_ref[b] = dispatch
            comb_ref[b] = combine
            spread[b] = per_slot_rows(combine, image)
            own[b] = per_slot_rows(dispatch, image)
        for b in pair:
            acc[b * rows : (b + 1) * rows, :feat] = jnp.dot(
                own[b], x_ref[b * width : (b + 1) * width, :], preferred_element_type=f32
            ).astype(bf16)
    for copy in weight_copies:
        copy.start()
    for b in range(steps):
        g_copies[b].wait()
    for b in range(steps):
        acc[b * rows : (b + 1) * rows, feat:] = jnp.dot(
            spread[b], g_ref[b * width : (b + 1) * width, :], preferred_element_type=f32
        ).astype(bf16)
    slots_ref[...] = (
        jnp.dot(swap_matrix(total, experts), acc[...], preferred_element_type=f32)
        .astype(bf16)
        .reshape(experts, images, double)
    )
    for copy in weight_copies:
        copy.wait()


def token_forward(tokens, rt, g_outputs):
    rows, feat = tokens.shape
    experts = rt.shape[0]
    images = rows // PATCHES
    width = GROUP * PATCHES
    steps = rows // width
    return pl.pallas_call(
        token_forward_body,
        in_specs=[IN_PLACE] * 3,
        out_specs=[IN_VMEM, IN_PLACE, IN_PLACE],
        out_shape=[
            jax.ShapeDtypeStruct((experts, images, 2 * feat), bf16),
            pltpu.HBM((steps, experts, width), f32),
            pltpu.HBM((steps, experts, width), f32),
        ],
        scratch_shapes=[
            pltpu.VMEM((experts, feat), bf16),
            pltpu.VMEM((steps, experts, width), f32),
            pltpu.VMEM((steps, experts, width), f32),
            pltpu.VMEM((rows, feat), bf16),
            pltpu.VMEM((rows, feat), bf16),
            pltpu.VMEM((experts * images, 2 * feat), bf16),
            pltpu.SemaphoreType.DMA((steps,)),
            pltpu.SemaphoreType.DMA((steps,)),
            pltpu.SemaphoreType.DMA(()),
            pltpu.SemaphoreType.DMA(()),
            pltpu.SemaphoreType.DMA(()),
        ],
        compiler_params=params(20),
        name="token_forward",
    )(pinned(rt), pinned(tokens), pinned(g_outputs))


def hidden_terms(rows, grads, w1, w2):
    act, slope = gelu_parts(jnp.dot(rows, w1, preferred_element_type=f32))
    return act.astype(bf16), (contract(grads, w2, 1, 1) * slope).astype(bf16)


def expert_body(
    rows_ref, w1_ref, w2_ref, out_hbm, act_hbm, pre_hbm, out_ref, act_ref, pre_ref, sem
):
    feat = w1_ref.shape[1]
    hidden = w1_ref.shape[2]
    tile = act_ref.shape[1]
    part_at = lax.axis_index("y")
    rows = rows_ref[:, :feat]
    grads = rows_ref[:, feat:]
    made, back = None, None
    stores = [
        pltpu.make_async_copy(src, dst, sem.at[k])
        for k, (src, dst) in enumerate(
            (
                (act_ref, act_hbm),
                (pre_ref, pre_hbm),
                (out_ref.at[:, pl.ds(0, feat)], out_hbm.at[:, pl.ds(0, feat)]),
                (out_ref.at[:, pl.ds(feat, feat)], out_hbm.at[:, pl.ds(feat, feat)]),
            )
        )
    ]
    for i in range(hidden // tile):
        w1 = w1_ref[0, :, i * tile : (i + 1) * tile]
        w2 = w2_ref[0, i * tile : (i + 1) * tile, :]
        act, grad_pre = hidden_terms(rows, grads, w1, w2)

        @pl.when(part_at == i)
        def _():
            act_ref[...] = act
            pre_ref[...] = grad_pre

        if i == hidden // tile - 1:
            stores[0].start()
            stores[1].start()
        part = jnp.dot(act, w2, preferred_element_type=f32)
        made = part if made is None else made + part
        if i == hidden // tile - 1:
            out_ref[:, :feat] = made.astype(bf16)
            stores[2].start()
        part = contract(grad_pre, w1, 1, 1)
        back = part if back is None else back + part
    out_ref[:, feat:] = back.astype(bf16)
    stores[3].start()
    for store in stores:
        store.wait()


def expert_rows(rows, w_in, w_out, parts):
    tile = w_in.shape[2] // parts
    shapes = [rows.shape, (rows.shape[0], tile), (rows.shape[0], tile)]
    return pl.pallas_call(
        expert_body,
        in_specs=[IN_VMEM] * 3,
        out_specs=[IN_PLACE] * 3,
        out_shape=[pltpu.HBM(shape, bf16) for shape in shapes],
        scratch_shapes=[pltpu.VMEM(shape, bf16) for shape in shapes]
        + [pltpu.SemaphoreType.DMA((4,))],
        compiler_params=params(12),
        name="expert_rows",
    )(rows, w_in, w_out)


def slice_copies(w1_hbm, w2_hbm, w1, w2, sem):
    tile = w1.shape[1]
    low = pl.multiple_of(lax.axis_index("y") * tile, tile)
    return (
        pltpu.make_async_copy(w1_hbm.at[0, :, pl.ds(low, tile)], w1, sem.at[0]),
        pltpu.make_async_copy(w2_hbm.at[0, pl.ds(low, tile), :], w2, sem.at[1]),
    )


def stacked_copies(sources, out, sem):
    copies, at = [], 0
    for k, source in enumerate(sources):
        rows = source.shape[0]
        copies.append(pltpu.make_async_copy(source, out.at[pl.ds(at, rows)], sem.at[k]))
        at += rows
    return copies


def join(pieces, low, high, out):
    at = 0
    for piece in pieces:
        out[at : at + piece.shape[0], :] = piece[:, low:high]
        at += piece.shape[0]


def near_terms_body(
    right_ref, left_ref, w1_hbm, w2_hbm, act_hbm, pre_hbm, act, pre, both, w1, w2, sem, out_sem
):
    feat = w1.shape[0]
    loads = slice_copies(w1_hbm, w2_hbm, w1, w2, sem)
    for load in loads:
        load.start()
    join((right_ref, left_ref), 0, 2 * feat, both)
    for load in loads:
        load.wait()
    act[...], pre[...] = hidden_terms(both[:, :feat], both[:, feat:], w1[...], w2[...])
    stores = (
        pltpu.make_async_copy(act, act_hbm, out_sem.at[0]),
        pltpu.make_async_copy(pre, pre_hbm, out_sem.at[1]),
    )
    for store in stores:
        store.start()
    for store in stores:
        store.wait()


def near_terms(right, left, w_in, w_out, parts):
    feat, hidden = w_in.shape[1:]
    tile = hidden // parts
    count = right.shape[0] + left.shape[0]
    return pl.pallas_call(
        near_terms_body,
        in_specs=[IN_VMEM] * 2 + [IN_PLACE] * 2,
        out_specs=[IN_PLACE] * 2,
        out_shape=[pltpu.HBM((count, tile), bf16)] * 2,
        scratch_shapes=[
            pltpu.VMEM((count, tile), bf16),
            pltpu.VMEM((count, tile), bf16),
            pltpu.VMEM((count, 2 * feat), bf16),
            pltpu.VMEM((feat, tile), bf16),
            pltpu.VMEM((tile, feat), bf16),
            pltpu.SemaphoreType.DMA((2,)),
            pltpu.SemaphoreType.DMA((2,)),
        ],
        compiler_params=params(16),
        name="near_terms",
    )(right, left, pinned(w_in), pinned(w_out))


def first_grads_body(
    own_ref, right_ref, left_ref, far_a, far_b, pre_own, pre_near, w1_hbm, w2_hbm,
    keep_ref, send_ref, act_far, rows, pre, far, w1, w2, sem, pre_sem
):
    feat = w1.shape[0]
    xh = lax.axis_index("xh")
    loads = slice_copies(w1_hbm, w2_hbm, w1, w2, sem)
    terms = stacked_copies((pre_own, pre_near), pre, pre_sem)
    for load in terms + list(loads):
        load.start()
    join((own_ref, right_ref, left_ref), 0, feat, rows)
    join((far_a, far_b), 0, 2 * feat, far)
    for load in terms:
        load.wait()
    total = contract(rows[...], pre[...], 0, 0)
    for load in loads:
        load.wait()
    act, pre_far = hidden_terms(far[:, :feat], far[:, feat:], w1[...], w2[...])
    act_far[...] = act
    total = total + contract(far[:, :feat], pre_far, 0, 0)
    parts, own, _ = keep_ref.shape
    for i in range(parts):
        low = total[XH * i * own : (XH * i + 1) * own]
        high = total[(XH * i + 1) * own : XH * (i + 1) * own]
        send_ref[i] = jnp.where(xh == 0, high, low).astype(bf16)
        keep_ref[i] = jnp.where(xh == 0, low, high)


def first_grads(pieces, pre_own, pre_near, w_in, w_out, parts):
    feat, hidden = w_in.shape[1:]
    tile = hidden // parts
    own = feat // (parts * XH)
    near_count = sum(p.shape[0] for p in pieces[:3])
    far_count = sum(p.shape[0] for p in pieces[3:])
    return pl.pallas_call(
        first_grads_body,
        in_specs=[IN_VMEM] * 5 + [IN_PLACE] * 4,
        out_specs=[IN_VMEM] * 3,
        out_shape=[
            jax.ShapeDtypeStruct((parts, own, tile), f32),
            jax.ShapeDtypeStruct((parts, own, tile), bf16),
            jax.ShapeDtypeStruct((far_count, tile), bf16),
        ],
        scratch_shapes=[
            pltpu.VMEM((near_count, feat), bf16),
            pltpu.VMEM((near_count, tile), bf16),
            pltpu.VMEM((far_count, 2 * feat), bf16),
            pltpu.VMEM((feat, tile), bf16),
            pltpu.VMEM((tile, feat), bf16),
            pltpu.SemaphoreType.DMA((2,)),
            pltpu.SemaphoreType.DMA((2,)),
        ],
        compiler_params=params(20),
        name="first_grads",
    )(*pieces, pinned(pre_own), pinned(pre_near), pinned(w_in), pinned(w_out))


def second_grads_body(
    own_ref, right_ref, left_ref, far_a, far_b, act_own, act_near, act_far,
    keep_ref, send_ref, grads, act, sem
):
    feat = grads.shape[1]
    tile = keep_ref.shape[0]
    xh = lax.axis_index("xh")
    terms = stacked_copies((act_own, act_near), act, sem)
    for load in terms:
        load.start()
    join((own_ref, right_ref, left_ref, far_a, far_b), feat, 2 * feat, grads)
    act[act.shape[0] - act_far.shape[0] :, :] = act_far[...]
    for load in terms:
        load.wait()

    def rows_of(part):
        low = pl.multiple_of(part * tile, tile)
        return contract(act[:, pl.ds(low, tile)], grads[...], 0, 0)

    send_ref[...] = rows_of(1 - xh).astype(bf16)
    keep_ref[...] = rows_of(xh)


def second_grads(pieces, acts):
    feat = pieces[0].shape[1] // 2
    count = sum(p.shape[0] for p in pieces)
    width = acts[0].shape[1]
    tile = width // XH
    return pl.pallas_call(
        second_grads_body,
        in_specs=[IN_VMEM] * 5 + [IN_PLACE] * 2 + [IN_VMEM],
        out_specs=[IN_VMEM] * 2,
        out_shape=[
            jax.ShapeDtypeStruct((tile, feat), f32),
            jax.ShapeDtypeStruct((tile, feat), bf16),
        ],
        scratch_shapes=[
            pltpu.VMEM((count, feat), bf16),
            pltpu.VMEM((count, width), bf16),
            pltpu.SemaphoreType.DMA((2,)),
        ],
        compiler_params=params(12),
        name="second_grads",
    )(*pieces, pinned(acts[0]), pinned(acts[1]), acts[2])


def finish_body(spread_ref, keep_ref, came_ref, first_ref, second_ref):
    parts, _, tile = spread_ref.shape
    for i in range(parts):
        first_ref[0, :, i * tile : (i + 1) * tile] = spread_ref[i].astype(f32)
    second_ref[0] = keep_ref[...] + came_ref[...].astype(f32)


def finish(spread, keep, came):
    parts, own, tile = spread.shape
    return pl.pallas_call(
        finish_body,
        in_specs=[IN_VMEM] * 3,
        out_specs=[IN_VMEM] * 2,
        out_shape=[
            jax.ShapeDtypeStruct((1, own, parts * tile), f32),
            jax.ShapeDtypeStruct((1,) + keep.shape, f32),
        ],
        compiler_params=params(8),
        name="finish",
    )(spread, keep, came)


def token_logits_body(
    back_ref, x_hbm, g_hbm, disp_hbm, comb_hbm, gl_ref, slots_ref, router_ref,
    mix, disp_ref, comb_ref, x_ref, g_ref, x_sem, g_sem, weight_sem
):
    experts, images, double = back_ref.shape
    feat = double // 2
    width = GROUP * PATCHES
    rows = GROUP * experts
    total = experts * images
    x_copies = block_copies(x_hbm, x_ref, x_sem)
    g_copies = block_copies(g_hbm, g_ref, g_sem)
    for x_copy, g_copy in zip(x_copies, g_copies):
        g_copy.start()
        x_copy.start()
    weight_copies = [
        pltpu.make_async_copy(disp_hbm, disp_ref, weight_sem.at[0]),
        pltpu.make_async_copy(comb_hbm, comb_ref, weight_sem.at[1]),
    ]
    for copy in weight_copies:
        copy.start()
    mix[...] = jnp.dot(
        swap_matrix(total, images),
        back_ref[...].reshape(total, double),
        preferred_element_type=f32,
    ).astype(bf16)
    image = lane_images(width)

    def picked(both):
        out = both[:experts]
        for i in range(1, GROUP):
            out = jnp.where(image == i, both[i * experts : (i + 1) * experts], out)
        return out

    for copy in weight_copies:
        copy.wait()
    router_sum = None
    for first in range(0, images // GROUP, 2):
        pair = (first, first + 1)
        grad_comb, grad_disp, grad_logits = {}, {}, {}
        for b in pair:
            g_copies[b].wait()
            x_copies[b].wait()
        for b in pair:
            block = mix[b * rows : (b + 1) * rows, :]
            slots_ref[b] = block[:, feat:]
            g = g_ref[b * width : (b + 1) * width, :]
            grad_comb[b] = picked(contract(block[:, :feat], g, 1, 1))
            x = x_ref[b * width : (b + 1) * width, :]
            grad_disp[b] = picked(contract(block[:, feat:], x, 1, 1))
        for b in pair:
            both = comb_ref[b] * grad_comb[b]
            comb_part = both - comb_ref[b] * jnp.sum(both, axis=0, keepdims=True)
            both = disp_ref[b] * grad_disp[b]
            disp_part = both - disp_ref[b] * per_image(both, image, jnp.sum, 0.0)
            grad_logits[b] = (comb_part + disp_part).astype(bf16)
            gl_ref[b] = grad_logits[b]
        for b in pair:
            part = jnp.dot(
                grad_logits[b], x_ref[b * width : (b + 1) * width, :], preferred_element_type=f32
            )
            router_sum = part if router_sum is None else router_sum + part
    router_ref[...] = router_sum


def token_logits(back, tokens, g_outputs, dispatch, combine):
    experts, images, double = back.shape
    rows, feat = tokens.shape
    steps, _, width = dispatch.shape
    return pl.pallas_call(
        token_logits_body,
        in_specs=[IN_VMEM] + [IN_PLACE] * 4,
        out_specs=[IN_VMEM] * 3,
        out_shape=[
            jax.ShapeDtypeStruct((steps, experts, width), bf16),
            jax.ShapeDtypeStruct((steps, GROUP * experts, feat), bf16),
            jax.ShapeDtypeStruct((experts, feat), f32),
        ],
        scratch_shapes=[
            pltpu.VMEM((experts * images, double), bf16),
            pltpu.VMEM(dispatch.shape, f32),
            pltpu.VMEM(combine.shape, f32),
            pltpu.VMEM((rows, feat), bf16),
            pltpu.VMEM((rows, feat), bf16),
            pltpu.SemaphoreType.DMA((steps,)),
            pltpu.SemaphoreType.DMA((steps,)),
            pltpu.SemaphoreType.DMA((2,)),
        ],
        compiler_params=params(20),
        name="token_logits",
    )(back, *[pinned(v) for v in (tokens, g_outputs, dispatch, combine)])


def token_grads_body(gl_ref, slots_ref, disp_ref, rt_ref, out_hbm, out, sem):
    steps, _, width = gl_ref.shape
    image = lane_images(width)
    stores = []
    for b in range(steps):
        left = jnp.concatenate([per_slot_rows(disp_ref[b], image), gl_ref[b]], axis=0)
        right = jnp.concatenate([slots_ref[b], rt_ref[...]], axis=0)
        out[b * width : (b + 1) * width, :] = contract(left, right, 0, 0).astype(bf16)
        at = pl.ds(b * width, width)
        stores.append(pltpu.make_async_copy(out.at[at], out_hbm.at[at], sem.at[b]))
        stores[b].start()
    for store in stores:
        store.wait()


def token_grads(grad_logits, slots, dispatch, rt):
    steps, _, width = grad_logits.shape
    shape = (steps * width, slots.shape[2])
    return pl.pallas_call(
        token_grads_body,
        in_specs=[IN_VMEM] * 4,
        out_specs=IN_PLACE,
        out_shape=pltpu.HBM(shape, bf16),
        scratch_shapes=[pltpu.VMEM(shape, bf16), pltpu.SemaphoreType.DMA((steps,))],
        compiler_params=params(12),
        name="token_grads",
    )(grad_logits, slots, dispatch, rt)


def shift(value, axis, by, count):
    return lax.ppermute(value, axis, [(i, (i + by) % count) for i in range(count)])


def axis_sum(value, axis, count):
    return sum([shift(value, axis, by, count) for by in range(1, count)], value)


def pair_sum(value, axis, count, by):
    return value + lax.ppermute(value, axis, [(i, i ^ by) for i in range(count)])


def solution(mesh):
    dp, experts = mesh.shape["dp"], mesh.shape["expert"]
    ny, nz = dp // XH, experts // 4
    fine = Mesh(
        mesh.devices.reshape(ny, XH, nz, 2, 2), ("y", "xh", "z", "xl", "core")
    )
    dp_axes = ("y", "xh")
    ex_axes = ("z", "xl", "core")

    def over_experts(value):
        return lax.all_to_all(value, ex_axes, split_axis=0, concat_axis=0, tiled=True)

    def on_device(tokens, router, w_in, w_out, g_outputs):
        rt = router.T
        slots, dispatch, combine = token_forward(tokens, rt, g_outputs)
        rows = over_experts(slots).reshape(-1, slots.shape[2])
        mid = rows.shape[0] // 2
        right = shift(rows, "y", 1, ny)
        left = shift(rows, "y", ny - 1, ny)
        results, act_own, pre_own = expert_rows(rows, w_in, w_out, ny)
        back = over_experts(results.reshape(slots.shape))
        far_a = shift(right[:mid], "y", 1, ny)
        far_b = shift(left[mid:], "y", ny - 1, ny)
        act_near, pre_near = near_terms(right, left, w_in, w_out, ny)
        back, act_near, pre_near = lax.optimization_barrier((back, act_near, pre_near))
        grad_logits, slot_grads, router_term = token_logits(
            back, tokens, g_outputs, dispatch, combine
        )
        far_a, far_b, router_term = lax.optimization_barrier((far_a, far_b, router_term))
        pieces = (rows, right, left, far_a, far_b)
        keep_in, send_in, act_far = first_grads(pieces, pre_own, pre_near, w_in, w_out, ny)
        keep_out, send_out = second_grads(pieces, (act_own, act_near, act_far))
        total = axis_sum(router_term, ("xh", "xl"), 2 * XH)
        total, send_in = lax.optimization_barrier((total, send_in))
        came_in = shift(send_in, "xh", 1, XH)
        came_out = shift(send_out, "xh", 1, XH)
        total, keep_out = lax.optimization_barrier((total, keep_out))
        total = pair_sum(axis_sum(total, "core", 2), "y", ny, 1)
        part_in = (keep_in + came_in.astype(f32)).astype(bf16)
        grad_tok = token_grads(grad_logits, slot_grads, dispatch, rt)
        total, grad_tok = lax.optimization_barrier((total, grad_tok))
        total = pair_sum(total, "y", ny, 2)
        total, part_in, grad_tok = lax.optimization_barrier((total, part_in, grad_tok))
        spread = lax.all_to_all(part_in, "y", split_axis=0, concat_axis=0, tiled=True)
        grad_router = axis_sum(total, "z", nz).T
        grad_first, grad_second = finish(spread, keep_out, came_out)
        return grad_tok, grad_router, grad_first, grad_second

    return jax.shard_map(
        on_device,
        mesh=fine,
        in_specs=(
            P(dp_axes + ex_axes, None),
            P(),
            P(ex_axes, None, None),
            P(ex_axes, None, None),
            P(dp_axes + ex_axes, None),
        ),
        out_specs=(
            P(dp_axes + ex_axes, None),
            P(),
            P(ex_axes, dp_axes, None),
            P(ex_axes, dp_axes, None),
        ),
        check_vma=False,
    )
```
